32 devices in a mesh: row: 8 (over y, x, core), depth: 4 (over z).
Axes of the slice: x: 2, y: 2, z: 4, core: 2. Of those that a mesh axis runs over, the one named last changes fastest.
Arguments:
- density: float32 [64, 128, 1024], P('depth', 'row'), may hold values from 0.2 to 1.5
- velocity: float32 [3, 64, 128, 1024], P(None, 'depth', 'row'), may hold values from -3 to 3
- palette: float32 [3, 4], replicated, may hold values from -6 to 6
Outputs:
- filtered: float32 [4, 128, 1024], P(None, 'row', 'depth')
- settled_density: float32 [64, 128, 1024], P('depth', 'row')
- settled_velocity: float32 [3, 64, 128, 1024], P(None, 'depth', 'row')
The draws below stay inside these ranges and needn't reach their ends.
All inputs are finite; a program needn't handle non-finite values.
Results may differ from the reference program's by a relative error of at most 0.00013.
Values sent between devices are 32-bit elements; how exact they have to be, the bound alone decides.
No kernel may reach another device: no remote copies, remote signals or barrier semaphores. Data moves between devices by JAX's collectives and lax.ppermute only.
A program may use at most 128 MiB of HBM per device.

```python
import math
import jax
import jax.numpy as jnp
from jax import lax

NX = 1024
NY = 128
NZ = 64


def level_of(rng, dims, split, smallest, high):
    def one(axis_at, shards_of):
        draws = jax.random.uniform(jax.random.fold_in(jax.random.fold_in(rng, 6), axis_at), (shards_of,), jnp.float32, smallest / len(split), high / len(split))
        return jnp.repeat(jnp.exp(draws), dims[axis_at] // shards_of).reshape((-1,) + (1,) * (len(dims) - axis_at - 1))

    factor_of = one(*split[0])
    for cut in split[1:]:
        factor_of = factor_of * one(*cut)
    return factor_of


def normal_values(key, dims, spread, bound, split=(), kind=jnp.bfloat16):
    array = spread * jax.random.normal(key, dims, jnp.float32)
    if split:
        array = array * level_of(key, dims, split, -0.22, 0.18)
    return jnp.clip(array, -bound, bound).astype(kind)


def setup_inputs(seed: int = 0) -> dict:
    arg_keys = jax.random.split(jax.random.key(seed), 4)
    density = jnp.clip(0.2 + 1.3 * jax.random.uniform(arg_keys[0], (NZ, NY, NX), jnp.float32) ** level_of(arg_keys[0], (NZ, NY, NX), ((0, 4), (1, 8)), -0.2, 0.2), 0.2, 1.5)
    velocity = normal_values(arg_keys[1], (3, NZ, NY, NX), 0.5, 3.0, ((1, 4), (2, 8)), jnp.float32)
    palette = normal_values(arg_keys[2], (3, 4), 1.5, 6.0, (), jnp.float32)
    return {"density": density, "velocity": velocity, "palette": palette}


DIFFUSION = 0.1
ADVECTION = 0.25
VISCOSITY = 0.15
FRICTION = 0.2
OPTICAL = 2.0
RANGE_SCALE = 0.1
SPACE_SCALE = 1.5


def advance(padded):
    widened = jnp.pad(padded, ((0, 0), (0, 0), (0, 0), (1, 1)))
    centre = widened[:, 1:-1, 1:-1, 1:-1]
    front_side = widened[:, :-2, 1:-1, 1:-1]
    back_side = widened[:, 2:, 1:-1, 1:-1]
    upper_side = widened[:, 1:-1, :-2, 1:-1]
    lower_side = widened[:, 1:-1, 2:, 1:-1]
    left_side = widened[:, 1:-1, 1:-1, :-2]
    right_side = widened[:, 1:-1, 1:-1, 2:]
    laplace = front_side + back_side + upper_side + lower_side + left_side + right_side - 6.0 * centre
    flux_div = 0.5 * (right_side[0] * right_side[1] - left_side[0] * left_side[1]
                      + lower_side[0] * lower_side[2] - upper_side[0] * upper_side[2]
                      + back_side[0] * back_side[3] - front_side[0] * front_side[3])
    density = centre[0]
    squared = density * density
    new_density = density + DIFFUSION * laplace[0] - ADVECTION * flux_div
    viscous = VISCOSITY * squared / (1.0 + squared)
    new_velocity = (centre[1:] + viscous * laplace[1:]) / (1.0 + FRICTION * squared)
    return jnp.concatenate([new_density[None], new_velocity], 0)


def bilateral(padded, valid):
    height = padded.shape[1] - 4
    width = padded.shape[2] - 4
    luminance = (padded[0] + padded[1] + padded[2]) / 3.0
    centre_lum = luminance[2:2 + height, 2:2 + width]
    numerator = jnp.zeros((4, height, width), jnp.float32)
    denominator = jnp.zeros((height, width), jnp.float32)
    for row_offset in range(5):
        for col_offset in range(5):
            spatial = math.exp(-((row_offset - 2) * (row_offset - 2) + (col_offset - 2) * (col_offset - 2)) / (2.0 * SPACE_SCALE * SPACE_SCALE))
            shifted = padded[:, row_offset:row_offset + height, col_offset:col_offset + width]
            shifted_lum = luminance[row_offset:row_offset + height, col_offset:col_offset + width]
            shifted_valid = valid[row_offset:row_offset + height, col_offset:col_offset + width]
            diff = shifted_lum - centre_lum
            weight = shifted_valid * spatial * jnp.exp(-diff * diff / (2.0 * RANGE_SCALE * RANGE_SCALE))
            numerator = numerator + weight[None] * shifted
            denominator = denominator + weight
    return numerator / denominator[None]


def reference(density, velocity, palette):
    volume = jnp.concatenate([density[None], velocity], 0)
    for repeat_index in range(2):
        volume = advance(jnp.pad(volume, ((0, 0), (1, 1), (1, 1), (0, 0))))
    depth_total = volume.shape[1]

    def march(running, layer):
        depth_sum, colour = running
        optical = (OPTICAL / depth_total) * layer[0] * layer[0]
        opacity = 1.0 - jnp.exp(-optical)
        shading = jax.nn.sigmoid(jnp.einsum("ck,kyx->cyx", palette, layer, precision=lax.Precision.HIGHEST))
        colour = colour + (jnp.exp(-depth_sum) * opacity)[None] * shading
        return (depth_sum + optical, colour), None

    slices = jnp.moveaxis(volume, 1, 0)
    start_sum = jnp.zeros(volume.shape[2:], jnp.float32)
    start_colour = jnp.zeros((3,) + volume.shape[2:], jnp.float32)
    (depth_sum, colour), unused_out = lax.scan(march, (start_sum, start_colour), slices)
    picture = jnp.concatenate([colour, (1.0 - jnp.exp(-depth_sum))[None]], 0)
    valid = jnp.pad(jnp.ones(picture.shape[1:], jnp.float32), 2)
    filtered = bilateral(jnp.pad(picture, ((0, 0), (2, 2), (2, 2))), valid)
    return filtered, volume[0], volume[1:]
```

```python
import functools
import math

import jax
import jax.numpy as jnp
from jax import lax
from jax.experimental import pallas as pl
from jax.experimental.pallas import tpu as pltpu
from jax.sharding import PartitionSpec as P

DIFFUSION = 0.1
ADVECTION = 0.25
VISCOSITY = 0.15
FRICTION = 0.2
OPTICAL = 2.0
RANGE_SCALE = 0.1
SPACE_SCALE = 1.5
SUB = 8
LANES = 128
AXES = ("row", "depth")


def shift_permute(array, row_step, depth_step):
    rows, depths = lax.axis_size("row"), lax.axis_size("depth")
    pairs = []
    for r in range(rows):
        for d in range(depths):
            if 0 <= r + row_step < rows and 0 <= d + depth_step < depths:
                pairs.append((r * depths + d, (r + row_step) * depths + d + depth_step))
    return lax.ppermute(array, AXES, pairs)


def pack_kernel(den_ref, vel_ref, row_low_ref, row_high_ref, corner_ref):
    layers, rows = den_ref.shape[0], den_ref.shape[1]
    for comp in range(4):
        for z in range(layers):
            line = (lambda r: den_ref[z, r : r + 1, :]) if comp == 0 else (
                lambda r: vel_ref[comp - 1, z, r : r + 1, :]
            )
            for k in range(2):
                row_low_ref[comp, k, z : z + 1, :] = line(k)
                row_high_ref[comp, k, z : z + 1, :] = line(rows - 2 + k)
    for comp in range(4):
        for side, r in ((0, 0), (1, rows - 1)):
            for far, z in ((0, 0), (1, layers - 1)):
                value = den_ref[z, r : r + 1, :] if comp == 0 else vel_ref[comp - 1, z, r : r + 1, :]
                corner_ref[2 * side + far, comp : comp + 1, :] = value


def tile_step(cur, before, after, t, j, tiles, spans, sub, lane):
    up_tile, down_tile = (t - 1) % tiles, (t + 1) % tiles
    zero = jnp.zeros((SUB, LANES), jnp.float32)

    def at(ref, c, tt, jj):
        return ref[c, tt * SUB : (tt + 1) * SUB, jj * LANES : (jj + 1) * LANES]

    centre, front, back, lap = [], [], [], []
    up, down, left, right = [], [], [], []
    for c in range(4):
        here = at(cur, c, t, j)
        west = at(cur, c, t, j - 1) if j > 0 else zero
        east = at(cur, c, t, j + 1) if j < spans - 1 else zero
        u = pltpu.roll(jnp.where(sub == SUB - 1, at(cur, c, up_tile, j), here), 1, 0)
        d = pltpu.roll(jnp.where(sub == 0, at(cur, c, down_tile, j), here), SUB - 1, 0)
        w = pltpu.roll(jnp.where(lane == LANES - 1, west, here), 1, 1)
        e = pltpu.roll(jnp.where(lane == 0, east, here), LANES - 1, 1)
        f, b = at(before, c, t, j), at(after, c, t, j)
        centre.append(here)
        front.append(f)
        back.append(b)
        up.append(u)
        down.append(d)
        left.append(w)
        right.append(e)
        lap.append(((f + b) + (u + d)) + ((w + e) - 6.0 * here))
    flux = (
        (right[0] * right[1] - left[0] * left[1])
        + (down[0] * down[2] - up[0] * up[2])
        + (back[0] * back[3] - front[0] * front[3])
    )
    density = centre[0]
    squared = density * density
    new = [density + DIFFUSION * lap[0] - (0.5 * ADVECTION) * flux]
    grown = 1.0 + squared
    inverse = 1.0 / (grown * (1.0 + FRICTION * squared))
    spread = VISCOSITY * squared
    for c in range(1, 4):
        new.append((centre[c] * grown + spread * lap[c]) * inverse)
    return new


def settle_kernel(
    place_ref, palette_ref, den_ref, vel_ref, front_ref, back_ref, above_ref, below_ref,
    corner_af_ref, corner_ab_ref, corner_bf_ref, corner_bb_ref,
    den_out, vel_out, picture_ref, ring, stepped, accum,
    *, layers, rows, columns, depth_total, pieces,
):
    i = pl.program_id(0)
    tiles = rows // SUB + 1
    own_tiles = rows // SUB
    spans = columns // LANES
    halo = rows
    newest = lax.rem(i, 3)
    middle = lax.rem(i + 2, 3)
    oldest = lax.rem(i + 1, 3)

    @pl.when(i == 0)
    def _():
        ring[...] = jnp.zeros_like(ring)
        stepped[...] = jnp.zeros_like(stepped)
        for c in range(3):
            accum[c] = jnp.zeros((rows, columns), jnp.float32)
        accum[3] = jnp.ones((rows, columns), jnp.float32)

    @pl.when(i < 2)
    def _():
        for c in range(4):
            ring[newest, c, 0:rows, :] = front_ref[c, i]

    @pl.when(i == 1)
    def _():
        for c in range(4):
            ring[newest, c, halo : halo + 1, :] = corner_bf_ref[0, c : c + 1, :]
            ring[newest, c, halo + SUB - 1 : halo + SUB, :] = corner_af_ref[0, c : c + 1, :]

    @pl.when((i >= 2) & (i < layers + 2))
    def _():
        ring[newest, 0, 0:rows, :] = den_ref[0]
        for c in range(3):
            ring[newest, c + 1, 0:rows, :] = vel_ref[c, 0]
        for c in range(4):
            for k in range(2):
                ring[newest, c, halo + k : halo + k + 1, :] = below_ref[c, k, pl.ds(i - 2, 1), :]
                ring[newest, c, halo + SUB - 2 + k : halo + SUB - 1 + k, :] = above_ref[
                    c, k, pl.ds(i - 2, 1), :
                ]

    @pl.when(i >= layers + 2)
    def _():
        for c in range(4):
            ring[newest, c, 0:rows, :] = back_ref[c, i - (layers + 2)]

    @pl.when(i == layers + 2)
    def _():
        for c in range(4):
            ring[newest, c, halo : halo + 1, :] = corner_bb_ref[0, c : c + 1, :]
            ring[newest, c, halo + SUB - 1 : halo + SUB, :] = corner_ab_ref[0, c : c + 1, :]

    sub = lax.broadcasted_iota(jnp.int32, (SUB, LANES), 0)
    lane = lax.broadcasted_iota(jnp.int32, (SUB, LANES), 1)

    @pl.when(i >= 2)
    def _():
        outside = ((i == 2) & (place_ref[0] == 1)) | ((i == layers + 3) & (place_ref[1] == 1))
        keep = jnp.where(outside, 0, 1)
        keep_above = keep * (1 - place_ref[2])
        keep_below = keep * (1 - place_ref[3])
        inside = jnp.full((SUB, LANES), keep, jnp.int32) == 1
        halo_inside = jnp.where(sub < SUB // 2, keep_below, keep_above) == 1
        for j in range(spans):
            for t in range(tiles):
                new = tile_step(
                    ring.at[middle], ring.at[oldest], ring.at[newest], t, j, tiles, spans, sub, lane
                )
                mask = inside if t < own_tiles else halo_inside
                for c in range(4):
                    stepped[
                        newest, c, t * SUB : (t + 1) * SUB, j * LANES : (j + 1) * LANES
                    ] = jnp.where(mask, new[c], 0.0)

    @pl.when(i >= 4)
    def _():
        for j in range(spans):
            for t in range(own_tiles):
                new = tile_step(
                    stepped.at[middle], stepped.at[oldest], stepped.at[newest],
                    t, j, tiles, spans, sub, lane,
                )
                here = (slice(t * SUB, (t + 1) * SUB), slice(j * LANES, (j + 1) * LANES))
                den_out[(0,) + here] = new[0]
                for c in range(3):
                    vel_out[(c, 0) + here] = new[c + 1]
                before = accum[(3,) + here]
                passed = before * jnp.exp((-OPTICAL / depth_total) * (new[0] * new[0]))
                weight = before - passed
                accum[(3,) + here] = passed
                for c in range(3):
                    mixed = palette_ref[c, 0] * new[0]
                    for k in range(1, 4):
                        mixed = mixed + palette_ref[c, k] * new[k]
                    accum[(c,) + here] = accum[(c,) + here] + weight * jnp.tanh(mixed)

    @pl.when(i == layers + 3)
    def _():
        width = columns // pieces
        for t in range(own_tiles):
            r = slice(t * SUB, (t + 1) * SUB)
            through = accum[3, r, :]
            channels = [0.5 * (accum[c, r, :] + (1.0 - through)) for c in range(3)] + [through]
            for p in range(pieces):
                for c in range(4):
                    picture_ref[p, r, c * width : (c + 1) * width] = channels[c][
                        :, p * width : (p + 1) * width
                    ]
                edge = jnp.zeros((SUB, LANES), jnp.float32)
                for c in range(4):
                    if p > 0:
                        west = channels[c][:, p * width - LANES : p * width]
                        turned = pltpu.roll(west, (4 * c + 2) % LANES, 1)
                        edge = jnp.where((lane >= 4 * c) & (lane < 4 * c + 2), turned, edge)
                    if p < pieces - 1:
                        east = channels[c][:, (p + 1) * width : (p + 1) * width + LANES]
                        turned = pltpu.roll(east, 4 * c + 2, 1)
                        edge = jnp.where((lane >= 4 * c + 2) & (lane < 4 * c + 4), turned, edge)
                picture_ref[p, r, 4 * width : 4 * width + LANES] = edge


def over_kernel(*refs, count, width):
    place_ref = refs[0]
    parts = refs[1 : 1 + count]
    picture_ref, top_ref, bottom_ref = refs[1 + count :]
    rows = picture_ref.shape[0]
    lane = lax.broadcasted_iota(jnp.int32, (rows, LANES), 1)

    def split(ref):
        return [ref[:, c * width : (c + 1) * width] for c in range(4)] + [
            ref[:, 4 * width : 4 * width + LANES]
        ]

    def spread_through(edge):
        out = jnp.ones_like(edge)
        for c in range(3):
            turned = pltpu.roll(edge, LANES - 12 + 4 * c, 1)
            out = jnp.where((lane >= 4 * c) & (lane < 4 * c + 4), turned, out)
        return out

    def over(flag, a, b):
        swapped = flag == 1
        near = [jnp.where(swapped, y, x) for x, y in zip(a, b)]
        far = [jnp.where(swapped, x, y) for x, y in zip(a, b)]
        out = [near[c] + near[3] * far[c] for c in range(3)]
        out.append(near[3] * far[3])
        is_through = lane >= 12
        edge = near[4] + spread_through(near[4]) * far[4]
        out.append(jnp.where(is_through, near[4] * far[4], edge))
        return out

    values = [split(ref) for ref in parts]
    bit = 0
    while len(values) > 1:
        flag = place_ref[bit]
        values = [over(flag, values[k], values[k + 1]) for k in range(0, len(values), 2)]
        bit += 1
    final = values[0]
    for c in range(4):
        v = (1.0 - final[3]) if c == 3 else final[c]
        picture_ref[:, c * width : (c + 1) * width] = v
    edge = jnp.where((lane >= 12) & (lane < 16), 1.0 - final[4], final[4])
    picture_ref[:, 4 * width : 4 * width + LANES] = edge
    top_ref[...] = picture_ref[0:SUB, :]
    bottom_ref[...] = picture_ref[rows - SUB : rows, :]


def filter_kernel(place_ref, picture_ref, above_ref, below_ref, out_ref, *, width):
    rows = picture_ref.shape[0]
    own_tiles = rows // SUB
    spans = width // LANES
    lane = lax.broadcasted_iota(jnp.int32, (SUB, LANES), 1)
    sub = lax.broadcasted_iota(jnp.int32, (SUB, LANES), 0)

    def tile(t, c, j):
        if j == -1 or j == spans:
            cols = slice(4 * width, 4 * width + LANES)
        else:
            cols = slice(c * width + j * LANES, c * width + (j + 1) * LANES)
        if t == -1:
            v = above_ref[:, cols]
        elif t == own_tiles:
            v = below_ref[:, cols]
        else:
            v = picture_ref[t * SUB : (t + 1) * SUB, cols]
        if j == -1:
            v = pltpu.roll(v, LANES - 2 - 4 * c, 1)
        elif j == spans:
            v = pltpu.roll(v, (LANES - 2 - 4 * c) % LANES, 1)
        return v

    tiles = {}
    for t in range(-1, own_tiles + 1):
        for j in range(-1, spans + 1):
            four = [tile(t, c, j) for c in range(4)]
            tiles[t, j] = four + [(four[0] + four[1] + four[2]) / 3.0]

    def column_shift(t, j, q, dx):
        if dx == 0:
            return tiles[t, j][q]
        if dx > 0:
            mixed = jnp.where(lane < dx, tiles[t, j + 1][q], tiles[t, j][q])
        else:
            mixed = jnp.where(lane >= LANES + dx, tiles[t, j - 1][q], tiles[t, j][q])
        return pltpu.roll(mixed, (-dx) % LANES, 1)

    no_above, no_below = place_ref[0] == 1, place_ref[1] == 1
    no_west, no_east = place_ref[2] == 1, place_ref[3] == 1
    for j in range(spans):
        sums = [[None] * 5 for _ in range(own_tiles)]
        for dx in range(-2, 3):
            shifted = {
                t: [column_shift(t, j, q, dx) for q in range(5)] for t in range(-1, own_tiles + 1)
            }
            for dy in range(-2, 3):
                spatial = -(dx * dx + dy * dy) / (2.0 * SPACE_SCALE * SPACE_SCALE)
                for t in range(own_tiles):
                    if dy == 0:
                        near = shifted[t]
                    elif dy > 0:
                        near = [
                            pltpu.roll(
                                jnp.where(sub < dy, shifted[t + 1][q], shifted[t][q]), SUB - dy, 0
                            )
                            for q in range(5)
                        ]
                    else:
                        near = [
                            pltpu.roll(
                                jnp.where(sub >= SUB + dy, shifted[t - 1][q], shifted[t][q]), -dy, 0
                            )
                            for q in range(5)
                        ]
                    diff = near[4] - tiles[t, j][4]
                    weight = jnp.exp(
                        spatial - diff * diff * (1.0 / (2.0 * RANGE_SCALE * RANGE_SCALE))
                    )
                    blocked = None
                    if t == 0 and dy < 0:
                        blocked = no_above & (sub < -dy)
                    if t == own_tiles - 1 and dy > 0:
                        blocked = no_below & (sub >= SUB - dy)
                    if j == 0 and dx < 0:
                        side = no_west & (lane < -dx)
                        blocked = side if blocked is None else blocked | side
                    if j == spans - 1 and dx > 0:
                        side = no_east & (lane >= LANES - dx)
                        blocked = side if blocked is None else blocked | side
                    if blocked is not None:
                        weight = jnp.where(blocked, 0.0, weight)
                    terms = [weight * near[c] for c in range(4)] + [weight]
                    sums[t] = terms if sums[t][0] is None else [a + b for a, b in zip(sums[t], terms)]
        for t in range(own_tiles):
            inverse = 1.0 / sums[t][4]
            for c in range(4):
                out_ref[c, t * SUB : (t + 1) * SUB, j * LANES : (j + 1) * LANES] = (
                    sums[t][c] * inverse
                )


def body(density, velocity, palette):
    layers, rows, columns = density.shape
    depth_count, row_count = lax.axis_size("depth"), lax.axis_size("row")
    depth_rank, row_rank = lax.axis_index("depth"), lax.axis_index("row")
    vmem = pl.BlockSpec(memory_space=pltpu.VMEM)
    smem = pl.BlockSpec(memory_space=pltpu.SMEM)
    f32 = jnp.float32

    first_depth = (depth_rank == 0).astype(jnp.int32)
    last_depth = (depth_rank == depth_count - 1).astype(jnp.int32)
    first_row = (row_rank == 0).astype(jnp.int32)
    last_row = (row_rank == row_count - 1).astype(jnp.int32)

    row_low, row_high, corner = pl.pallas_call(
        pack_kernel,
        out_shape=(
            jax.ShapeDtypeStruct((4, 2, layers, columns), f32),
            jax.ShapeDtypeStruct((4, 2, layers, columns), f32),
            jax.ShapeDtypeStruct((4, 4, columns), f32),
        ),
        in_specs=[vmem, vmem],
        out_specs=(vmem, vmem, vmem),
        name="pack",
    )(density, velocity)
    depth_low = jnp.concatenate([density[None, :2], velocity[:, :2]], 0)
    depth_high = jnp.concatenate([density[None, -2:], velocity[:, -2:]], 0)

    above = shift_permute(row_high, 1, 0)
    below = shift_permute(row_low, -1, 0)
    front = shift_permute(depth_high, 0, 1)
    back = shift_permute(depth_low, 0, -1)
    corner_af = shift_permute(corner[3:4], 1, 1)
    corner_ab = shift_permute(corner[2:3], 1, -1)
    corner_bf = shift_permute(corner[1:2], -1, 1)
    corner_bb = shift_permute(corner[0:1], -1, -1)

    width = columns // depth_count
    line = 4 * width + LANES
    tiles = rows // SUB + 1
    settled, moving, picture = pl.pallas_call(
        functools.partial(
            settle_kernel, layers=layers, rows=rows, columns=columns,
            depth_total=layers * depth_count, pieces=depth_count,
        ),
        grid=(layers + 4,),
        out_shape=(
            jax.ShapeDtypeStruct((layers, rows, columns), f32),
            jax.ShapeDtypeStruct((3, layers, rows, columns), f32),
            jax.ShapeDtypeStruct((depth_count, rows, line), f32),
        ),
        in_specs=[
            smem,
            smem,
            pl.BlockSpec((1, rows, columns), lambda i: (jnp.clip(i - 2, 0, layers - 1), 0, 0)),
            pl.BlockSpec(
                (3, 1, rows, columns), lambda i: (0, jnp.clip(i - 2, 0, layers - 1), 0, 0)
            ),
        ]
        + [vmem] * 8,
        out_specs=(
            pl.BlockSpec((1, rows, columns), lambda i: (jnp.maximum(i - 4, 0), 0, 0)),
            pl.BlockSpec((3, 1, rows, columns), lambda i: (0, jnp.maximum(i - 4, 0), 0, 0)),
            vmem,
        ),
        scratch_shapes=[
            pltpu.VMEM((3, 4, tiles * SUB, columns), f32),
            pltpu.VMEM((3, 4, tiles * SUB, columns), f32),
            pltpu.VMEM((4, rows, columns), f32),
        ],
        name="settle",
    )(
        jnp.stack([first_depth, last_depth, first_row, last_row]), 0.5 * palette,
        density, velocity, front, back, above, below, corner_af, corner_ab, corner_bf, corner_bb,
    )

    bits = depth_count.bit_length() - 1
    parts = []
    for k in range(depth_count):
        piece = lax.dynamic_index_in_dim(picture, depth_rank ^ k, 0, False)
        if k:
            piece = lax.ppermute(piece, "depth", [(i, i ^ k) for i in range(depth_count)])
        parts.append(piece)
    composed, top, bottom = pl.pallas_call(
        functools.partial(over_kernel, count=depth_count, width=width),
        out_shape=(
            jax.ShapeDtypeStruct((rows, line), f32),
            jax.ShapeDtypeStruct((SUB, line), f32),
            jax.ShapeDtypeStruct((SUB, line), f32),
        ),
        in_specs=[smem] + [vmem] * depth_count,
        out_specs=(vmem, vmem, vmem),
        name="over",
    )(jnp.stack([depth_rank >> b & 1 for b in range(bits)]).astype(jnp.int32), *parts)

    above_rows = shift_permute(bottom, 1, 0)
    below_rows = shift_permute(top, -1, 0)
    filtered = pl.pallas_call(
        functools.partial(filter_kernel, width=width),
        out_shape=jax.ShapeDtypeStruct((4, rows, width), f32),
        in_specs=[smem] + [vmem] * 3,
        out_specs=vmem,
        name="bilateral",
    )(
        jnp.stack([first_row, last_row, first_depth, last_depth]),
        composed, above_rows, below_rows,
    )
    return (filtered, settled, moving)


def solution(mesh):
    in_specs = (P("depth", "row", None), P(None, "depth", "row", None), P())
    out_specs = (P(None, "row", "depth"), P("depth", "row", None), P(None, "depth", "row", None))
    return jax.shard_map(body, mesh=mesh, in_specs=in_specs, out_specs=out_specs, check_vma=False)
```

```python
import functools
import math

import jax
import jax.numpy as jnp
from jax import lax
from jax.experimental import pallas as pl
from jax.experimental.pallas import tpu as pltpu
from jax.sharding import PartitionSpec as P

DIFFUSION = 0.1
ADVECTION = 0.25
VISCOSITY = 0.15
FRICTION = 0.2
OPTICAL = 2.0
RANGE_SCALE = 0.1
SPACE_SCALE = 1.5
SUB = 8
LANES = 128
PITCH = 40
AXES = ("row", "depth")


def row_pairs(kind, count):
    pairs = []
    for low in range(kind, count - 1, 2):
        pairs += [(low, low + 1), (low + 1, low)]
    return pairs


def swap_rows(array, kind):
    return lax.ppermute(array, "row", row_pairs(kind, lax.axis_size("row")))


def swap_depths(array, kind):
    return lax.ppermute(array, "depth", row_pairs(kind, lax.axis_size("depth")))


def swap_corners(array, row_kind, depth_kind):
    depths = lax.axis_size("depth")
    pairs = [
        (a * depths + c, b * depths + d)
        for a, b in row_pairs(row_kind, lax.axis_size("row"))
        for c, d in row_pairs(depth_kind, depths)
    ]
    return lax.ppermute(array, AXES, pairs)


def pack_kernel(
    den_ref, vel_ref, row0_ref, row1_ref, depth0_ref, depth1_ref, c00_ref, c01_ref, c10_ref, c11_ref,
    block, load_sem, send_sem, *, layers, rows, spans,
):
    row_odd = lax.rem(lax.axis_index("row"), 2)
    depth_odd = lax.rem(lax.axis_index("depth"), 2)
    own_tiles = rows // SUB

    def load(c, t, j):
        source = den_ref if c == 0 else vel_ref.at[c - 1]
        return pltpu.make_async_copy(
            source.at[:, t * SUB : (t + 1) * SUB, j * LANES : (j + 1) * LANES],
            block.at[c, :, t, j * SUB : (j + 1) * SUB, :],
            load_sem.at[c, t, j],
        )

    def send(c, kind):
        follows = 1 - depth_odd if kind == 0 else depth_odd
        target = depth0_ref if kind == 0 else depth1_ref
        return pltpu.make_async_copy(
            block.at[c, pl.ds(follows * (layers - 2), 2)], target.at[c], send_sem.at[kind, c]
        )

    for c in range(4):
        for t in range(own_tiles):
            for j in range(spans):
                load(c, t, j).start()
    row_sides = [1 - row_odd, row_odd]
    for c in range(4):
        for t in range(own_tiles):
            for j in range(spans):
                load(c, t, j).wait()
        for kind in range(2):
            send(c, kind).start()
        for kind, target in ((0, row0_ref), (1, row1_ref)):
            side = row_sides[kind]
            t = side * (own_tiles - 1)
            for k in range(2):
                start = side * (SUB - 2) + k
                for z in range(layers):
                    target[c, z, k] = block[c, z, t, pl.ds(start, SUB, stride=SUB), :]
    corners = ((c00_ref, c01_ref), (c10_ref, c11_ref))
    for c in range(4):
        for row_kind in range(2):
            for depth_kind in range(2):
                side = row_sides[row_kind]
                z = (1 - depth_odd if depth_kind == 0 else depth_odd) * (layers - 1)
                corners[row_kind][depth_kind][c] = block[
                    c, z, side * (own_tiles - 1), pl.ds(side * (SUB - 1), SUB, stride=SUB), :
                ]
    for c in range(4):
        for kind in range(2):
            send(c, kind).wait()


def advance(here, up, down, left, right, front, back):
    around = [
        ((front[c] + back[c]) + (up[c] + down[c])) + (left[c] + right[c]) for c in range(4)
    ]
    flux = (
        (right[0] * right[1] - left[0] * left[1])
        + (down[0] * down[2] - up[0] * up[2])
        + (back[0] * back[3] - front[0] * front[3])
    )
    squared = here[0] * here[0]
    new = [
        (1.0 - 6.0 * DIFFUSION) * here[0] + (DIFFUSION * around[0] - (0.5 * ADVECTION) * flux)
    ]
    inverse = 1.0 / ((1.0 + squared) * (1.0 + FRICTION * squared))
    own_share = (1.0 + (1.0 - 6.0 * VISCOSITY) * squared) * inverse
    near_share = (VISCOSITY * squared) * inverse
    for c in range(1, 4):
        new.append(here[c] * own_share + around[c] * near_share)
    return new


def settle_kernel(
    palette_ref, den_ref, vel_ref, row0_ref, row1_ref, depth0_ref, depth1_ref,
    c00_ref, c01_ref, c10_ref, c11_ref, den_out, vel_out, *rest,
    layers, rows, columns, depth_count, row_count,
):
    pieces = rest[:depth_count]
    (base, west, east, sbase, swest, seast, accum, rowbuf, depthbuf, cornerbuf, sem) = rest[
        depth_count:
    ]
    i = pl.program_id(0)
    own_tiles, spans = rows // SUB, columns // LANES
    row_rank, depth_rank = lax.axis_index("row"), lax.axis_index("depth")
    row_odd, depth_odd = lax.rem(row_rank, 2), lax.rem(depth_rank, 2)
    above, below = 1 - row_odd, row_odd
    front, back = 1 - depth_odd, depth_odd
    newest, middle, oldest = lax.rem(i, 3), lax.rem(i + 2, 3), lax.rem(i + 1, 3)
    sub = lax.broadcasted_iota(jnp.int32, (SUB, LANES), 0)
    lane = lax.broadcasted_iota(jnp.int32, (SUB, LANES), 1)
    first, last = lane == 0, lane == LANES - 1
    not_first, not_last = lane > 0, lane < LANES - 1

    copies = [
        pltpu.make_async_copy(source, target, sem.at[n])
        for n, (source, target) in enumerate(
            (
                (depth0_ref, depthbuf.at[0]), (depth1_ref, depthbuf.at[1]),
                (row0_ref, rowbuf.at[0]), (row1_ref, rowbuf.at[1]),
                (c00_ref, cornerbuf.at[0, 0]), (c01_ref, cornerbuf.at[0, 1]),
                (c10_ref, cornerbuf.at[1, 0]), (c11_ref, cornerbuf.at[1, 1]),
            )
        )
    ]

    def row_of(j, row):
        return PITCH * j + SUB + row

    def store_sides(west_ref, east_ref, slot, c, t, j, value):
        to_right = pltpu.roll(value, 1, 1)
        to_left = pltpu.roll(value, LANES - 1, 1)

        def at(ref, jj):
            return ref.at[slot, c, pl.ds(jj * rows + t * SUB, SUB), :]

        pltpu.store(at(west_ref, j), to_right, mask=not_first)
        pltpu.store(at(east_ref, j), to_left, mask=not_last)
        if j < spans - 1:
            pltpu.store(at(west_ref, j + 1), to_right, mask=first)
        if j > 0:
            pltpu.store(at(east_ref, j - 1), to_left, mask=last)

    def take_layer(tile, sides):
        for c in range(4):
            for t in range(own_tiles):
                for j in range(spans):
                    value = tile(c, t, j)
                    base[newest, c, pl.ds(row_of(j, t * SUB), SUB), :] = value
                    if sides:
                        store_sides(west, east, newest, c, t, j, value)

    def set_row(c, row, value):
        base[newest, c, pl.ds(row_of(0, row), spans, stride=PITCH), :] = value

    @pl.when(i == 0)
    def _():
        for copy in copies:
            copy.start()
        edge = jnp.zeros((rows, LANES), jnp.float32)
        for slot in range(3):
            for c in range(4):
                west[slot, c, 0:rows, :] = edge
                swest[slot, c, 0:rows, :] = edge
                east[slot, c, (spans - 1) * rows : spans * rows, :] = edge
                seast[slot, c, (spans - 1) * rows : spans * rows, :] = edge
        for c in range(3):
            accum[c] = jnp.zeros((spans * rows, LANES), jnp.float32)
        accum[3] = jnp.ones((spans * rows, LANES), jnp.float32)
        for copy in copies[:2]:
            copy.wait()

    @pl.when(i == 1)
    def _():
        for copy in copies[2:]:
            copy.wait()

    @pl.when((i == 0) | (i == layers + 3))
    def _():
        side = jnp.where(i == 0, front, back)
        k = jnp.where(i == 0, 0, 1)
        take_layer(lambda c, t, j: depthbuf[side, c, k, t, pl.ds(j * SUB, SUB), :], False)

    @pl.when((i == 1) | (i == layers + 2))
    def _():
        side = jnp.where(i == 1, front, back)
        k = jnp.where(i == 1, 1, 0)
        take_layer(lambda c, t, j: depthbuf[side, c, k, t, pl.ds(j * SUB, SUB), :], True)
        for c in range(4):
            set_row(c, -1, cornerbuf[above, side, c])
            set_row(c, rows, cornerbuf[below, side, c])

    @pl.when((i >= 2) & (i < layers + 2))
    def _():
        def tile(c, t, j):
            there = (slice(t * SUB, (t + 1) * SUB), slice(j * LANES, (j + 1) * LANES))
            return den_ref[(0,) + there] if c == 0 else vel_ref[(c - 1, 0) + there]

        take_layer(tile, True)
        for c in range(4):
            for k in range(2):
                set_row(c, k - 2, rowbuf[above, c, i - 2, k])
                set_row(c, rows + k, rowbuf[below, c, i - 2, k])

    def neighbours(cells, west_ref, east_ref, t, j):
        def at(slot, row):
            return [cells[slot, c, pl.ds(row_of(j, row), SUB), :] for c in range(4)]

        def beside(ref):
            return [ref[middle, c, pl.ds(j * rows + t * SUB, SUB), :] for c in range(4)]

        row = t * SUB
        return (
            at(middle, row), at(middle, row - 1), at(middle, row + 1),
            beside(west_ref), beside(east_ref), at(oldest, row), at(newest, row),
        )

    @pl.when(i >= 2)
    def _():
        for j in range(spans):
            for t in range(own_tiles):
                new = advance(*neighbours(base, west, east, t, j))
                for c in range(4):
                    sbase[newest, c, pl.ds(row_of(j, t * SUB), SUB), :] = new[c]
                    store_sides(swest, seast, newest, c, t, j, new[c])
        for row, exists in ((-1, row_rank > 0), (rows, row_rank < row_count - 1)):

            def at(slot, r):
                return [
                    base[slot, c, pl.ds(row_of(0, r), spans, stride=PITCH), :] for c in range(4)
                ]

            here = at(middle, row)
            left, right = [], []
            for value in here:
                before = jnp.where(sub == 0, 0.0, pltpu.roll(value, 1, 0))
                after = jnp.where(sub == SUB - 1, 0.0, pltpu.roll(value, SUB - 1, 0))
                left.append(pltpu.roll(jnp.where(last, before, value), 1, 1))
                right.append(pltpu.roll(jnp.where(first, after, value), LANES - 1, 1))
            new = advance(
                here, at(middle, row - 1), at(middle, row + 1), left, right,
                at(oldest, row), at(newest, row),
            )
            keep = jnp.full((SUB, LANES), jnp.where(exists, 1, 0), jnp.int32) == 1
            for c in range(4):
                sbase[newest, c, pl.ds(row_of(0, row), spans, stride=PITCH), :] = jnp.where(
                    keep, new[c], 0.0
                )

    @pl.when(
        ((i == 2) & (depth_rank == 0)) | ((i == layers + 3) & (depth_rank == depth_count - 1))
    )
    def _():
        for c in range(4):
            sbase[newest, c] = jnp.zeros((PITCH * spans, LANES), jnp.float32)

    @pl.when(i >= 4)
    def _():
        rate = -OPTICAL / (layers * depth_count) / math.log(2.0)
        mix = [[0.5 * palette_ref[c, k] for k in range(4)] for c in range(3)]
        for j in range(spans):
            for t in range(own_tiles):
                new = advance(*neighbours(sbase, swest, seast, t, j))
                there = (slice(t * SUB, (t + 1) * SUB), slice(j * LANES, (j + 1) * LANES))
                den_out[(0,) + there] = new[0]
                for c in range(3):
                    vel_out[(c, 0) + there] = new[c + 1]
                pixels = pl.ds(j * rows + t * SUB, SUB)
                before = accum[3, pixels, :]
                passed = before * jnp.exp2(rate * (new[0] * new[0]))
                weight = before - passed
                accum[3, pixels, :] = passed
                for c in range(3):
                    mixed = (mix[c][0] * new[0] + mix[c][1] * new[1]) + (
                        mix[c][2] * new[2] + mix[c][3] * new[3]
                    )
                    accum[c, pixels, :] = accum[c, pixels, :] + weight * jnp.tanh(mixed)

    @pl.when(i == layers + 3)
    def _():
        width = columns // depth_count
        per_piece = width // LANES

        def channels(j, t):
            pixels = pl.ds(j * rows + t * SUB, SUB)
            through = accum[3, pixels, :]
            return [0.5 * (accum[c, pixels, :] + (1.0 - through)) for c in range(3)] + [through]

        for k in range(depth_count):
            piece = depth_rank ^ k
            start = piece * per_piece
            for t in range(own_tiles):
                r = slice(t * SUB, (t + 1) * SUB)
                for jj in range(per_piece):
                    values = channels(start + jj, t)
                    for c in range(4):
                        pieces[k][r, c * width + jj * LANES : c * width + (jj + 1) * LANES] = (
                            values[c]
                        )
                before = channels(jnp.maximum(start - 1, 0), t)
                after = channels(jnp.minimum(start + per_piece, spans - 1), t)
                edge = jnp.zeros((SUB, LANES), jnp.float32)
                for c in range(4):
                    for values, low in ((before, 4 * c), (after, 4 * c + 2)):
                        turned = pltpu.roll(values[c], (4 * c + 2) % LANES, 1)
                        edge = jnp.where((lane >= low) & (lane < low + 2), turned, edge)
                pieces[k][r, 4 * width : 4 * width + LANES] = edge


def over_kernel(*refs, count, width):
    parts = refs[:count]
    picture_ref, swap0_ref, swap1_ref = refs[count:]
    rows = picture_ref.shape[0]
    depth_rank = lax.axis_index("depth")
    row_odd = lax.rem(lax.axis_index("row"), 2)
    lane = lax.broadcasted_iota(jnp.int32, (rows, LANES), 1)

    def split(ref):
        return [ref[:, c * width : (c + 1) * width] for c in range(4)] + [
            ref[:, 4 * width : 4 * width + LANES]
        ]

    def spread_through(edge):
        out = jnp.ones_like(edge)
        for c in range(3):
            turned = pltpu.roll(edge, LANES - 12 + 4 * c, 1)
            out = jnp.where((lane >= 4 * c) & (lane < 4 * c + 4), turned, out)
        return out

    def over(swapped, a, b):
        near = [jnp.where(swapped, y, x) for x, y in zip(a, b)]
        far = [jnp.where(swapped, x, y) for x, y in zip(a, b)]
        out = [near[c] + near[3] * far[c] for c in range(3)]
        out.append(near[3] * far[3])
        edge = near[4] + spread_through(near[4]) * far[4]
        out.append(jnp.where(lane >= 12, near[4] * far[4], edge))
        return out

    values = [split(ref) for ref in parts]
    bit = 0
    while len(values) > 1:
        swapped = (depth_rank >> bit & 1) == 1
        values = [over(swapped, values[k], values[k + 1]) for k in range(0, len(values), 2)]
        bit += 1
    final = values[0]
    for c in range(4):
        picture_ref[:, c * width : (c + 1) * width] = (1.0 - final[3]) if c == 3 else final[c]
    edge = jnp.where((lane >= 12) & (lane < 16), 1.0 - final[4], final[4])
    picture_ref[:, 4 * width : 4 * width + LANES] = edge
    top, bottom = picture_ref[0:SUB, :], picture_ref[rows - SUB : rows, :]
    odd = row_odd == 1
    swap0_ref[...] = jnp.where(odd, top, bottom)
    swap1_ref[...] = jnp.where(odd, bottom, top)


def filter_kernel(picture_ref, swap0_ref, swap1_ref, out_ref, *, width, row_count, depth_count):
    row_rank, depth_rank = lax.axis_index("row"), lax.axis_index("depth")
    odd = lax.rem(row_rank, 2) == 1
    rows = picture_ref.shape[0]
    own_tiles = rows // SUB
    spans = width // LANES
    lane = lax.broadcasted_iota(jnp.int32, (SUB, LANES), 1)
    sub = lax.broadcasted_iota(jnp.int32, (SUB, LANES), 0)

    def tile(t, c, j):
        if j == -1 or j == spans:
            cols = slice(4 * width, 4 * width + LANES)
        else:
            cols = slice(c * width + j * LANES, c * width + (j + 1) * LANES)
        if t == -1:
            v = jnp.where(odd, swap0_ref[:, cols], swap1_ref[:, cols])
        elif t == own_tiles:
            v = jnp.where(odd, swap1_ref[:, cols], swap0_ref[:, cols])
        else:
            v = picture_ref[t * SUB : (t + 1) * SUB, cols]
        if j == -1:
            v = pltpu.roll(v, LANES - 2 - 4 * c, 1)
        elif j == spans:
            v = pltpu.roll(v, (LANES - 2 - 4 * c) % LANES, 1)
        return v

    tiles = {}
    for t in range(-1, own_tiles + 1):
        for j in range(-1, spans + 1):
            four = [tile(t, c, j) for c in range(4)]
            tiles[t, j] = four + [(four[0] + four[1] + four[2]) / 3.0]

    def column_shift(t, j, q, dx):
        if dx == 0:
            return tiles[t, j][q]
        if dx > 0:
            mixed = jnp.where(lane < dx, tiles[t, j + 1][q], tiles[t, j][q])
        else:
            mixed = jnp.where(lane >= LANES + dx, tiles[t, j - 1][q], tiles[t, j][q])
        return pltpu.roll(mixed, (-dx) % LANES, 1)

    no_above, no_below = row_rank == 0, row_rank == row_count - 1
    no_west, no_east = depth_rank == 0, depth_rank == depth_count - 1
    for j in range(spans):
        sums = [[None] * 5 for _ in range(own_tiles)]
        for dx in range(-2, 3):
            shifted = {
                t: [column_shift(t, j, q, dx) for q in range(5)] for t in range(-1, own_tiles + 1)
            }
            for dy in range(-2, 3):
                spatial = -(dx * dx + dy * dy) / (2.0 * SPACE_SCALE * SPACE_SCALE)
                for t in range(own_tiles):
                    if dy == 0:
                        near = shifted[t]
                    elif dy > 0:
                        near = [
                            pltpu.roll(
                                jnp.where(sub < dy, shifted[t + 1][q], shifted[t][q]), SUB - dy, 0
                            )
                            for q in range(5)
                        ]
                    else:
                        near = [
                            pltpu.roll(
                                jnp.where(sub >= SUB + dy, shifted[t - 1][q], shifted[t][q]), -dy, 0
                            )
                            for q in range(5)
                        ]
                    diff = near[4] - tiles[t, j][4]
                    weight = jnp.exp(
                        spatial - diff * diff * (1.0 / (2.0 * RANGE_SCALE * RANGE_SCALE))
                    )
                    blocked = None
                    if t == 0 and dy < 0:
                        blocked = no_above & (sub < -dy)
                    if t == own_tiles - 1 and dy > 0:
                        blocked = no_below & (sub >= SUB - dy)
                    if j == 0 and dx < 0:
                        side = no_west & (lane < -dx)
                        blocked = side if blocked is None else blocked | side
                    if j == spans - 1 and dx > 0:
                        side = no_east & (lane >= LANES - dx)
                        blocked = side if blocked is None else blocked | side
                    if blocked is not None:
                        weight = jnp.where(blocked, 0.0, weight)
                    terms = [weight * near[c] for c in range(4)] + [weight]
                    sums[t] = terms if sums[t][0] is None else [a + b for a, b in zip(sums[t], terms)]
        for t in range(own_tiles):
            inverse = 1.0 / sums[t][4]
            for c in range(4):
                out_ref[c, t * SUB : (t + 1) * SUB, j * LANES : (j + 1) * LANES] = (
                    sums[t][c] * inverse
                )


def body(density, velocity, palette):
    layers, rows, columns = density.shape
    depth_count, row_count = lax.axis_size("depth"), lax.axis_size("row")
    spans, own_tiles = columns // LANES, rows // SUB
    width = columns // depth_count
    line = 4 * width + LANES
    assert spans == SUB and rows % SUB == 0 and width % LANES == 0
    vmem = pl.BlockSpec(memory_space=pltpu.VMEM)
    smem = pl.BlockSpec(memory_space=pltpu.SMEM)
    anywhere = pl.BlockSpec(memory_space=pl.ANY)
    f32 = jnp.float32

    def shape(*dims):
        return jax.ShapeDtypeStruct(dims, f32)

    row_shape = (4, layers, 2, spans, LANES)
    depth_shape = (4, 2, own_tiles, spans * SUB, LANES)
    corner_shape = (4, spans, LANES)
    row0, row1, depth0, depth1, *corners = pl.pallas_call(
        functools.partial(pack_kernel, layers=layers, rows=rows, spans=spans),
        out_shape=(shape(*row_shape),) * 2 + (shape(*depth_shape),) * 2 + (shape(*corner_shape),) * 4,
        in_specs=[anywhere, anywhere],
        out_specs=(vmem,) * 2 + (anywhere,) * 2 + (vmem,) * 4,
        scratch_shapes=[
            pltpu.VMEM((4, layers, own_tiles, spans * SUB, LANES), f32),
            pltpu.SemaphoreType.DMA((4, own_tiles, spans)),
            pltpu.SemaphoreType.DMA((2, 4)),
        ],
        name="pack",
    )(density, velocity)
    row1, row0 = swap_rows(row1, 1), swap_rows(row0, 0)
    depth0, depth1 = swap_depths(depth0, 0), swap_depths(depth1, 1)
    corners = [swap_corners(corner, k // 2, k % 2) for k, corner in enumerate(corners)]

    settled, moving, *parts = pl.pallas_call(
        functools.partial(
            settle_kernel, layers=layers, rows=rows, columns=columns,
            depth_count=depth_count, row_count=row_count,
        ),
        grid=(layers + 4,),
        out_shape=(shape(layers, rows, columns), shape(3, layers, rows, columns))
        + (shape(rows, line),) * depth_count,
        in_specs=[
            smem,
            pl.BlockSpec((1, rows, columns), lambda i: (jnp.clip(i - 2, 0, layers - 1), 0, 0)),
            pl.BlockSpec(
                (3, 1, rows, columns), lambda i: (0, jnp.clip(i - 2, 0, layers - 1), 0, 0)
            ),
        ]
        + [anywhere] * 8,
        out_specs=(
            pl.BlockSpec((1, rows, columns), lambda i: (jnp.maximum(i - 4, 0), 0, 0)),
            pl.BlockSpec((3, 1, rows, columns), lambda i: (0, jnp.maximum(i - 4, 0), 0, 0)),
        )
        + (vmem,) * depth_count,
        scratch_shapes=[
            pltpu.VMEM((3, 4, spans * PITCH, LANES), f32),
            pltpu.VMEM((3, 4, spans * rows, LANES), f32),
            pltpu.VMEM((3, 4, spans * rows, LANES), f32),
            pltpu.VMEM((3, 4, spans * PITCH, LANES), f32),
            pltpu.VMEM((3, 4, spans * rows, LANES), f32),
            pltpu.VMEM((3, 4, spans * rows, LANES), f32),
            pltpu.VMEM((4, spans * rows, LANES), f32),
            pltpu.VMEM((2,) + row_shape, f32),
            pltpu.VMEM((2,) + depth_shape, f32),
            pltpu.VMEM((2, 2) + corner_shape, f32),
            pltpu.SemaphoreType.DMA((8,)),
        ],
        name="settle",
    )(palette, density, velocity, row0, row1, depth0, depth1, *corners)

    parts = [
        lax.ppermute(part, "depth", [(i, i ^ k) for i in range(depth_count)]) if k else part
        for k, part in enumerate(parts)
    ]
    composed, swap0, swap1 = pl.pallas_call(
        functools.partial(over_kernel, count=depth_count, width=width),
        out_shape=(shape(rows, line), shape(SUB, line), shape(SUB, line)),
        in_specs=[vmem] * depth_count,
        out_specs=(vmem, vmem, vmem),
        name="over",
    )(*parts)

    swap1, swap0 = swap_rows(swap1, 1), swap_rows(swap0, 0)
    filtered = pl.pallas_call(
        functools.partial(
            filter_kernel, width=width, row_count=row_count, depth_count=depth_count
        ),
        out_shape=shape(4, rows, width),
        in_specs=[vmem] * 3,
        out_specs=vmem,
        name="bilateral",
    )(composed, swap0, swap1)
    return (filtered, settled, moving)


def solution(mesh):
    in_specs = (P("depth", "row", None), P(None, "depth", "row", None), P())
    out_specs = (P(None, "row", "depth"), P("depth", "row", None), P(None, "depth", "row", None))
    return jax.shard_map(body, mesh=mesh, in_specs=in_specs, out_specs=out_specs, check_vma=False)
```

```python
import functools
import math

import jax
import jax.numpy as jnp
from jax import lax
from jax.experimental import pallas as pl
from jax.experimental.pallas import tpu as pltpu
from jax.sharding import PartitionSpec as P

DIFFUSION = 0.1
ADVECTION = 0.25
VISCOSITY = 0.15
FRICTION = 0.2
OPTICAL = 2.0
RANGE_SCALE = 0.1
SPACE_SCALE = 1.5
SUB = 8
LANES = 128
PITCH = 40
AXES = ("row", "depth")


def row_pairs(kind, count):
    pairs = []
    for low in range(kind, count - 1, 2):
        pairs += [(low, low + 1), (low + 1, low)]
    return pairs


def swap_rows(array, kind):
    return lax.ppermute(array, "row", row_pairs(kind, lax.axis_size("row")))


def swap_depths(array, kind):
    return lax.ppermute(array, "depth", row_pairs(kind, lax.axis_size("depth")))


def swap_corners(array, row_kind, depth_kind):
    depths = lax.axis_size("depth")
    pairs = [
        (a * depths + c, b * depths + d)
        for a, b in row_pairs(row_kind, lax.axis_size("row"))
        for c, d in row_pairs(depth_kind, depths)
    ]
    return lax.ppermute(array, AXES, pairs)


def pack_kernel(
    den_ref, vel_ref, row0_ref, row1_ref, depth0_ref, depth1_ref, c00_ref, c01_ref, c10_ref, c11_ref,
    block, sides, load_sem, row_sem, depth_sem, corner_sem, *, layers, rows, spans, chunks,
):
    row_odd = lax.rem(lax.axis_index("row"), 2)
    depth_odd = lax.rem(lax.axis_index("depth"), 2)
    size = layers // chunks

    def loads(k):
        z = slice(k * size, (k + 1) * size)
        return (
            pltpu.make_async_copy(den_ref.at[z], block.at[0, z], load_sem.at[k, 0]),
            pltpu.make_async_copy(vel_ref.at[:, z], block.at[1:4, z], load_sem.at[k, 1]),
        )

    for k in range(chunks):
        for copy in loads(k):
            copy.start()
    row_side = (1 - row_odd, row_odd)
    depth_side = (1 - depth_odd, depth_odd)
    sends = []
    for k in range(chunks):
        for copy in loads(k):
            copy.wait()
        for c in range(4):
            for z in range(k * size, (k + 1) * size):
                for side in range(2):
                    for n in range(2):
                        row = n + side * (rows - 2)
                        for j in range(spans):
                            sides[side, c, z, n, j : j + 1, :] = block[
                                c, z, row : row + 1, j * LANES : (j + 1) * LANES
                            ]
    for kind, target in ((0, row0_ref), (1, row1_ref)):
        sends.append(pltpu.make_async_copy(sides.at[row_side[kind]], target, row_sem.at[kind]))
    for kind, target in ((0, depth0_ref), (1, depth1_ref)):
        source = block.at[:, pl.ds(depth_side[kind] * (layers - 2), 2)]
        sends.append(pltpu.make_async_copy(source, target, depth_sem.at[kind]))
    for n, target in enumerate((c00_ref, c01_ref, c10_ref, c11_ref)):
        source = sides.at[
            row_side[n // 2], :, depth_side[n % 2] * (layers - 1), row_side[n // 2]
        ]
        sends.append(pltpu.make_async_copy(source, target, corner_sem.at[n]))
    for copy in sends:
        copy.start()
    for copy in sends:
        copy.wait()


def advance(here, up, down, left, right, front, back):
    around = [
        ((front[c] + back[c]) + (up[c] + down[c])) + (left[c] + right[c]) for c in range(4)
    ]
    flux = (
        (right[0] * right[1] - left[0] * left[1])
        + (down[0] * down[2] - up[0] * up[2])
        + (back[0] * back[3] - front[0] * front[3])
    )
    squared = here[0] * here[0]
    new = [
        (1.0 - 6.0 * DIFFUSION) * here[0] + (DIFFUSION * around[0] - (0.5 * ADVECTION) * flux)
    ]
    inverse = 1.0 / ((1.0 + squared) * (1.0 + FRICTION * squared))
    own_share = (1.0 + (1.0 - 6.0 * VISCOSITY) * squared) * inverse
    near_share = (VISCOSITY * squared) * inverse
    for c in range(1, 4):
        new.append(here[c] * own_share + around[c] * near_share)
    return new


def settle_kernel(
    palette_ref, den_ref, vel_ref, row0_ref, row1_ref, depth0_ref, depth1_ref,
    c00_ref, c01_ref, c10_ref, c11_ref, den_out, vel_out, *rest,
    layers, rows, columns, depth_count, row_count,
):
    pieces = rest[:depth_count]
    (
        incoming, rowbuf, base, west, east, sbase, swest, seast, accum, layer_sem, halo_sem
    ) = rest[depth_count:]
    step = pl.program_id(0)
    own_tiles, spans = rows // SUB, columns // LANES
    row_rank, depth_rank = lax.axis_index("row"), lax.axis_index("depth")
    row_odd, depth_odd = lax.rem(row_rank, 2), lax.rem(depth_rank, 2)
    above, below = 1 - row_odd, row_odd
    sub = lax.broadcasted_iota(jnp.int32, (SUB, LANES), 0)
    lane = lax.broadcasted_iota(jnp.int32, (SUB, LANES), 1)
    first, last = lane == 0, lane == LANES - 1
    not_first, not_last = lane > 0, lane < LANES - 1

    def halo_copies():
        copies = []
        for kind, source in ((0, depth0_ref), (1, depth1_ref)):
            is_front = depth_odd if kind == 0 else 1 - depth_odd
            place = (1 - is_front) * (layers + 2)
            copies.append(
                pltpu.make_async_copy(
                    source, incoming.at[:, pl.ds(place, 2)], halo_sem.at[kind]
                )
            )
        for kind, source in ((0, row0_ref), (1, row1_ref)):
            copies.append(
                pltpu.make_async_copy(
                    source, rowbuf.at[kind, :, 1 : layers + 1], halo_sem.at[2 + kind]
                )
            )
        for n, source in enumerate((c00_ref, c01_ref, c10_ref, c11_ref)):
            row_kind, depth_kind = n // 2, n % 2
            is_above = row_odd if row_kind == 0 else 1 - row_odd
            is_front = depth_odd if depth_kind == 0 else 1 - depth_odd
            target = rowbuf.at[row_kind, :, (1 - is_front) * (layers + 1), is_above]
            copies.append(pltpu.make_async_copy(source, target, halo_sem.at[4 + n]))
        return copies

    def layer_copies(z):
        return (
            pltpu.make_async_copy(den_ref.at[z], incoming.at[0, z + 2], layer_sem.at[z, 0]),
            pltpu.make_async_copy(vel_ref.at[:, z], incoming.at[1:4, z + 2], layer_sem.at[z, 1]),
        )

    def row_of(j, row):
        return PITCH * j + SUB + row

    def store_sides(west_ref, east_ref, slot, c, t, j, value):
        to_right = pltpu.roll(value, 1, 1)
        to_left = pltpu.roll(value, LANES - 1, 1)

        def at(ref, jj):
            return ref.at[slot, c, pl.ds(jj * rows + t * SUB, SUB), :]

        pltpu.store(at(west_ref, j), to_right, mask=not_first)
        pltpu.store(at(east_ref, j), to_left, mask=not_last)
        if j < spans - 1:
            pltpu.store(at(west_ref, j + 1), to_right, mask=first)
        if j > 0:
            pltpu.store(at(east_ref, j - 1), to_left, mask=last)

    def load_tile(n, slot, t, j):
        for c in range(4):
            value = incoming[c, n, t * SUB : (t + 1) * SUB, j * LANES : (j + 1) * LANES]
            base[slot, c, pl.ds(row_of(j, t * SUB), SUB), :] = value
            store_sides(west, east, slot, c, t, j, value)

    def load_rows(n, slot):
        z = jnp.clip(n - 1, 0, layers + 1)
        for c in range(4):
            for k in range(2):
                for row, kind in ((k - 2, above), (rows + k, below)):
                    base[slot, c, pl.ds(row_of(0, row), spans, stride=PITCH), :] = rowbuf[
                        kind, c, z, k
                    ]

    def neighbours(cells, west_ref, east_ref, slot, t, j):
        oldest, middle, newest = (slot + 2) % 4, (slot + 3) % 4, slot

        def at(which, row):
            return [cells[which, c, pl.ds(row_of(j, row), SUB), :] for c in range(4)]

        def beside(ref):
            return [ref[middle, c, pl.ds(j * rows + t * SUB, SUB), :] for c in range(4)]

        row = t * SUB
        return (
            at(middle, row), at(middle, row - 1), at(middle, row + 1),
            beside(west_ref), beside(east_ref), at(oldest, row), at(newest, row),
        )

    def first_step(slot, keep):
        oldest, middle, newest = (slot + 2) % 4, (slot + 3) % 4, slot
        for row, exists in ((-1, row_rank > 0), (rows, row_rank < row_count - 1)):

            def at(which, r):
                return [
                    base[which, c, pl.ds(row_of(0, r), spans, stride=PITCH), :] for c in range(4)
                ]

            here = at(middle, row)
            left, right = [], []
            for value in here:
                before = jnp.where(sub == 0, 0.0, pltpu.roll(value, 1, 0))
                after = jnp.where(sub == SUB - 1, 0.0, pltpu.roll(value, SUB - 1, 0))
                left.append(pltpu.roll(jnp.where(last, before, value), 1, 1))
                right.append(pltpu.roll(jnp.where(first, after, value), LANES - 1, 1))
            new = advance(
                here, at(middle, row - 1), at(middle, row + 1), left, right,
                at(oldest, row), at(newest, row),
            )
            inside = jnp.full((SUB, LANES), jnp.where(exists, 1, 0), jnp.int32) == 1
            for c in range(4):
                sbase[slot, c, pl.ds(row_of(0, row), spans, stride=PITCH), :] = jnp.where(
                    inside, new[c], 0.0
                )
        for j in range(spans):
            for t in range(own_tiles):
                new = advance(*neighbours(base, west, east, slot, t, j))
                for c in range(4):
                    value = new[c] if keep is None else jnp.where(keep, new[c], 0.0)
                    sbase[slot, c, pl.ds(row_of(j, t * SUB), SUB), :] = value
                    store_sides(swest, seast, slot, c, t, j, value)

    @pl.when(step == 0)
    def _():
        for copy in halo_copies():
            copy.start()
        for z in range(layers):
            for copy in layer_copies(z):
                copy.start()
        edge = jnp.zeros((rows, LANES), jnp.float32)
        for slot in range(4):
            for c in range(4):
                west[slot, c, 0:rows, :] = edge
                swest[slot, c, 0:rows, :] = edge
                east[slot, c, (spans - 1) * rows : spans * rows, :] = edge
                seast[slot, c, (spans - 1) * rows : spans * rows, :] = edge
        for c in range(3):
            accum[c] = jnp.zeros((spans * rows, LANES), jnp.float32)
        accum[3] = jnp.ones((spans * rows, LANES), jnp.float32)
        for copy in halo_copies():
            copy.wait()
        for z in range(3):
            for copy in layer_copies(z):
                copy.wait()
        for n in range(5):
            load_rows(n, n % 4)
            for j in range(spans):
                for t in range(own_tiles):
                    load_tile(n, n % 4, t, j)
            if n == 2:
                first_step(2, jnp.full((SUB, LANES), depth_rank, jnp.int32) > 0)
            if n == 3:
                first_step(3, None)

    @pl.when(step < layers // 4 - 1)
    def _():
        for q in range(4):
            for copy in layer_copies(4 * step + 3 + q):
                copy.wait()

    @pl.when(step == layers // 4 - 1)
    def _():
        for copy in layer_copies(layers - 1):
            copy.wait()

    rate = -OPTICAL / (layers * depth_count) / math.log(2.0)
    mix = [[0.5 * palette_ref[c, k] for k in range(4)] for c in range(3)]
    final_outside = (step == layers // 4 - 1) & (depth_rank == depth_count - 1)
    final_keep = jnp.full((SUB, LANES), jnp.where(final_outside, 0, 1), jnp.int32) == 1

    for q in range(4):
        first_step(q, final_keep if q == 3 else None)
        n = jnp.minimum(4 * step + 5 + q, layers + 3)
        load_rows(n, (q + 1) % 4)
        for j in range(spans):
            for t in range(own_tiles):
                load_tile(n, (q + 1) % 4, t, j)
                new = advance(*neighbours(sbase, swest, seast, q, t, j))
                there = (slice(t * SUB, (t + 1) * SUB), slice(j * LANES, (j + 1) * LANES))
                den_out[(q,) + there] = new[0]
                for c in range(3):
                    vel_out[(c, q) + there] = new[c + 1]
                pixels = pl.ds(j * rows + t * SUB, SUB)
                before = accum[3, pixels, :]
                passed = before * jnp.exp2(rate * (new[0] * new[0]))
                weight = before - passed
                accum[3, pixels, :] = passed
                for c in range(3):
                    mixed = (mix[c][0] * new[0] + mix[c][1] * new[1]) + (
                        mix[c][2] * new[2] + mix[c][3] * new[3]
                    )
                    accum[c, pixels, :] = accum[c, pixels, :] + weight * jnp.tanh(mixed)

    @pl.when(step == layers // 4 - 1)
    def _():
        width = columns // depth_count
        per_piece = width // LANES

        def channels(j, t):
            pixels = pl.ds(j * rows + t * SUB, SUB)
            through = accum[3, pixels, :]
            return [0.5 * (accum[c, pixels, :] + (1.0 - through)) for c in range(3)] + [through]

        for k in range(depth_count):
            piece = depth_rank ^ k
            start = piece * per_piece
            for t in range(own_tiles):
                r = slice(t * SUB, (t + 1) * SUB)
                for jj in range(per_piece):
                    values = channels(start + jj, t)
                    for c in range(4):
                        pieces[k][r, c * width + jj * LANES : c * width + (jj + 1) * LANES] = (
                            values[c]
                        )
                before = channels(jnp.maximum(start - 1, 0), t)
                after = channels(jnp.minimum(start + per_piece, spans - 1), t)
                edge = jnp.zeros((SUB, LANES), jnp.float32)
                for c in range(4):
                    for values, low in ((before, 4 * c), (after, 4 * c + 2)):
                        turned = pltpu.roll(values[c], (4 * c + 2) % LANES, 1)
                        edge = jnp.where((lane >= low) & (lane < low + 2), turned, edge)
                pieces[k][r, 4 * width : 4 * width + LANES] = edge


def over_kernel(*refs, count, width):
    parts = refs[:count]
    picture_ref, swap0_ref, swap1_ref = refs[count:]
    rows = picture_ref.shape[0]
    depth_rank = lax.axis_index("depth")
    row_odd = lax.rem(lax.axis_index("row"), 2)
    lane = lax.broadcasted_iota(jnp.int32, (rows, LANES), 1)

    def split(ref):
        return [ref[:, c * width : (c + 1) * width] for c in range(4)] + [
            ref[:, 4 * width : 4 * width + LANES]
        ]

    def spread_through(edge):
        out = jnp.ones_like(edge)
        for c in range(3):
            turned = pltpu.roll(edge, LANES - 12 + 4 * c, 1)
            out = jnp.where((lane >= 4 * c) & (lane < 4 * c + 4), turned, out)
        return out

    def over(swapped, a, b):
        near = [jnp.where(swapped, y, x) for x, y in zip(a, b)]
        far = [jnp.where(swapped, x, y) for x, y in zip(a, b)]
        out = [near[c] + near[3] * far[c] for c in range(3)]
        out.append(near[3] * far[3])
        edge = near[4] + spread_through(near[4]) * far[4]
        out.append(jnp.where(lane >= 12, near[4] * far[4], edge))
        return out

    values = [split(ref) for ref in parts]
    bit = 0
    while len(values) > 1:
        swapped = (depth_rank >> bit & 1) == 1
        values = [over(swapped, values[k], values[k + 1]) for k in range(0, len(values), 2)]
        bit += 1
    final = values[0]
    for c in range(4):
        picture_ref[:, c * width : (c + 1) * width] = (1.0 - final[3]) if c == 3 else final[c]
    edge = jnp.where((lane >= 12) & (lane < 16), 1.0 - final[4], final[4])
    picture_ref[:, 4 * width : 4 * width + LANES] = edge
    top, bottom = picture_ref[0:SUB, :], picture_ref[rows - SUB : rows, :]
    odd = row_odd == 1
    swap0_ref[...] = jnp.where(odd, top, bottom)
    swap1_ref[...] = jnp.where(odd, bottom, top)


def filter_kernel(picture_ref, swap0_ref, swap1_ref, out_ref, *, width, row_count, depth_count):
    row_rank, depth_rank = lax.axis_index("row"), lax.axis_index("depth")
    odd = lax.rem(row_rank, 2) == 1
    rows = picture_ref.shape[0]
    own_tiles = rows // SUB
    spans = width // LANES
    lane = lax.broadcasted_iota(jnp.int32, (SUB, LANES), 1)
    sub = lax.broadcasted_iota(jnp.int32, (SUB, LANES), 0)

    def tile(t, c, j):
        if j == -1 or j == spans:
            cols = slice(4 * width, 4 * width + LANES)
        else:
            cols = slice(c * width + j * LANES, c * width + (j + 1) * LANES)
        if t == -1:
            v = jnp.where(odd, swap0_ref[:, cols], swap1_ref[:, cols])
        elif t == own_tiles:
            v = jnp.where(odd, swap1_ref[:, cols], swap0_ref[:, cols])
        else:
            v = picture_ref[t * SUB : (t + 1) * SUB, cols]
        if j == -1:
            v = pltpu.roll(v, LANES - 2 - 4 * c, 1)
        elif j == spans:
            v = pltpu.roll(v, (LANES - 2 - 4 * c) % LANES, 1)
        return v

    tiles = {}
    for t in range(-1, own_tiles + 1):
        for j in range(-1, spans + 1):
            four = [tile(t, c, j) for c in range(4)]
            tiles[t, j] = four + [(four[0] + four[1] + four[2]) / 3.0]

    def column_shift(t, j, q, dx):
        if dx == 0:
            return tiles[t, j][q]
        if dx > 0:
            mixed = jnp.where(lane < dx, tiles[t, j + 1][q], tiles[t, j][q])
        else:
            mixed = jnp.where(lane >= LANES + dx, tiles[t, j - 1][q], tiles[t, j][q])
        return pltpu.roll(mixed, (-dx) % LANES, 1)

    no_above, no_below = row_rank == 0, row_rank == row_count - 1
    no_west, no_east = depth_rank == 0, depth_rank == depth_count - 1
    for j in range(spans):
        sums = [[None] * 5 for _ in range(own_tiles)]
        for dx in range(-2, 3):
            shifted = {
                t: [column_shift(t, j, q, dx) for q in range(5)] for t in range(-1, own_tiles + 1)
            }
            for dy in range(-2, 3):
                spatial = -(dx * dx + dy * dy) / (2.0 * SPACE_SCALE * SPACE_SCALE)
                for t in range(own_tiles):
                    if dy == 0:
                        near = shifted[t]
                    elif dy > 0:
                        near = [
                            pltpu.roll(
                                jnp.where(sub < dy, shifted[t + 1][q], shifted[t][q]), SUB - dy, 0
                            )
                            for q in range(5)
                        ]
                    else:
                        near = [
                            pltpu.roll(
                                jnp.where(sub >= SUB + dy, shifted[t - 1][q], shifted[t][q]), -dy, 0
                            )
                            for q in range(5)
                        ]
                    diff = near[4] - tiles[t, j][4]
                    weight = jnp.exp(
                        spatial - diff * diff * (1.0 / (2.0 * RANGE_SCALE * RANGE_SCALE))
                    )
                    blocked = None
                    if t == 0 and dy < 0:
                        blocked = no_above & (sub < -dy)
                    if t == own_tiles - 1 and dy > 0:
                        blocked = no_below & (sub >= SUB - dy)
                    if j == 0 and dx < 0:
                        side = no_west & (lane < -dx)
                        blocked = side if blocked is None else blocked | side
                    if j == spans - 1 and dx > 0:
                        side = no_east & (lane >= LANES - dx)
                        blocked = side if blocked is None else blocked | side
                    if blocked is not None:
                        weight = jnp.where(blocked, 0.0, weight)
                    terms = [weight * near[c] for c in range(4)] + [weight]
                    sums[t] = terms if sums[t][0] is None else [a + b for a, b in zip(sums[t], terms)]
        for t in range(own_tiles):
            inverse = 1.0 / sums[t][4]
            for c in range(4):
                out_ref[c, t * SUB : (t + 1) * SUB, j * LANES : (j + 1) * LANES] = (
                    sums[t][c] * inverse
                )


def body(density, velocity, palette):
    layers, rows, columns = density.shape
    depth_count, row_count = lax.axis_size("depth"), lax.axis_size("row")
    spans, own_tiles = columns // LANES, rows // SUB
    width = columns // depth_count
    line = 4 * width + LANES
    assert spans == SUB and rows % SUB == 0 and width % LANES == 0 and layers % 4 == 0
    vmem = pl.BlockSpec(memory_space=pltpu.VMEM)
    smem = pl.BlockSpec(memory_space=pltpu.SMEM)
    anywhere = pl.BlockSpec(memory_space=pl.ANY)
    f32 = jnp.float32

    def shape(*dims):
        return jax.ShapeDtypeStruct(dims, f32)

    row_shape = (4, layers, 2, spans, LANES)
    depth_shape = (4, 2, rows, columns)
    corner_shape = (4, spans, LANES)
    row0, row1, depth0, depth1, *corners = pl.pallas_call(
        functools.partial(pack_kernel, layers=layers, rows=rows, spans=spans, chunks=4),
        out_shape=(shape(*row_shape),) * 2 + (shape(*depth_shape),) * 2 + (shape(*corner_shape),) * 4,
        in_specs=[anywhere, anywhere],
        out_specs=(anywhere,) * 8,
        scratch_shapes=[
            pltpu.VMEM((4, layers, rows, columns), f32),
            pltpu.VMEM((2,) + row_shape, f32),
            pltpu.SemaphoreType.DMA((4, 2)),
            pltpu.SemaphoreType.DMA((2,)),
            pltpu.SemaphoreType.DMA((2,)),
            pltpu.SemaphoreType.DMA((4,)),
        ],
        name="pack",
    )(density, velocity)
    row1, row0 = swap_rows(row1, 1), swap_rows(row0, 0)
    depth0, depth1 = swap_depths(depth0, 0), swap_depths(depth1, 1)
    corners = [swap_corners(corner, k // 2, k % 2) for k, corner in enumerate(corners)]

    settled, moving, *parts = pl.pallas_call(
        functools.partial(
            settle_kernel, layers=layers, rows=rows, columns=columns,
            depth_count=depth_count, row_count=row_count,
        ),
        grid=(layers // 4,),
        out_shape=(shape(layers, rows, columns), shape(3, layers, rows, columns))
        + (shape(rows, line),) * depth_count,
        in_specs=[smem] + [anywhere] * 10,
        out_specs=(
            pl.BlockSpec((4, rows, columns), lambda i: (i, 0, 0)),
            pl.BlockSpec((3, 4, rows, columns), lambda i: (0, i, 0, 0)),
        )
        + (vmem,) * depth_count,
        scratch_shapes=[
            pltpu.VMEM((4, layers + 4, rows, columns), f32),
            pltpu.VMEM((2, 4, layers + 2, 2, spans, LANES), f32),
        ]
        + [
            pltpu.VMEM((4, 4, spans * PITCH, LANES), f32),
            pltpu.VMEM((4, 4, spans * rows, LANES), f32),
            pltpu.VMEM((4, 4, spans * rows, LANES), f32),
        ] * 2
        + [
            pltpu.VMEM((4, spans * rows, LANES), f32),
            pltpu.SemaphoreType.DMA((layers, 2)),
            pltpu.SemaphoreType.DMA((8,)),
        ],
        name="settle",
    )(palette, density, velocity, row0, row1, depth0, depth1, *corners)

    parts = [
        lax.ppermute(part, "depth", [(i, i ^ k) for i in range(depth_count)]) if k else part
        for k, part in enumerate(parts)
    ]
    composed, swap0, swap1 = pl.pallas_call(
        functools.partial(over_kernel, count=depth_count, width=width),
        out_shape=(shape(rows, line), shape(SUB, line), shape(SUB, line)),
        in_specs=[vmem] * depth_count,
        out_specs=(vmem, vmem, vmem),
        name="over",
    )(*parts)

    swap1, swap0 = swap_rows(swap1, 1), swap_rows(swap0, 0)
    filtered = pl.pallas_call(
        functools.partial(
            filter_kernel, width=width, row_count=row_count, depth_count=depth_count
        ),
        out_shape=shape(4, rows, width),
        in_specs=[vmem] * 3,
        out_specs=vmem,
        name="bilateral",
    )(composed, swap0, swap1)
    return (filtered, settled, moving)


def solution(mesh):
    in_specs = (P("depth", "row", None), P(None, "depth", "row", None), P())
    out_specs = (P(None, "row", "depth"), P("depth", "row", None), P(None, "depth", "row", None))
    return jax.shard_map(body, mesh=mesh, in_specs=in_specs, out_specs=out_specs, check_vma=False)
```

```python
import functools
import math

import jax
import jax.numpy as jnp
from jax import lax
from jax.experimental import pallas as pl
from jax.experimental.pallas import tpu as pltpu
from jax.sharding import PartitionSpec as P

DIFFUSION = 0.1
ADVECTION = 0.25
VISCOSITY = 0.15
FRICTION = 0.2
OPTICAL = 2.0
RANGE_SCALE = 0.1
SPACE_SCALE = 1.5
SUB = 8
LANES = 128
PITCH = 40
AXES = ("row", "depth")


def row_pairs(kind, count):
    pairs = []
    for low in range(kind, count - 1, 2):
        pairs += [(low, low + 1), (low + 1, low)]
    return pairs


def swap_rows(array, kind):
    return lax.ppermute(array, "row", row_pairs(kind, lax.axis_size("row")))


def swap_depths(array, kind):
    return lax.ppermute(array, "depth", row_pairs(kind, lax.axis_size("depth")))


def swap_corners(array, row_kind, depth_kind):
    depths = lax.axis_size("depth")
    pairs = [
        (a * depths + c, b * depths + d)
        for a, b in row_pairs(row_kind, lax.axis_size("row"))
        for c, d in row_pairs(depth_kind, depths)
    ]
    return lax.ppermute(array, AXES, pairs)


def in_vmem(array):
    return pltpu.with_memory_space_constraint(array, pltpu.VMEM)


def pack_kernel(
    den_ref, vel_ref, row0_ref, row1_ref, depth0_ref, depth1_ref, c00_ref, c01_ref, c10_ref, c11_ref,
    block, sides, load_sem, row_sem, depth_sem, corner_sem, *, layers, rows, spans, chunks,
):
    row_odd = lax.rem(lax.axis_index("row"), 2)
    depth_odd = lax.rem(lax.axis_index("depth"), 2)
    size = layers // chunks

    def loads(k):
        z = slice(k * size, (k + 1) * size)
        return (
            pltpu.make_async_copy(den_ref.at[z], block.at[0, z], load_sem.at[k, 0]),
            pltpu.make_async_copy(vel_ref.at[:, z], block.at[1:4, z], load_sem.at[k, 1]),
        )

    for k in range(chunks):
        for copy in loads(k):
            copy.start()
    row_side = (1 - row_odd, row_odd)
    depth_side = (1 - depth_odd, depth_odd)
    sends = []
    for k in range(chunks):
        for copy in loads(k):
            copy.wait()
        for c in range(4):
            for z in range(k * size, (k + 1) * size):
                for side in range(2):
                    for n in range(2):
                        row = n + side * (rows - 2)
                        for j in range(spans):
                            sides[side, c, z, n, j : j + 1, :] = block[
                                c, z, row : row + 1, j * LANES : (j + 1) * LANES
                            ]
    for kind, target in ((0, row0_ref), (1, row1_ref)):
        sends.append(pltpu.make_async_copy(sides.at[row_side[kind]], target, row_sem.at[kind]))
    for kind, target in ((0, depth0_ref), (1, depth1_ref)):
        source = block.at[:, pl.ds(depth_side[kind] * (layers - 2), 2)]
        sends.append(pltpu.make_async_copy(source, target, depth_sem.at[kind]))
    for n, target in enumerate((c00_ref, c01_ref, c10_ref, c11_ref)):
        source = sides.at[
            row_side[n // 2], :, depth_side[n % 2] * (layers - 1), row_side[n // 2]
        ]
        sends.append(pltpu.make_async_copy(source, target, corner_sem.at[n]))
    for copy in sends:
        copy.start()
    for copy in sends:
        copy.wait()


def row_of(j, row):
    return PITCH * j + SUB + row


def advance(here, up, down, left, right, front, back):
    around = [
        ((front[c] + back[c]) + (up[c] + down[c])) + (left[c] + right[c]) for c in range(4)
    ]
    flux = (
        (right[0] * right[1] - left[0] * left[1])
        + (down[0] * down[2] - up[0] * up[2])
        + (back[0] * back[3] - front[0] * front[3])
    )
    squared = here[0] * here[0]
    new = [
        (1.0 - 6.0 * DIFFUSION) * here[0] + (DIFFUSION * around[0] - (0.5 * ADVECTION) * flux)
    ]
    inverse = 1.0 / ((1.0 + squared) * (1.0 + FRICTION * squared))
    own_share = (1.0 + (1.0 - 6.0 * VISCOSITY) * squared) * inverse
    near_share = (VISCOSITY * squared) * inverse
    for c in range(1, 4):
        new.append(here[c] * own_share + around[c] * near_share)
    return new, near_share


def late_share(value, neighbour, near_share, along, sign):
    out = [
        value[0]
        + neighbour[0] * (DIFFUSION + (sign * 0.5 * ADVECTION) * neighbour[along])
    ]
    return out + [value[c] + near_share * neighbour[c] for c in range(1, 4)]


def neighbours(cells, slots, t, j, spans, first, last):
    oldest, middle, newest = slots
    row = t * SUB

    def at(which, r, jj=j):
        return [cells[which, c, pl.ds(row_of(jj, r), SUB), :] for c in range(4)]

    here = at(middle, row)
    zeros = [jnp.zeros((SUB, LANES), jnp.float32)] * 4
    before = at(middle, row, j - 1) if j > 0 else zeros
    after = at(middle, row, j + 1) if j < spans - 1 else zeros
    left = [pltpu.roll(jnp.where(last, b, x), 1, 1) for b, x in zip(before, here)]
    right = [pltpu.roll(jnp.where(first, a, x), LANES - 1, 1) for a, x in zip(after, here)]
    return (
        here, at(middle, row - 1), at(middle, row + 1), left, right,
        at(oldest, row), at(newest, row),
    )


def interior_kernel(
    den_ref, vel_ref, early_ref, share_ref, edge_ref, base, *, layers, rows, columns
):
    step = pl.program_id(0)
    own_tiles, spans = rows // SUB, columns // LANES
    lane = lax.broadcasted_iota(jnp.int32, (SUB, LANES), 1)
    first, last = lane == 0, lane == LANES - 1

    @pl.when(step == 0)
    def _():
        line = jnp.zeros((spans, LANES), jnp.float32)
        for slot in range(4):
            for c in range(4):
                for row in (-1, rows):
                    base[slot, c, pl.ds(row_of(0, row), spans, stride=PITCH), :] = line
        base[3] = jnp.zeros((4, spans * PITCH, LANES), jnp.float32)
        base[2] = jnp.zeros((4, spans * PITCH, LANES), jnp.float32)

    def first_step(z, slots):
        for j in range(spans):
            for t in range(own_tiles):
                new, share = advance(*neighbours(base, slots, t, j, spans, first, last))
                cells = pl.ds(j * rows + t * SUB, SUB)
                share_ref[z, cells, :] = share
                for c in range(4):
                    early_ref[z, c, cells, :] = new[c]

    for q in range(4):
        z = 4 * step + q
        for t in range(own_tiles):
            for j in range(spans):
                there = (slice(t * SUB, (t + 1) * SUB), slice(j * LANES, (j + 1) * LANES))
                for c in range(4):
                    base[q, c, pl.ds(row_of(j, t * SUB), SUB), :] = (
                        den_ref[(q,) + there] if c == 0 else vel_ref[(c - 1, q) + there]
                    )
        for side, row in ((0, 0), (1, rows - 1)):
            for c in range(4):
                edge_ref[z, side, c] = base[q, c, pl.ds(row_of(0, row), spans, stride=PITCH), :]
        first_step(jnp.maximum(z - 1, 0), ((q + 2) % 4, (q + 3) % 4, q))

    @pl.when(step == layers // 4 - 1)
    def _():
        base[0] = jnp.zeros((4, spans * PITCH, LANES), jnp.float32)
        first_step(layers - 1, (2, 3, 0))


def settle_kernel(
    palette_ref, den_ref, vel_ref, row0_ref, row1_ref, depth0_ref, depth1_ref,
    c00_ref, c01_ref, c10_ref, c11_ref, early_ref, share_ref, edge_ref, den_out, vel_out, *rest,
    layers, rows, columns, depth_count, row_count,
):
    pieces = rest[:depth_count]
    outer, rowbuf, base, sbase, accum, outer_sem = rest[depth_count:]
    step = pl.program_id(0)
    steps = layers // 4
    own_tiles, spans = rows // SUB, columns // LANES
    row_rank, depth_rank = lax.axis_index("row"), lax.axis_index("depth")
    row_odd, depth_odd = lax.rem(row_rank, 2), lax.rem(depth_rank, 2)
    above, below = 1 - row_odd, row_odd
    sub = lax.broadcasted_iota(jnp.int32, (SUB, LANES), 0)
    lane = lax.broadcasted_iota(jnp.int32, (SUB, LANES), 1)
    first, last = lane == 0, lane == LANES - 1
    from_front = jnp.full((SUB, LANES), depth_odd, jnp.int32) == 1

    def outer_copies():
        copies = []
        for n, z in ((0, 0), (1, layers - 1)):
            copies.append(pltpu.make_async_copy(den_ref.at[z], outer.at[n, 0], outer_sem.at[n, 0]))
            copies.append(
                pltpu.make_async_copy(vel_ref.at[:, z], outer.at[n, 1:4], outer_sem.at[n, 1])
            )
        return copies

    tiles = [(t, j) for j in range(spans) for t in range(own_tiles)]

    def tile_of(t, j):
        return slice(t * SUB, (t + 1) * SUB), slice(j * LANES, (j + 1) * LANES)

    def cells_of(t, j):
        return pl.ds(j * rows + t * SUB, SUB)

    def line(row):
        return pl.ds(row_of(0, row), spans, stride=PITCH)

    def outer_step(slot, front):
        kept = (depth_rank > 0) if front else (depth_rank < depth_count - 1)
        keep = jnp.full((SUB, LANES), jnp.where(kept, 1, 0), jnp.int32) == 1
        chosen = from_front if front else jnp.logical_not(from_front)
        far, near = (0, 1) if front else (1, 0)
        for t, j in tiles:
            there = tile_of(t, j)
            for c in range(4):
                for k, n in ((0, far), (1, near)):
                    base[k, c, pl.ds(row_of(j, t * SUB), SUB), :] = jnp.where(
                        chosen, depth0_ref[(c, n) + there], depth1_ref[(c, n) + there]
                    )
                base[2, c, pl.ds(row_of(j, t * SUB), SUB), :] = outer[
                    (0 if front else 1, c) + there
                ]
        z = 0 if front else layers + 1
        for c in range(4):
            base[1, c, line(-1), :] = rowbuf[above, c, z, 1]
            base[1, c, line(rows), :] = rowbuf[below, c, z, 0]
        slots = (0, 1, 2) if front else (2, 1, 0)
        for t, j in tiles:
            new, unused = advance(*neighbours(base, slots, t, j, spans, first, last))
            for c in range(4):
                sbase[slot, c, pl.ds(row_of(j, t * SUB), SUB), :] = jnp.where(keep, new[c], 0.0)

    def add_layer(z, slot, sign):
        for t, j in tiles:
            cells = pl.ds(row_of(j, t * SUB), SUB)
            new = late_share(
                [sbase[slot, c, cells, :] for c in range(4)],
                [base[1, c, cells, :] for c in range(4)],
                share_ref[z, cells_of(t, j), :], 3, sign,
            )
            for c in range(4):
                sbase[slot, c, cells, :] = new[c]

    def take_layer(z, slot):
        for t, j in tiles:
            for c in range(4):
                sbase[slot, c, pl.ds(row_of(j, t * SUB), SUB), :] = early_ref[z, c, cells_of(t, j), :]
        for side, kind, k, row, exists in (
            (0, above, 1, -1, row_rank > 0), (1, below, 0, rows, row_rank < row_count - 1),
        ):
            own_row = 0 if side == 0 else rows - 1
            own_cells = pl.ds(own_row, spans, stride=rows)

            def halo(layer, n):
                return [rowbuf[kind, c, layer, n] for c in range(4)]

            here, farther = halo(z + 1, k), halo(z + 1, 1 - k)
            own = [edge_ref[z, side, c] for c in range(4)]
            new = late_share(
                [early_ref[z, c, own_cells, :] for c in range(4)], here,
                share_ref[z, own_cells, :], 2, 1.0 if side == 0 else -1.0,
            )
            for c in range(4):
                sbase[slot, c, line(own_row), :] = new[c]
            left, right = [], []
            for value in here:
                before = jnp.where(sub == 0, 0.0, pltpu.roll(value, 1, 0))
                after = jnp.where(sub == SUB - 1, 0.0, pltpu.roll(value, SUB - 1, 0))
                left.append(pltpu.roll(jnp.where(last, before, value), 1, 1))
                right.append(pltpu.roll(jnp.where(first, after, value), LANES - 1, 1))
            up, down = (farther, own) if side == 0 else (own, farther)
            new, unused = advance(here, up, down, left, right, halo(z, k), halo(z + 2, k))
            inside = jnp.full((SUB, LANES), jnp.where(exists, 1, 0), jnp.int32) == 1
            for c in range(4):
                sbase[slot, c, line(row), :] = jnp.where(inside, new[c], 0.0)

    @pl.when(step == 0)
    def _():
        for copy in outer_copies():
            copy.start()
        for kind, source in ((0, row0_ref), (1, row1_ref)):
            for c in range(4):
                for z in range(layers):
                    for k in range(2):
                        rowbuf[kind, c, z + 1, k] = source[c, z, k]
        for n, source in enumerate((c00_ref, c01_ref, c10_ref, c11_ref)):
            row_kind, depth_kind = n // 2, n % 2
            is_above = row_odd if row_kind == 0 else 1 - row_odd
            is_front = depth_odd if depth_kind == 0 else 1 - depth_odd
            for c in range(4):
                rowbuf[row_kind, c, (1 - is_front) * (layers + 1), is_above] = source[c]
        for c in range(3):
            accum[c] = jnp.zeros((spans * rows, LANES), jnp.float32)
        accum[3] = jnp.ones((spans * rows, LANES), jnp.float32)
        for copy in outer_copies():
            copy.wait()
        outer_step(3, True)
        take_layer(0, 0)
        add_layer(0, 0, 1.0)

    rate = -OPTICAL / (layers * depth_count) / math.log(2.0)
    mix = [[0.5 * palette_ref[c, k] for k in range(4)] for c in range(3)]

    def second_step(q):
        for t, j in tiles:
            slots = ((q + 3) % 4, q, (q + 1) % 4)
            new, unused = advance(*neighbours(sbase, slots, t, j, spans, first, last))
            there = tile_of(t, j)
            den_out[(q,) + there] = new[0]
            for c in range(3):
                vel_out[(c, q) + there] = new[c + 1]
            pixels = cells_of(t, j)
            before = accum[3, pixels, :]
            passed = before * jnp.exp2(rate * (new[0] * new[0]))
            weight = before - passed
            accum[3, pixels, :] = passed
            for c in range(3):
                mixed = (mix[c][0] * new[0] + mix[c][1] * new[1]) + (
                    mix[c][2] * new[2] + mix[c][3] * new[3]
                )
                accum[c, pixels, :] = accum[c, pixels, :] + weight * jnp.tanh(mixed)

    for q in range(3):
        take_layer(4 * step + q + 1, q + 1)
        if q == 2:

            @pl.when(step == steps - 1)
            def _():
                outer_step(0, False)
                add_layer(layers - 1, 3, -1.0)

        second_step(q)

    @pl.when(step < steps - 1)
    def _():
        take_layer(4 * step + 4, 0)

    second_step(3)

    @pl.when(step == steps - 1)
    def _():
        width = columns // depth_count
        per_piece = width // LANES

        def channels(j, t):
            pixels = pl.ds(j * rows + t * SUB, SUB)
            through = accum[3, pixels, :]
            return [0.5 * (accum[c, pixels, :] + (1.0 - through)) for c in range(3)] + [through]

        for k in range(depth_count):
            piece = depth_rank ^ k
            start = piece * per_piece
            for t in range(own_tiles):
                r = slice(t * SUB, (t + 1) * SUB)
                for jj in range(per_piece):
                    values = channels(start + jj, t)
                    for c in range(4):
                        pieces[k][r, c * width + jj * LANES : c * width + (jj + 1) * LANES] = (
                            values[c]
                        )
                before = channels(jnp.maximum(start - 1, 0), t)
                after = channels(jnp.minimum(start + per_piece, spans - 1), t)
                edge = jnp.zeros((SUB, LANES), jnp.float32)
                for c in range(4):
                    for values, low in ((before, 4 * c), (after, 4 * c + 2)):
                        turned = pltpu.roll(values[c], (4 * c + 2) % LANES, 1)
                        edge = jnp.where((lane >= low) & (lane < low + 2), turned, edge)
                pieces[k][r, 4 * width : 4 * width + LANES] = edge


def over_kernel(*refs, count, width):
    parts = refs[:count]
    picture_ref, swap0_ref, swap1_ref = refs[count:]
    rows = picture_ref.shape[0]
    depth_rank = lax.axis_index("depth")
    row_odd = lax.rem(lax.axis_index("row"), 2)
    lane = lax.broadcasted_iota(jnp.int32, (rows, LANES), 1)

    def split(ref):
        return [ref[:, c * width : (c + 1) * width] for c in range(4)] + [
            ref[:, 4 * width : 4 * width + LANES]
        ]

    def spread_through(edge):
        out = jnp.ones_like(edge)
        for c in range(3):
            turned = pltpu.roll(edge, LANES - 12 + 4 * c, 1)
            out = jnp.where((lane >= 4 * c) & (lane < 4 * c + 4), turned, out)
        return out

    def over(swapped, a, b):
        near = [jnp.where(swapped, y, x) for x, y in zip(a, b)]
        far = [jnp.where(swapped, x, y) for x, y in zip(a, b)]
        out = [near[c] + near[3] * far[c] for c in range(3)]
        out.append(near[3] * far[3])
        edge = near[4] + spread_through(near[4]) * far[4]
        out.append(jnp.where(lane >= 12, near[4] * far[4], edge))
        return out

    values = [split(ref) for ref in parts]
    bit = 0
    while len(values) > 1:
        swapped = (depth_rank >> bit & 1) == 1
        values = [over(swapped, values[k], values[k + 1]) for k in range(0, len(values), 2)]
        bit += 1
    final = values[0]
    for c in range(4):
        picture_ref[:, c * width : (c + 1) * width] = (1.0 - final[3]) if c == 3 else final[c]
    edge = jnp.where((lane >= 12) & (lane < 16), 1.0 - final[4], final[4])
    picture_ref[:, 4 * width : 4 * width + LANES] = edge
    top, bottom = picture_ref[0:SUB, :], picture_ref[rows - SUB : rows, :]
    odd = row_odd == 1
    swap0_ref[...] = jnp.where(odd, top, bottom)
    swap1_ref[...] = jnp.where(odd, bottom, top)


def filter_kernel(picture_ref, swap0_ref, swap1_ref, out_ref, *, width, row_count, depth_count):
    row_rank, depth_rank = lax.axis_index("row"), lax.axis_index("depth")
    odd = lax.rem(row_rank, 2) == 1
    rows = picture_ref.shape[0]
    own_tiles = rows // SUB
    spans = width // LANES
    lane = lax.broadcasted_iota(jnp.int32, (SUB, LANES), 1)
    sub = lax.broadcasted_iota(jnp.int32, (SUB, LANES), 0)

    def tile(t, c, j):
        if j == -1 or j == spans:
            cols = slice(4 * width, 4 * width + LANES)
        else:
            cols = slice(c * width + j * LANES, c * width + (j + 1) * LANES)
        if t == -1:
            v = jnp.where(odd, swap0_ref[:, cols], swap1_ref[:, cols])
        elif t == own_tiles:
            v = jnp.where(odd, swap1_ref[:, cols], swap0_ref[:, cols])
        else:
            v = picture_ref[t * SUB : (t + 1) * SUB, cols]
        if j == -1:
            v = pltpu.roll(v, LANES - 2 - 4 * c, 1)
        elif j == spans:
            v = pltpu.roll(v, (LANES - 2 - 4 * c) % LANES, 1)
        return v

    tiles = {}
    for t in range(-1, own_tiles + 1):
        for j in range(-1, spans + 1):
            four = [tile(t, c, j) for c in range(4)]
            tiles[t, j] = four + [(four[0] + four[1] + four[2]) / 3.0]

    def column_shift(t, j, q, dx):
        if dx == 0:
            return tiles[t, j][q]
        if dx > 0:
            mixed = jnp.where(lane < dx, tiles[t, j + 1][q], tiles[t, j][q])
        else:
            mixed = jnp.where(lane >= LANES + dx, tiles[t, j - 1][q], tiles[t, j][q])
        return pltpu.roll(mixed, (-dx) % LANES, 1)

    no_above, no_below = row_rank == 0, row_rank == row_count - 1
    no_west, no_east = depth_rank == 0, depth_rank == depth_count - 1
    for j in range(spans):
        sums = [[None] * 5 for _ in range(own_tiles)]
        for dx in range(-2, 3):
            shifted = {
                t: [column_shift(t, j, q, dx) for q in range(5)] for t in range(-1, own_tiles + 1)
            }
            for dy in range(-2, 3):
                spatial = -(dx * dx + dy * dy) / (2.0 * SPACE_SCALE * SPACE_SCALE)
                for t in range(own_tiles):
                    if dy == 0:
                        near = shifted[t]
                    elif dy > 0:
                        near = [
                            pltpu.roll(
                                jnp.where(sub < dy, shifted[t + 1][q], shifted[t][q]), SUB - dy, 0
                            )
                            for q in range(5)
                        ]
                    else:
                        near = [
                            pltpu.roll(
                                jnp.where(sub >= SUB + dy, shifted[t - 1][q], shifted[t][q]), -dy, 0
                            )
                            for q in range(5)
                        ]
                    diff = near[4] - tiles[t, j][4]
                    weight = jnp.exp(
                        spatial - diff * diff * (1.0 / (2.0 * RANGE_SCALE * RANGE_SCALE))
                    )
                    blocked = None
                    if t == 0 and dy < 0:
                        blocked = no_above & (sub < -dy)
                    if t == own_tiles - 1 and dy > 0:
                        blocked = no_below & (sub >= SUB - dy)
                    if j == 0 and dx < 0:
                        side = no_west & (lane < -dx)
                        blocked = side if blocked is None else blocked | side
                    if j == spans - 1 and dx > 0:
                        side = no_east & (lane >= LANES - dx)
                        blocked = side if blocked is None else blocked | side
                    if blocked is not None:
                        weight = jnp.where(blocked, 0.0, weight)
                    terms = [weight * near[c] for c in range(4)] + [weight]
                    sums[t] = terms if sums[t][0] is None else [a + b for a, b in zip(sums[t], terms)]
        for t in range(own_tiles):
            inverse = 1.0 / sums[t][4]
            for c in range(4):
                out_ref[c, t * SUB : (t + 1) * SUB, j * LANES : (j + 1) * LANES] = (
                    sums[t][c] * inverse
                )


def body(density, velocity, palette):
    layers, rows, columns = density.shape
    depth_count, row_count = lax.axis_size("depth"), lax.axis_size("row")
    spans, own_tiles = columns // LANES, rows // SUB
    width = columns // depth_count
    line = 4 * width + LANES
    assert spans == SUB and rows % SUB == 0 and width % LANES == 0 and layers % 4 == 0
    vmem = pl.BlockSpec(memory_space=pltpu.VMEM)
    smem = pl.BlockSpec(memory_space=pltpu.SMEM)
    anywhere = pl.BlockSpec(memory_space=pl.ANY)
    f32 = jnp.float32

    def shape(*dims):
        return jax.ShapeDtypeStruct(dims, f32)

    row_shape = (4, layers, 2, spans, LANES)
    depth_shape = (4, 2, rows, columns)
    corner_shape = (4, spans, LANES)
    row0, row1, depth0, depth1, *corners = pl.pallas_call(
        functools.partial(pack_kernel, layers=layers, rows=rows, spans=spans, chunks=4),
        out_shape=(shape(*row_shape),) * 2 + (shape(*depth_shape),) * 2 + (shape(*corner_shape),) * 4,
        in_specs=[anywhere, anywhere],
        out_specs=(anywhere,) * 8,
        scratch_shapes=[
            pltpu.VMEM((4, layers, rows, columns), f32),
            pltpu.VMEM((2,) + row_shape, f32),
            pltpu.SemaphoreType.DMA((4, 2)),
            pltpu.SemaphoreType.DMA((2,)),
            pltpu.SemaphoreType.DMA((2,)),
            pltpu.SemaphoreType.DMA((4,)),
        ],
        name="pack",
        compiler_params=pltpu.CompilerParams(vmem_limit_bytes=24 << 20),
    )(density, velocity)
    row1, row0 = swap_rows(row1, 1), swap_rows(row0, 0)
    depth0, depth1 = swap_depths(depth0, 0), swap_depths(depth1, 1)
    corners = [swap_corners(corner, k // 2, k % 2) for k, corner in enumerate(corners)]

    with jax.named_scope("interior"):
        early, share, edge = pl.pallas_call(
            functools.partial(interior_kernel, layers=layers, rows=rows, columns=columns),
            grid=(layers // 4,),
            out_shape=(
                pltpu.VMEM((layers, 4, spans * rows, LANES), f32),
                pltpu.VMEM((layers, spans * rows, LANES), f32),
                pltpu.VMEM((layers, 2, 4, spans, LANES), f32),
            ),
            in_specs=[
                pl.BlockSpec((4, rows, columns), lambda i: (i, 0, 0)),
                pl.BlockSpec((3, 4, rows, columns), lambda i: (0, i, 0, 0)),
            ],
            out_specs=(vmem,) * 3,
            scratch_shapes=[pltpu.VMEM((4, 4, spans * PITCH, LANES), f32)],
            cost_estimate=pl.CostEstimate(
                flops=80 * layers * rows * columns, bytes_accessed=16 * layers * rows * columns,
                transcendentals=layers * rows * columns,
            ),
            name="interior",
            compiler_params=pltpu.CompilerParams(vmem_limit_bytes=24 << 20),
        )(density, velocity)

    settled, moving, *parts = pl.pallas_call(
        functools.partial(
            settle_kernel, layers=layers, rows=rows, columns=columns,
            depth_count=depth_count, row_count=row_count,
        ),
        grid=(layers // 4,),
        out_shape=(shape(layers, rows, columns), shape(3, layers, rows, columns))
        + (shape(rows, line),) * depth_count,
        in_specs=[smem] + [anywhere] * 2 + [vmem] * 11,
        out_specs=(
            pl.BlockSpec((4, rows, columns), lambda i: (i, 0, 0)),
            pl.BlockSpec((3, 4, rows, columns), lambda i: (0, i, 0, 0)),
        )
        + (vmem,) * depth_count,
        scratch_shapes=[
            pltpu.VMEM((2, 4, rows, columns), f32),
            pltpu.VMEM((2, 4, layers + 2, 2, spans, LANES), f32),
            pltpu.VMEM((3, 4, spans * PITCH, LANES), f32),
            pltpu.VMEM((4, 4, spans * PITCH, LANES), f32),
            pltpu.VMEM((4, spans * rows, LANES), f32),
            pltpu.SemaphoreType.DMA((2, 2)),
        ],
        name="settle",
        compiler_params=pltpu.CompilerParams(vmem_limit_bytes=32 << 20),
    )(
        palette, density, velocity,
        *(in_vmem(x) for x in (row0, row1, depth0, depth1, *corners, early, share, edge)),
    )

    parts = [
        lax.ppermute(part, "depth", [(i, i ^ k) for i in range(depth_count)]) if k else part
        for k, part in enumerate(parts)
    ]
    composed, swap0, swap1 = pl.pallas_call(
        functools.partial(over_kernel, count=depth_count, width=width),
        out_shape=(shape(rows, line), shape(SUB, line), shape(SUB, line)),
        in_specs=[vmem] * depth_count,
        out_specs=(vmem, vmem, vmem),
        name="over",
        compiler_params=pltpu.CompilerParams(vmem_limit_bytes=8 << 20),
    )(parts[0], *(in_vmem(part) for part in parts[1:]))

    swap1, swap0 = swap_rows(swap1, 1), swap_rows(swap0, 0)
    filtered = pl.pallas_call(
        functools.partial(
            filter_kernel, width=width, row_count=row_count, depth_count=depth_count
        ),
        out_shape=shape(4, rows, width),
        in_specs=[vmem] * 3,
        out_specs=vmem,
        name="bilateral",
        compiler_params=pltpu.CompilerParams(vmem_limit_bytes=8 << 20),
    )(composed, in_vmem(swap0), in_vmem(swap1))
    return (filtered, settled, moving)


def solution(mesh):
    in_specs = (P("depth", "row", None), P(None, "depth", "row", None), P())
    out_specs = (P(None, "row", "depth"), P("depth", "row", None), P(None, "depth", "row", None))
    return jax.shard_map(body, mesh=mesh, in_specs=in_specs, out_specs=out_specs, check_vma=False)
```

```python
import functools
import math

import jax
import jax.numpy as jnp
from jax import lax
from jax.experimental import pallas as pl
from jax.experimental.pallas import tpu as pltpu
from jax.sharding import PartitionSpec as P


DIFFUSION = 0.1
ADVECTION = 0.25
VISCOSITY = 0.15
FRICTION = 0.2
OPTICAL = 2.0
RANGE_SCALE = 0.1
SPACE_SCALE = 1.5
SUB = 8
LANES = 128
PITCH = 40
AXES = ("row", "depth")


def row_pairs(kind, count):
    pairs = []
    for low in range(kind, count - 1, 2):
        pairs += [(low, low + 1), (low + 1, low)]
    return pairs


def swap_rows(array, kind):
    return lax.ppermute(array, "row", row_pairs(kind, lax.axis_size("row")))


def swap_depths(array, kind):
    return lax.ppermute(array, "depth", row_pairs(kind, lax.axis_size("depth")))


def swap_corners(array, row_kind, depth_kind):
    depths = lax.axis_size("depth")
    pairs = [
        (a * depths + c, b * depths + d)
        for a, b in row_pairs(row_kind, lax.axis_size("row"))
        for c, d in row_pairs(depth_kind, depths)
    ]
    return lax.ppermute(array, AXES, pairs)


def in_vmem(array):
    return pltpu.with_memory_space_constraint(array, pltpu.VMEM)


def pack_kernel(
    den_ref, vel_ref, block, row0_ref, row1_ref, c10_ref, c11_ref, sides, load_sem,
    *, layers, rows, spans, chunks,
):
    row_odd = lax.rem(lax.axis_index("row"), 2)
    depth_odd = lax.rem(lax.axis_index("depth"), 2)
    size = layers // chunks

    def loads(k):
        z = slice(k * size, (k + 1) * size)
        return (
            pltpu.make_async_copy(den_ref.at[z], block.at[0, z], load_sem.at[k, 0]),
            pltpu.make_async_copy(vel_ref.at[:, z], block.at[1:4, z], load_sem.at[k, 1]),
        )

    for k in range(chunks):
        for copy in loads(k):
            copy.start()
    for k in range(chunks):
        for copy in loads(k):
            copy.wait()
        for c in range(4):
            for z in range(k * size, (k + 1) * size):
                for side in range(2):
                    for n in range(2):
                        row = n + side * (rows - 2)
                        for j in range(spans):
                            sides[side, c, z, n, j : j + 1, :] = block[
                                c, z, row : row + 1, j * LANES : (j + 1) * LANES
                            ]
        for c in range(4):
            for z in range(k * size, (k + 1) * size):
                for n in range(2):
                    row0_ref[c, z, n] = sides[1 - row_odd, c, z, n]
                    row1_ref[c, z, n] = sides[row_odd, c, z, n]
    for target, side in ((c10_ref, 1 - depth_odd), (c11_ref, depth_odd)):
        for c in range(4):
            target[c] = row1_ref[c, side * (layers - 1), row_odd]


def pack_depth_kernel(block, row0_ref, depth0_ref, depth1_ref, *, layers, rows, spans):
    row_odd = lax.rem(lax.axis_index("row"), 2)
    depth_odd = lax.rem(lax.axis_index("depth"), 2)
    for target, side in ((depth0_ref, 1 - depth_odd), (depth1_ref, depth_odd)):
        for c in range(4):
            for n in range(2):
                z = side * (layers - 2) + n
                for j in range(spans):
                    target[c, pl.ds((n * spans + j) * rows, rows), :] = block[
                        c, z, :, j * LANES : (j + 1) * LANES
                    ]
            target[c, pl.ds(2 * spans * rows, spans), :] = row0_ref[
                c, side * (layers - 1), row_odd
            ]


def row_of(j, row):
    return PITCH * j + SUB + row


def advance(here, up, down, left, right, front, back):
    around = [
        ((front[c] + back[c]) + (up[c] + down[c])) + (left[c] + right[c]) for c in range(4)
    ]
    flux = (
        (right[0] * right[1] - left[0] * left[1])
        + (down[0] * down[2] - up[0] * up[2])
        + (back[0] * back[3] - front[0] * front[3])
    )
    squared = here[0] * here[0]
    new = [
        (1.0 - 6.0 * DIFFUSION) * here[0] + (DIFFUSION * around[0] - (0.5 * ADVECTION) * flux)
    ]
    inverse = 1.0 / ((1.0 + squared) * (1.0 + FRICTION * squared))
    own_share = (1.0 + (1.0 - 6.0 * VISCOSITY) * squared) * inverse
    near_share = (VISCOSITY * squared) * inverse
    for c in range(1, 4):
        new.append(here[c] * own_share + around[c] * near_share)
    return new, near_share


def late_share(value, neighbour, near_share, along, sign):
    out = [
        value[0]
        + neighbour[0] * (DIFFUSION + (sign * 0.5 * ADVECTION) * neighbour[along])
    ]
    return out + [value[c] + near_share * neighbour[c] for c in range(1, 4)]


def neighbours(cells, slots, t, j, spans, first, last):
    oldest, middle, newest = slots
    row = t * SUB

    def at(which, r, jj=j):
        return [cells[which, c, pl.ds(row_of(jj, r), SUB), :] for c in range(4)]

    here = at(middle, row)
    zeros = [jnp.zeros((SUB, LANES), jnp.float32)] * 4
    before = at(middle, row, j - 1) if j > 0 else zeros
    after = at(middle, row, j + 1) if j < spans - 1 else zeros
    left = [pltpu.roll(jnp.where(last, b, x), 1, 1) for b, x in zip(before, here)]
    right = [pltpu.roll(jnp.where(first, a, x), LANES - 1, 1) for a, x in zip(after, here)]
    return (
        here, at(middle, row - 1), at(middle, row + 1), left, right,
        at(oldest, row), at(newest, row),
    )


def interior_kernel(
    block, early_ref, share_ref, edge_ref, base, *, layers, rows, columns
):
    step = pl.program_id(0)
    own_tiles, spans = rows // SUB, columns // LANES
    lane = lax.broadcasted_iota(jnp.int32, (SUB, LANES), 1)
    first, last = lane == 0, lane == LANES - 1

    @pl.when(step == 0)
    def _():
        line = jnp.zeros((spans, LANES), jnp.float32)
        for slot in range(4):
            for c in range(4):
                for row in (-1, rows):
                    base[slot, c, pl.ds(row_of(0, row), spans, stride=PITCH), :] = line
        base[3] = jnp.zeros((4, spans * PITCH, LANES), jnp.float32)
        base[2] = jnp.zeros((4, spans * PITCH, LANES), jnp.float32)

    def first_step(z, slots):
        for j in range(spans):
            for t in range(own_tiles):
                new, share = advance(*neighbours(base, slots, t, j, spans, first, last))
                cells = pl.ds(j * rows + t * SUB, SUB)
                share_ref[z, cells, :] = share
                for c in range(4):
                    early_ref[z, c, cells, :] = new[c]

    for q in range(4):
        z = 4 * step + q
        for t in range(own_tiles):
            for j in range(spans):
                there = (slice(t * SUB, (t + 1) * SUB), slice(j * LANES, (j + 1) * LANES))
                for c in range(4):
                    base[q, c, pl.ds(row_of(j, t * SUB), SUB), :] = block[(c, z) + there]
        for side, row in ((0, 0), (1, rows - 1)):
            for c in range(4):
                edge_ref[z, side, c] = base[q, c, pl.ds(row_of(0, row), spans, stride=PITCH), :]
        first_step(jnp.maximum(z - 1, 0), ((q + 2) % 4, (q + 3) % 4, q))

    @pl.when(step == layers // 4 - 1)
    def _():
        base[0] = jnp.zeros((4, spans * PITCH, LANES), jnp.float32)
        first_step(layers - 1, (2, 3, 0))


def settle_kernel(
    palette_ref, block, row0_ref, row1_ref, depth0_ref, depth1_ref, c10_ref, c11_ref,
    early_ref, share_ref, edge_ref, den_out, vel_out, *rest,
    layers, rows, columns, depth_count, row_count,
):
    pieces = rest[:depth_count]
    rowbuf, base, sbase, accum = rest[depth_count:]
    step = pl.program_id(0)
    steps = layers // 4
    own_tiles, spans = rows // SUB, columns // LANES
    row_rank, depth_rank = lax.axis_index("row"), lax.axis_index("depth")
    row_odd, depth_odd = lax.rem(row_rank, 2), lax.rem(depth_rank, 2)
    above, below = 1 - row_odd, row_odd
    sub = lax.broadcasted_iota(jnp.int32, (SUB, LANES), 0)
    lane = lax.broadcasted_iota(jnp.int32, (SUB, LANES), 1)
    first, last = lane == 0, lane == LANES - 1
    from_front = jnp.full((SUB, LANES), depth_odd, jnp.int32) == 1

    tiles = [(t, j) for j in range(spans) for t in range(own_tiles)]

    def tile_of(t, j):
        return slice(t * SUB, (t + 1) * SUB), slice(j * LANES, (j + 1) * LANES)

    def cells_of(t, j):
        return pl.ds(j * rows + t * SUB, SUB)

    def line(row):
        return pl.ds(row_of(0, row), spans, stride=PITCH)

    def outer_step(slot, front):
        kept = (depth_rank > 0) if front else (depth_rank < depth_count - 1)
        keep = jnp.full((SUB, LANES), jnp.where(kept, 1, 0), jnp.int32) == 1
        chosen = from_front if front else jnp.logical_not(from_front)
        far, near = (0, 1) if front else (1, 0)
        for t, j in tiles:
            there = tile_of(t, j)
            for c in range(4):
                for k, n in ((0, far), (1, near)):
                    cells = pl.ds((n * spans + j) * rows + t * SUB, SUB)
                    base[k, c, pl.ds(row_of(j, t * SUB), SUB), :] = jnp.where(
                        chosen, depth0_ref[c, cells, :], depth1_ref[c, cells, :]
                    )
                base[2, c, pl.ds(row_of(j, t * SUB), SUB), :] = block[
                    (c, 0 if front else layers - 1) + there
                ]
        z = 0 if front else layers + 1
        for c in range(4):
            base[1, c, line(-1), :] = rowbuf[above, c, z, 1]
            base[1, c, line(rows), :] = rowbuf[below, c, z, 0]
        slots = (0, 1, 2) if front else (2, 1, 0)
        for t, j in tiles:
            new, _ = advance(*neighbours(base, slots, t, j, spans, first, last))
            for c in range(4):
                sbase[slot, c, pl.ds(row_of(j, t * SUB), SUB), :] = jnp.where(keep, new[c], 0.0)

    def add_layer(z, slot, sign):
        for t, j in tiles:
            cells = pl.ds(row_of(j, t * SUB), SUB)
            new = late_share(
                [sbase[slot, c, cells, :] for c in range(4)],
                [base[1, c, cells, :] for c in range(4)],
                share_ref[z, cells_of(t, j), :], 3, sign,
            )
            for c in range(4):
                sbase[slot, c, cells, :] = new[c]

    def take_layer(z, slot):
        for t, j in tiles:
            for c in range(4):
                sbase[slot, c, pl.ds(row_of(j, t * SUB), SUB), :] = early_ref[z, c, cells_of(t, j), :]
        for side, kind, k, row, exists in (
            (0, above, 1, -1, row_rank > 0), (1, below, 0, rows, row_rank < row_count - 1),
        ):
            own_row = 0 if side == 0 else rows - 1
            own_cells = pl.ds(own_row, spans, stride=rows)

            def halo(layer, n):
                return [rowbuf[kind, c, layer, n] for c in range(4)]

            here, farther = halo(z + 1, k), halo(z + 1, 1 - k)
            own = [edge_ref[z, side, c] for c in range(4)]
            new = late_share(
                [early_ref[z, c, own_cells, :] for c in range(4)], here,
                share_ref[z, own_cells, :], 2, 1.0 if side == 0 else -1.0,
            )
            for c in range(4):
                sbase[slot, c, line(own_row), :] = new[c]
            left, right = [], []
            for value in here:
                before = jnp.where(sub == 0, 0.0, pltpu.roll(value, 1, 0))
                after = jnp.where(sub == SUB - 1, 0.0, pltpu.roll(value, SUB - 1, 0))
                left.append(pltpu.roll(jnp.where(last, before, value), 1, 1))
                right.append(pltpu.roll(jnp.where(first, after, value), LANES - 1, 1))
            up, down = (farther, own) if side == 0 else (own, farther)
            new, _ = advance(here, up, down, left, right, halo(z, k), halo(z + 2, k))
            inside = jnp.full((SUB, LANES), jnp.where(exists, 1, 0), jnp.int32) == 1
            for c in range(4):
                sbase[slot, c, line(row), :] = jnp.where(inside, new[c], 0.0)

    @pl.when(step == 0)
    def _():
        for kind, source in ((0, row0_ref), (1, row1_ref)):
            for c in range(4):
                for z in range(layers):
                    for k in range(2):
                        rowbuf[kind, c, z + 1, k] = source[c, z, k]
        beside = pl.ds(2 * spans * rows, spans)
        corners = (
            (0, 0, lambda c: depth0_ref[c, beside, :]), (0, 1, lambda c: depth1_ref[c, beside, :]),
            (1, 0, lambda c: c10_ref[c]), (1, 1, lambda c: c11_ref[c]),
        )
        for row_kind, depth_kind, source in corners:
            is_above = row_odd if row_kind == 0 else 1 - row_odd
            is_front = depth_odd if depth_kind == 0 else 1 - depth_odd
            for c in range(4):
                rowbuf[row_kind, c, (1 - is_front) * (layers + 1), is_above] = source(c)
        for c in range(3):
            accum[c] = jnp.zeros((spans * rows, LANES), jnp.float32)
        accum[3] = jnp.ones((spans * rows, LANES), jnp.float32)
        outer_step(3, True)
        take_layer(0, 0)
        add_layer(0, 0, 1.0)

    rate = -OPTICAL / (layers * depth_count) / math.log(2.0)
    mix = [[0.5 * palette_ref[c, k] for k in range(4)] for c in range(3)]

    def second_step(q):
        for t, j in tiles:
            slots = ((q + 3) % 4, q, (q + 1) % 4)
            new, _ = advance(*neighbours(sbase, slots, t, j, spans, first, last))
            there = tile_of(t, j)
            den_out[(q,) + there] = new[0]
            for c in range(3):
                vel_out[(c, q) + there] = new[c + 1]
            pixels = cells_of(t, j)
            before = accum[3, pixels, :]
            passed = before * jnp.exp2(rate * (new[0] * new[0]))
            weight = before - passed
            accum[3, pixels, :] = passed
            for c in range(3):
                mixed = (mix[c][0] * new[0] + mix[c][1] * new[1]) + (
                    mix[c][2] * new[2] + mix[c][3] * new[3]
                )
                accum[c, pixels, :] = accum[c, pixels, :] + weight * jnp.tanh(mixed)

    for q in range(3):
        take_layer(4 * step + q + 1, q + 1)
        if q == 2:

            @pl.when(step == steps - 1)
            def _():
                outer_step(0, False)
                add_layer(layers - 1, 3, -1.0)

        second_step(q)

    @pl.when(step < steps - 1)
    def _():
        take_layer(4 * step + 4, 0)

    second_step(3)

    @pl.when(step == steps - 1)
    def _():
        width = columns // depth_count
        per_piece = width // LANES

        def channels(j, t):
            pixels = pl.ds(j * rows + t * SUB, SUB)
            through = accum[3, pixels, :]
            return [0.5 * (accum[c, pixels, :] + (1.0 - through)) for c in range(3)] + [through]

        for k in range(depth_count):
            piece = depth_rank ^ k
            start = piece * per_piece
            for t in range(own_tiles):
                r = slice(t * SUB, (t + 1) * SUB)
                for jj in range(per_piece):
                    values = channels(start + jj, t)
                    for c in range(4):
                        pieces[k][r, c * width + jj * LANES : c * width + (jj + 1) * LANES] = (
                            values[c]
                        )
                before = channels(jnp.maximum(start - 1, 0), t)
                after = channels(jnp.minimum(start + per_piece, spans - 1), t)
                edge = jnp.zeros((SUB, LANES), jnp.float32)
                for c in range(4):
                    for values, low in ((before, 4 * c), (after, 4 * c + 2)):
                        turned = pltpu.roll(values[c], (4 * c + 2) % LANES, 1)
                        edge = jnp.where((lane >= low) & (lane < low + 2), turned, edge)
                pieces[k][r, 4 * width : 4 * width + LANES] = edge


def transfer_order(count):
    return sorted(range(count), key=lambda k: (k != 0, k % 2, k)) if count > 2 else list(range(count))


def over_kernel(*refs, count, width):
    parts = [refs[transfer_order(count).index(k)] for k in range(count)]
    picture_ref, swap0_ref, swap1_ref = refs[count:]
    rows = picture_ref.shape[0]
    depth_rank = lax.axis_index("depth")
    row_odd = lax.rem(lax.axis_index("row"), 2)
    lane = lax.broadcasted_iota(jnp.int32, (rows, LANES), 1)

    def split(ref):
        return [ref[:, c * width : (c + 1) * width] for c in range(4)] + [
            ref[:, 4 * width : 4 * width + LANES]
        ]

    def spread_through(edge):
        out = jnp.ones_like(edge)
        for c in range(3):
            turned = pltpu.roll(edge, LANES - 12 + 4 * c, 1)
            out = jnp.where((lane >= 4 * c) & (lane < 4 * c + 4), turned, out)
        return out

    def over(swapped, a, b):
        near = [jnp.where(swapped, y, x) for x, y in zip(a, b)]
        far = [jnp.where(swapped, x, y) for x, y in zip(a, b)]
        out = [near[c] + near[3] * far[c] for c in range(3)]
        out.append(near[3] * far[3])
        edge = near[4] + spread_through(near[4]) * far[4]
        out.append(jnp.where(lane >= 12, near[4] * far[4], edge))
        return out

    values = [split(ref) for ref in parts]
    bit = 0
    while len(values) > 1:
        swapped = (depth_rank >> bit & 1) == 1
        values = [over(swapped, values[k], values[k + 1]) for k in range(0, len(values), 2)]
        bit += 1
    final = values[0]
    for c in range(4):
        picture_ref[:, c * width : (c + 1) * width] = (1.0 - final[3]) if c == 3 else final[c]
    edge = jnp.where((lane >= 12) & (lane < 16), 1.0 - final[4], final[4])
    picture_ref[:, 4 * width : 4 * width + LANES] = edge
    top, bottom = picture_ref[0:2, :], picture_ref[rows - 2 : rows, :]
    odd = row_odd == 1
    swap0_ref[...] = jnp.where(odd, top, bottom)
    swap1_ref[...] = jnp.where(odd, bottom, top)


def filter_kernel(picture_ref, swap0_ref, swap1_ref, out_ref, *, width, row_count, depth_count):
    row_rank, depth_rank = lax.axis_index("row"), lax.axis_index("depth")
    odd = lax.rem(row_rank, 2) == 1
    rows = picture_ref.shape[0]
    own_tiles = rows // SUB
    spans = width // LANES
    lane = lax.broadcasted_iota(jnp.int32, (SUB, LANES), 1)
    sub = lax.broadcasted_iota(jnp.int32, (SUB, LANES), 0)

    def tile(t, c, j):
        if j == -1 or j == spans:
            cols = slice(4 * width, 4 * width + LANES)
        else:
            cols = slice(c * width + j * LANES, c * width + (j + 1) * LANES)
        if t == -1:
            v = jnp.where(odd, swap0_ref[:, cols], swap1_ref[:, cols])
            v = jnp.concatenate([jnp.zeros((SUB - 2, LANES), jnp.float32), v], 0)
        elif t == own_tiles:
            v = jnp.where(odd, swap1_ref[:, cols], swap0_ref[:, cols])
            v = jnp.concatenate([v, jnp.zeros((SUB - 2, LANES), jnp.float32)], 0)
        else:
            v = picture_ref[t * SUB : (t + 1) * SUB, cols]
        if j == -1:
            v = pltpu.roll(v, LANES - 2 - 4 * c, 1)
        elif j == spans:
            v = pltpu.roll(v, (LANES - 2 - 4 * c) % LANES, 1)
        return v

    tiles = {}
    for t in range(-1, own_tiles + 1):
        for j in range(-1, spans + 1):
            four = [tile(t, c, j) for c in range(4)]
            tiles[t, j] = four + [(four[0] + four[1] + four[2]) / 3.0]

    def column_shift(t, j, q, dx):
        if dx == 0:
            return tiles[t, j][q]
        if dx > 0:
            mixed = jnp.where(lane < dx, tiles[t, j + 1][q], tiles[t, j][q])
        else:
            mixed = jnp.where(lane >= LANES + dx, tiles[t, j - 1][q], tiles[t, j][q])
        return pltpu.roll(mixed, (-dx) % LANES, 1)

    no_above, no_below = row_rank == 0, row_rank == row_count - 1
    no_west, no_east = depth_rank == 0, depth_rank == depth_count - 1
    for j in range(spans):
        sums = [[None] * 5 for _ in range(own_tiles)]
        for dx in range(-2, 3):
            shifted = {
                t: [column_shift(t, j, q, dx) for q in range(5)] for t in range(-1, own_tiles + 1)
            }
            for dy in range(-2, 3):
                spatial = -(dx * dx + dy * dy) / (2.0 * SPACE_SCALE * SPACE_SCALE)
                for t in range(own_tiles):
                    if dy == 0:
                        near = shifted[t]
                    elif dy > 0:
                        near = [
                            pltpu.roll(
                                jnp.where(sub < dy, shifted[t + 1][q], shifted[t][q]), SUB - dy, 0
                            )
                            for q in range(5)
                        ]
                    else:
                        near = [
                            pltpu.roll(
                                jnp.where(sub >= SUB + dy, shifted[t - 1][q], shifted[t][q]), -dy, 0
                            )
                            for q in range(5)
                        ]
                    diff = near[4] - tiles[t, j][4]
                    weight = jnp.exp(
                        spatial - diff * diff * (1.0 / (2.0 * RANGE_SCALE * RANGE_SCALE))
                    )
                    blocked = None
                    if t == 0 and dy < 0:
                        blocked = no_above & (sub < -dy)
                    if t == own_tiles - 1 and dy > 0:
                        blocked = no_below & (sub >= SUB - dy)
                    if j == 0 and dx < 0:
                        side = no_west & (lane < -dx)
                        blocked = side if blocked is None else blocked | side
                    if j == spans - 1 and dx > 0:
                        side = no_east & (lane >= LANES - dx)
                        blocked = side if blocked is None else blocked | side
                    if blocked is not None:
                        weight = jnp.where(blocked, 0.0, weight)
                    terms = [weight * near[c] for c in range(4)] + [weight]
                    sums[t] = terms if sums[t][0] is None else [a + b for a, b in zip(sums[t], terms)]
        for t in range(own_tiles):
            inverse = 1.0 / sums[t][4]
            for c in range(4):
                out_ref[c, t * SUB : (t + 1) * SUB, j * LANES : (j + 1) * LANES] = (
                    sums[t][c] * inverse
                )


def compute(density, velocity, palette):
    layers, rows, columns = density.shape
    depth_count, row_count = lax.axis_size("depth"), lax.axis_size("row")
    spans = columns // LANES
    width = columns // depth_count
    line = 4 * width + LANES
    assert spans == SUB and rows % SUB == 0 and width % LANES == 0 and layers % 4 == 0
    vmem = pl.BlockSpec(memory_space=pltpu.VMEM)
    smem = pl.BlockSpec(memory_space=pltpu.SMEM)
    f32 = jnp.float32

    def shape(*dims):
        return jax.ShapeDtypeStruct(dims, f32)

    def local(*dims):
        return pltpu.VMEM(dims, f32)

    def params(mebibytes):
        return pltpu.CompilerParams(vmem_limit_bytes=mebibytes << 20)

    row_shape = (4, layers, 2, spans, LANES)
    depth_shape = (4, (2 * rows + 1) * spans, LANES)
    corner_shape = (4, spans, LANES)
    block, row0, row1, corner0, corner1 = pl.pallas_call(
        functools.partial(pack_kernel, layers=layers, rows=rows, spans=spans, chunks=4),
        out_shape=(
            local(4, layers, rows, columns), local(*row_shape), local(*row_shape),
            local(*corner_shape), local(*corner_shape),
        ),
        in_specs=[pl.BlockSpec(memory_space=pltpu.HBM)] * 2,
        out_specs=(vmem,) * 5,
        scratch_shapes=[pltpu.VMEM((2,) + row_shape, f32), pltpu.SemaphoreType.DMA((4, 2))],
        name="pack",
        compiler_params=params(8),
    )(
        pltpu.with_memory_space_constraint(density, pltpu.HBM),
        pltpu.with_memory_space_constraint(velocity, pltpu.HBM),
    )
    row1 = swap_rows(row1, 1)
    row0 = swap_rows(row0, 0)
    depth0, depth1 = pl.pallas_call(
        functools.partial(pack_depth_kernel, layers=layers, rows=rows, spans=spans),
        out_shape=(local(*depth_shape), local(*depth_shape)),
        in_specs=[vmem] * 2,
        out_specs=(vmem,) * 2,
        name="pack_depth",
        compiler_params=params(8),
    )(in_vmem(block), in_vmem(row0))
    depth0, depth1 = swap_depths(depth0, 0), swap_depths(depth1, 1)
    corner0, corner1 = swap_corners(corner0, 1, 0), swap_corners(corner1, 1, 1)

    early, share, edge = pl.pallas_call(
        functools.partial(interior_kernel, layers=layers, rows=rows, columns=columns),
        grid=(layers // 4,),
        out_shape=(
            pltpu.VMEM((layers, 4, spans * rows, LANES), f32),
            pltpu.VMEM((layers, spans * rows, LANES), f32),
            pltpu.VMEM((layers, 2, 4, spans, LANES), f32),
        ),
        in_specs=[vmem],
        out_specs=(vmem,) * 3,
        scratch_shapes=[pltpu.VMEM((4, 4, spans * PITCH, LANES), f32)],
        cost_estimate=pl.CostEstimate(
            flops=80 * layers * rows * columns, bytes_accessed=16 * layers * rows * columns,
            transcendentals=layers * rows * columns,
        ),
        name="interior",
        compiler_params=pltpu.CompilerParams(vmem_limit_bytes=24 << 20),
    )(in_vmem(block))

    settled, moving, *parts = pl.pallas_call(
        functools.partial(
            settle_kernel, layers=layers, rows=rows, columns=columns,
            depth_count=depth_count, row_count=row_count,
        ),
        grid=(layers // 4,),
        out_shape=(shape(layers, rows, columns), shape(3, layers, rows, columns))
        + (shape(rows, line),) * depth_count,
        in_specs=[smem] + [vmem] * 10,
        out_specs=(
            pl.BlockSpec((4, rows, columns), lambda i: (i, 0, 0)),
            pl.BlockSpec((3, 4, rows, columns), lambda i: (0, i, 0, 0)),
        )
        + (vmem,) * depth_count,
        scratch_shapes=[
            pltpu.VMEM((2, 4, layers + 2, 2, spans, LANES), f32),
            pltpu.VMEM((3, 4, spans * PITCH, LANES), f32),
            pltpu.VMEM((4, 4, spans * PITCH, LANES), f32),
            pltpu.VMEM((4, spans * rows, LANES), f32),
        ],
        name="settle",
        compiler_params=pltpu.CompilerParams(vmem_limit_bytes=32 << 20),
    )(
        palette,
        *(
            in_vmem(x)
            for x in (block, row0, row1, depth0, depth1, corner0, corner1, early, share, edge)
        ),
    )

    parts = [
        lax.ppermute(part, "depth", [(i, i ^ k) for i in range(depth_count)]) if k else part
        for k, part in enumerate(parts)
    ]
    composed, swap0, swap1 = pl.pallas_call(
        functools.partial(over_kernel, count=depth_count, width=width),
        out_shape=(shape(rows, line), shape(2, line), shape(2, line)),
        in_specs=[vmem] * depth_count,
        out_specs=(vmem, vmem, vmem),
        name="over",
        compiler_params=pltpu.CompilerParams(vmem_limit_bytes=8 << 20),
    )(parts[0], *(in_vmem(parts[k]) for k in transfer_order(depth_count)[1:]))

    swap1, swap0 = swap_rows(swap1, 1), swap_rows(swap0, 0)
    filtered = pl.pallas_call(
        functools.partial(
            filter_kernel, width=width, row_count=row_count, depth_count=depth_count
        ),
        out_shape=shape(4, rows, width),
        in_specs=[vmem] * 3,
        out_specs=vmem,
        name="bilateral",
        compiler_params=pltpu.CompilerParams(vmem_limit_bytes=8 << 20),
    )(composed, in_vmem(swap0), in_vmem(swap1))
    return (filtered, settled, moving)


def solution(mesh):
    in_specs = (P("depth", "row", None), P(None, "depth", "row", None), P())
    out_specs = (P(None, "row", "depth"), P("depth", "row", None), P(None, "depth", "row", None))
    return jax.shard_map(
        compute, mesh=mesh, in_specs=in_specs, out_specs=out_specs, check_vma=False
    )
```

```python
import functools
import math

import jax
import jax.numpy as jnp
from jax import lax
from jax.experimental import pallas as pl
from jax.experimental.pallas import tpu as pltpu
from jax.sharding import PartitionSpec as P


DIFFUSION = 0.1
ADVECTION = 0.25
VISCOSITY = 0.15
FRICTION = 0.2
OPTICAL = 2.0
RANGE_SCALE = 0.1
SPACE_SCALE = 1.5
SUB = 8
LANES = 128
PITCH = 40
AXES = ("row", "depth")


def row_pairs(kind, count):
    pairs = []
    for low in range(kind, count - 1, 2):
        pairs += [(low, low + 1), (low + 1, low)]
    return pairs


def swap_rows(array, kind):
    return lax.ppermute(array, "row", row_pairs(kind, lax.axis_size("row")))


def swap_depths(array, kind):
    return lax.ppermute(array, "depth", row_pairs(kind, lax.axis_size("depth")))


def swap_corners(array, row_kind, depth_kind):
    depths = lax.axis_size("depth")
    pairs = [
        (a * depths + c, b * depths + d)
        for a, b in row_pairs(row_kind, lax.axis_size("row"))
        for c, d in row_pairs(depth_kind, depths)
    ]
    return lax.ppermute(array, AXES, pairs)


def in_vmem(array):
    return pltpu.with_memory_space_constraint(array, pltpu.VMEM)


def pack_kernel(
    den_ref, vel_ref, block, row0_ref, row1_ref, c10_ref, c11_ref, sides, load_sem,
    *, layers, rows, spans, chunks,
):
    row_odd = lax.rem(lax.axis_index("row"), 2)
    depth_odd = lax.rem(lax.axis_index("depth"), 2)
    size = layers // chunks

    def loads(k):
        z = slice(k * size, (k + 1) * size)
        return (
            pltpu.make_async_copy(den_ref.at[z], block.at[0, z], load_sem.at[k, 0]),
            pltpu.make_async_copy(vel_ref.at[:, z], block.at[1:4, z], load_sem.at[k, 1]),
        )

    for k in range(chunks):
        for copy in loads(k):
            copy.start()
    for k in range(chunks):
        for copy in loads(k):
            copy.wait()
        for c in range(4):
            for z in range(k * size, (k + 1) * size):
                for side in range(2):
                    for n in range(2):
                        row = n + side * (rows - 2)
                        for j in range(spans):
                            sides[side, c, z, n, j : j + 1, :] = block[
                                c, z, row : row + 1, j * LANES : (j + 1) * LANES
                            ]
        for c in range(4):
            for z in range(k * size, (k + 1) * size):
                for n in range(2):
                    row0_ref[c, z, n] = sides[1 - row_odd, c, z, n]
                    row1_ref[c, z, n] = sides[row_odd, c, z, n]
    for target, side in ((c10_ref, 1 - depth_odd), (c11_ref, depth_odd)):
        for c in range(4):
            target[c] = row1_ref[c, side * (layers - 1), row_odd]


def pack_depth_kernel(block, row0_ref, depth0_ref, depth1_ref, *, layers, rows, spans):
    row_odd = lax.rem(lax.axis_index("row"), 2)
    depth_odd = lax.rem(lax.axis_index("depth"), 2)
    for target, side in ((depth0_ref, 1 - depth_odd), (depth1_ref, depth_odd)):
        for c in range(4):
            for n in range(2):
                z = side * (layers - 2) + n
                for j in range(spans):
                    target[c, pl.ds((n * spans + j) * rows, rows), :] = block[
                        c, z, :, j * LANES : (j + 1) * LANES
                    ]
            target[c, pl.ds(2 * spans * rows, spans), :] = row0_ref[
                c, side * (layers - 1), row_odd
            ]


def row_of(j, row):
    return PITCH * j + SUB + row


def advance(here, up, down, left, right, front, back):
    around = [
        ((front[c] + back[c]) + (up[c] + down[c])) + (left[c] + right[c]) for c in range(4)
    ]
    flux = (
        (right[0] * right[1] - left[0] * left[1])
        + (down[0] * down[2] - up[0] * up[2])
        + (back[0] * back[3] - front[0] * front[3])
    )
    squared = here[0] * here[0]
    new = [
        (1.0 - 6.0 * DIFFUSION) * here[0] + (DIFFUSION * around[0] - (0.5 * ADVECTION) * flux)
    ]
    inverse = 1.0 / ((1.0 + squared) * (1.0 + FRICTION * squared))
    own_share = (1.0 + (1.0 - 6.0 * VISCOSITY) * squared) * inverse
    near_share = (VISCOSITY * squared) * inverse
    for c in range(1, 4):
        new.append(here[c] * own_share + around[c] * near_share)
    return new, near_share


def late_share(value, neighbour, near_share, along, sign):
    out = [
        value[0]
        + neighbour[0] * (DIFFUSION + (sign * 0.5 * ADVECTION) * neighbour[along])
    ]
    return out + [value[c] + near_share * neighbour[c] for c in range(1, 4)]


def neighbours(cells, slots, t, j, spans, first, last):
    oldest, middle, newest = slots
    row = t * SUB

    def at(which, r, jj=j):
        return [cells[which, c, pl.ds(row_of(jj, r), SUB), :] for c in range(4)]

    here = at(middle, row)
    zeros = [jnp.zeros((SUB, LANES), jnp.float32)] * 4
    before = at(middle, row, j - 1) if j > 0 else zeros
    after = at(middle, row, j + 1) if j < spans - 1 else zeros
    left = [pltpu.roll(jnp.where(last, b, x), 1, 1) for b, x in zip(before, here)]
    right = [pltpu.roll(jnp.where(first, a, x), LANES - 1, 1) for a, x in zip(after, here)]
    return (
        here, at(middle, row - 1), at(middle, row + 1), left, right,
        at(oldest, row), at(newest, row),
    )


def render(accum, pixels, cells, rate, mix):
    before = accum[3, pixels, :]
    passed = before * jnp.exp2(rate * (cells[0] * cells[0]))
    weight = before - passed
    accum[3, pixels, :] = passed
    for c in range(3):
        mixed = (mix[c][0] * cells[0] + mix[c][1] * cells[1]) + (
            mix[c][2] * cells[2] + mix[c][3] * cells[3]
        )
        accum[c, pixels, :] = accum[c, pixels, :] + weight * jnp.tanh(mixed)


def beside_in_lines(lines, sub, first, last):
    left, right = [], []
    for value in lines:
        before = jnp.where(sub == 0, 0.0, pltpu.roll(value, 1, 0))
        after = jnp.where(sub == SUB - 1, 0.0, pltpu.roll(value, SUB - 1, 0))
        left.append(pltpu.roll(jnp.where(last, before, value), 1, 1))
        right.append(pltpu.roll(jnp.where(first, after, value), LANES - 1, 1))
    return left, right


def constants(palette_ref, depth_total):
    rate = -OPTICAL / depth_total / math.log(2.0)
    return rate, [[0.5 * palette_ref[c, k] for k in range(4)] for c in range(3)]


def interior_kernel(
    palette_ref, block, early_ref, share_ref, edge_ref, late_ref, part_ref, base,
    *, layers, rows, columns, depth_count,
):
    step = pl.program_id(0)
    own_tiles, spans = rows // SUB, columns // LANES
    lane = lax.broadcasted_iota(jnp.int32, (SUB, LANES), 1)
    first, last = lane == 0, lane == LANES - 1

    @pl.when(step == 0)
    def _():
        line = jnp.zeros((spans, LANES), jnp.float32)
        for slot in range(4):
            for c in range(4):
                for row in (-1, rows):
                    base[slot, c, pl.ds(row_of(0, row), spans, stride=PITCH), :] = line
        base[3] = jnp.zeros((4, spans * PITCH, LANES), jnp.float32)
        base[2] = jnp.zeros((4, spans * PITCH, LANES), jnp.float32)
        for c in range(3):
            part_ref[c] = jnp.zeros((spans * rows, LANES), jnp.float32)
        part_ref[3] = jnp.ones((spans * rows, LANES), jnp.float32)

    def first_step(z, slots):
        for j in range(spans):
            for t in range(own_tiles):
                new, share = advance(*neighbours(base, slots, t, j, spans, first, last))
                cells = pl.ds(j * rows + t * SUB, SUB)
                share_ref[z, cells, :] = share
                for c in range(4):
                    early_ref[z, c, cells, :] = new[c]

    for q in range(4):
        z = 4 * step + q
        for t in range(own_tiles):
            for j in range(spans):
                there = (slice(t * SUB, (t + 1) * SUB), slice(j * LANES, (j + 1) * LANES))
                for c in range(4):
                    base[q, c, pl.ds(row_of(j, t * SUB), SUB), :] = block[(c, z) + there]
        for side, row in ((0, 0), (1, rows - 1)):
            for c in range(4):
                edge_ref[z, side, c] = base[q, c, pl.ds(row_of(0, row), spans, stride=PITCH), :]
        first_step(jnp.maximum(z - 1, 0), ((q + 2) % 4, (q + 3) % 4, q))

    rate, mix = constants(palette_ref, layers * depth_count)

    def inner_neighbours(z, t, j):
        row = j * rows + t * SUB

        def at(layer, start):
            return [early_ref[layer, c, pl.ds(start, SUB), :] for c in range(4)]

        here = at(z, row)
        zeros = [jnp.zeros((SUB, LANES), jnp.float32)] * 4
        before = at(z, row - rows) if j > 0 else zeros
        after = at(z, row + rows) if j < spans - 1 else zeros
        if row > 0:
            up = at(z, row - 1)
        else:
            up = [pltpu.roll(x, 1, 0) for x in here]
        if row + SUB < spans * rows:
            down = at(z, row + 1)
        else:
            down = [pltpu.roll(x, SUB - 1, 0) for x in here]
        left = [pltpu.roll(jnp.where(last, b, x), 1, 1) for b, x in zip(before, here)]
        right = [pltpu.roll(jnp.where(first, a, x), LANES - 1, 1) for a, x in zip(after, here)]
        return here, up, down, left, right, at(z - 1, row), at(z + 1, row)

    @pl.when(step > 0)
    def _():
        for q in range(4):
            z = 4 * step + q - 2
            for j in range(spans):
                for t in range(own_tiles):
                    new, _ = advance(*inner_neighbours(z, t, j))
                    cells = pl.ds(j * rows + t * SUB, SUB)
                    for c in range(4):
                        late_ref[z, c, cells, :] = new[c]
                    render(part_ref, cells, new, rate, mix)

    @pl.when(step == layers // 4 - 1)
    def _():
        base[0] = jnp.zeros((4, spans * PITCH, LANES), jnp.float32)
        first_step(layers - 1, (2, 3, 0))


def settle_kernel(
    palette_ref, block, row0_ref, row1_ref, depth0_ref, depth1_ref, c10_ref, c11_ref,
    early_ref, share_ref, edge_ref, late_ref, part_ref, den_out, vel_out, *rest,
    layers, rows, columns, depth_count, row_count,
):
    pieces = rest[:depth_count]
    rowbuf, srow, line_buffer, base, sbase, accum = rest[depth_count:]
    step = pl.program_id(0)
    steps = layers // 4
    own_tiles, spans = rows // SUB, columns // LANES
    row_rank, depth_rank = lax.axis_index("row"), lax.axis_index("depth")
    row_odd, depth_odd = lax.rem(row_rank, 2), lax.rem(depth_rank, 2)
    above, below = 1 - row_odd, row_odd
    sub = lax.broadcasted_iota(jnp.int32, (SUB, LANES), 0)
    lane = lax.broadcasted_iota(jnp.int32, (SUB, LANES), 1)
    first, last = lane == 0, lane == LANES - 1
    from_front = jnp.full((SUB, LANES), depth_odd, jnp.int32) == 1
    tiles = [(t, j) for j in range(spans) for t in range(own_tiles)]
    rate, mix = constants(palette_ref, layers * depth_count)

    def tile_of(t, j):
        return slice(t * SUB, (t + 1) * SUB), slice(j * LANES, (j + 1) * LANES)

    def cells_of(t, j):
        return pl.ds(j * rows + t * SUB, SUB)

    def line(row):
        return pl.ds(row_of(0, row), spans, stride=PITCH)

    def outer_step(slot, front):
        kept = (depth_rank > 0) if front else (depth_rank < depth_count - 1)
        keep = jnp.full((SUB, LANES), jnp.where(kept, 1, 0), jnp.int32) == 1
        chosen = from_front if front else jnp.logical_not(from_front)
        far, near = (0, 1) if front else (1, 0)
        for t, j in tiles:
            there = tile_of(t, j)
            for c in range(4):
                for k, n in ((0, far), (1, near)):
                    cells = pl.ds((n * spans + j) * rows + t * SUB, SUB)
                    base[k, c, pl.ds(row_of(j, t * SUB), SUB), :] = jnp.where(
                        chosen, depth0_ref[c, cells, :], depth1_ref[c, cells, :]
                    )
                base[2, c, pl.ds(row_of(j, t * SUB), SUB), :] = block[
                    (c, 0 if front else layers - 1) + there
                ]
        z = 0 if front else layers + 1
        for c in range(4):
            base[1, c, line(-1), :] = rowbuf[above, c, z, 1]
            base[1, c, line(rows), :] = rowbuf[below, c, z, 0]
        slots = (0, 1, 2) if front else (2, 1, 0)
        for t, j in tiles:
            new, _ = advance(*neighbours(base, slots, t, j, spans, first, last))
            for c in range(4):
                sbase[slot, c, pl.ds(row_of(j, t * SUB), SUB), :] = jnp.where(keep, new[c], 0.0)

    def add_layer(z, slot, sign):
        for t, j in tiles:
            cells = pl.ds(row_of(j, t * SUB), SUB)
            new = late_share(
                [sbase[slot, c, cells, :] for c in range(4)],
                [base[1, c, cells, :] for c in range(4)],
                share_ref[z, cells_of(t, j), :], 3, sign,
            )
            for c in range(4):
                sbase[slot, c, cells, :] = new[c]

    def edge_rows(z):
        for side, kind, k, exists in (
            (0, above, 1, row_rank > 0), (1, below, 0, row_rank < row_count - 1),
        ):
            own_cells = pl.ds(0 if side == 0 else rows - 1, spans, stride=rows)

            def halo(layer, n):
                return [rowbuf[kind, c, layer, n] for c in range(4)]

            here, farther = halo(z + 1, k), halo(z + 1, 1 - k)
            own = [edge_ref[z, side, c] for c in range(4)]
            new = late_share(
                [early_ref[z, c, own_cells, :] for c in range(4)], here,
                share_ref[z, own_cells, :], 2, 1.0 if side == 0 else -1.0,
            )
            for c in range(4):
                srow[z, 1 + side, c] = new[c]
            left, right = beside_in_lines(here, sub, first, last)
            up, down = (farther, own) if side == 0 else (own, farther)
            new, _ = advance(here, up, down, left, right, halo(z, k), halo(z + 2, k))
            inside = jnp.full((SUB, LANES), jnp.where(exists, 1, 0), jnp.int32) == 1
            for c in range(4):
                srow[z, 3 * side, c] = jnp.where(inside, new[c], 0.0)

    def take_layer(z, slot):
        for t, j in tiles:
            for c in range(4):
                sbase[slot, c, pl.ds(row_of(j, t * SUB), SUB), :] = early_ref[z, c, cells_of(t, j), :]
        for n, row in enumerate((-1, 0, rows - 1, rows)):
            for c in range(4):
                sbase[slot, c, line(row), :] = srow[z, n, c]

    def whole_layer(q, slots):
        for t, j in tiles:
            new, _ = advance(*neighbours(sbase, slots, t, j, spans, first, last))
            there = tile_of(t, j)
            den_out[(q,) + there] = new[0]
            for c in range(3):
                vel_out[(c, q) + there] = new[c + 1]
            render(accum, cells_of(t, j), new, rate, mix)

    def outer_rows(z, q):
        def values(layer, row):
            n = {-1: 0, 0: 1, rows - 1: 2, rows: 3}.get(row)
            if n is not None:
                return [srow[layer, n, c] for c in range(4)]
            return [early_ref[layer, c, pl.ds(row, spans, stride=rows), :] for c in range(4)]

        for t, j in tiles:
            there = tile_of(t, j)
            den_out[(q,) + there] = late_ref[z, 0, cells_of(t, j), :]
            for c in range(3):
                vel_out[(c, q) + there] = late_ref[z, c + 1, cells_of(t, j), :]
        for n, row in enumerate((0, 1, rows - 2, rows - 1)):
            here = values(z, row)
            left, right = beside_in_lines(here, sub, first, last)
            new, _ = advance(
                here, values(z, row - 1), values(z, row + 1), left, right,
                values(z - 1, row), values(z + 1, row),
            )
            render(accum, pl.ds(row, spans, stride=rows), new, rate, mix)
            for c in range(4):
                line_buffer[q, n, c] = new[c]
            for j in range(spans):
                there = (slice(row, row + 1), slice(j * LANES, (j + 1) * LANES))
                den_out[(q,) + there] = line_buffer[q, n, 0, j : j + 1, :]
                for c in range(3):
                    vel_out[(c, q) + there] = line_buffer[q, n, c + 1, j : j + 1, :]

    @pl.when(step == 0)
    def _():
        for kind, source in ((0, row0_ref), (1, row1_ref)):
            for c in range(4):
                for z in range(layers):
                    for k in range(2):
                        rowbuf[kind, c, z + 1, k] = source[c, z, k]
        beside = pl.ds(2 * spans * rows, spans)
        corners = (
            (0, 0, lambda c: depth0_ref[c, beside, :]), (0, 1, lambda c: depth1_ref[c, beside, :]),
            (1, 0, lambda c: c10_ref[c]), (1, 1, lambda c: c11_ref[c]),
        )
        for row_kind, depth_kind, source in corners:
            is_above = row_odd if row_kind == 0 else 1 - row_odd
            is_front = depth_odd if depth_kind == 0 else 1 - depth_odd
            for c in range(4):
                rowbuf[row_kind, c, (1 - is_front) * (layers + 1), is_above] = source(c)
        for c in range(3):
            accum[c] = jnp.zeros((spans * rows, LANES), jnp.float32)
        accum[3] = jnp.ones((spans * rows, LANES), jnp.float32)

        @pl.loop(0, layers // 2)
        def _(pair):
            edge_rows(2 * pair)
            edge_rows(2 * pair + 1)

        outer_step(3, True)
        take_layer(0, 0)
        add_layer(0, 0, 1.0)
        take_layer(1, 1)
        take_layer(2, 2)
        whole_layer(0, (3, 0, 1))
        whole_layer(1, (0, 1, 2))
        for t, j in tiles:
            pixels = cells_of(t, j)
            through = accum[3, pixels, :]
            inner = jnp.full((SUB, LANES), True)
            if t == 0:
                inner = sub >= 2
            if t == own_tiles - 1:
                inner = (sub < SUB - 2) if t > 0 else inner & (sub < SUB - 2)
            for c in range(3):
                value = accum[c, pixels, :]
                accum[c, pixels, :] = jnp.where(
                    inner, value + through * part_ref[c, pixels, :], value
                )
            accum[3, pixels, :] = jnp.where(inner, through * part_ref[3, pixels, :], through)
        outer_rows(2, 2)
        outer_rows(3, 3)

    @pl.when((step > 0) & (step < steps - 1))
    def _():
        for q in range(4):
            outer_rows(4 * step + q, q)

    @pl.when(step == steps - 1)
    def _():
        outer_rows(layers - 4, 0)
        outer_rows(layers - 3, 1)
        take_layer(layers - 3, 0)
        take_layer(layers - 2, 1)
        take_layer(layers - 1, 2)
        outer_step(3, False)
        add_layer(layers - 1, 2, -1.0)
        whole_layer(2, (0, 1, 2))
        whole_layer(3, (1, 2, 3))
        width = columns // depth_count
        per_piece = width // LANES

        def channels(j, t):
            pixels = pl.ds(j * rows + t * SUB, SUB)
            through = accum[3, pixels, :]
            return [0.5 * (accum[c, pixels, :] + (1.0 - through)) for c in range(3)] + [through]

        for k in range(depth_count):
            piece = depth_rank ^ k
            start = piece * per_piece
            for t in range(own_tiles):
                r = slice(t * SUB, (t + 1) * SUB)
                for jj in range(per_piece):
                    values = channels(start + jj, t)
                    for c in range(4):
                        pieces[k][r, c * width + jj * LANES : c * width + (jj + 1) * LANES] = (
                            values[c]
                        )
                before = channels(jnp.maximum(start - 1, 0), t)
                after = channels(jnp.minimum(start + per_piece, spans - 1), t)
                edge = jnp.zeros((SUB, LANES), jnp.float32)
                for c in range(4):
                    for values, low in ((before, 4 * c), (after, 4 * c + 2)):
                        turned = pltpu.roll(values[c], (4 * c + 2) % LANES, 1)
                        edge = jnp.where((lane >= low) & (lane < low + 2), turned, edge)
                pieces[k][r, 4 * width : 4 * width + LANES] = edge


def transfer_order(count):
    return sorted(range(count), key=lambda k: (k != 0, k % 2, k)) if count > 2 else list(range(count))


def over_kernel(*refs, count, width):
    parts = [refs[transfer_order(count).index(k)] for k in range(count)]
    picture_ref, swap0_ref, swap1_ref = refs[count:]
    rows = picture_ref.shape[0]
    depth_rank = lax.axis_index("depth")
    row_odd = lax.rem(lax.axis_index("row"), 2)
    lane = lax.broadcasted_iota(jnp.int32, (rows, LANES), 1)

    def split(ref):
        return [ref[:, c * width : (c + 1) * width] for c in range(4)] + [
            ref[:, 4 * width : 4 * width + LANES]
        ]

    def spread_through(edge):
        out = jnp.ones_like(edge)
        for c in range(3):
            turned = pltpu.roll(edge, LANES - 12 + 4 * c, 1)
            out = jnp.where((lane >= 4 * c) & (lane < 4 * c + 4), turned, out)
        return out

    def over(swapped, a, b):
        near = [jnp.where(swapped, y, x) for x, y in zip(a, b)]
        far = [jnp.where(swapped, x, y) for x, y in zip(a, b)]
        out = [near[c] + near[3] * far[c] for c in range(3)]
        out.append(near[3] * far[3])
        edge = near[4] + spread_through(near[4]) * far[4]
        out.append(jnp.where(lane >= 12, near[4] * far[4], edge))
        return out

    values = [split(ref) for ref in parts]
    bit = 0
    while len(values) > 1:
        swapped = (depth_rank >> bit & 1) == 1
        values = [over(swapped, values[k], values[k + 1]) for k in range(0, len(values), 2)]
        bit += 1
    final = values[0]
    for c in range(4):
        picture_ref[:, c * width : (c + 1) * width] = (1.0 - final[3]) if c == 3 else final[c]
    edge = jnp.where((lane >= 12) & (lane < 16), 1.0 - final[4], final[4])
    picture_ref[:, 4 * width : 4 * width + LANES] = edge
    top, bottom = picture_ref[0:2, :], picture_ref[rows - 2 : rows, :]
    odd = row_odd == 1
    swap0_ref[...] = jnp.where(odd, top, bottom)
    swap1_ref[...] = jnp.where(odd, bottom, top)


def filter_kernel(picture_ref, swap0_ref, swap1_ref, out_ref, *, width, row_count, depth_count):
    row_rank, depth_rank = lax.axis_index("row"), lax.axis_index("depth")
    odd = lax.rem(row_rank, 2) == 1
    rows = picture_ref.shape[0]
    own_tiles = rows // SUB
    spans = width // LANES
    lane = lax.broadcasted_iota(jnp.int32, (SUB, LANES), 1)
    sub = lax.broadcasted_iota(jnp.int32, (SUB, LANES), 0)

    def tile(t, c, j):
        if j == -1 or j == spans:
            cols = slice(4 * width, 4 * width + LANES)
        else:
            cols = slice(c * width + j * LANES, c * width + (j + 1) * LANES)
        if t == -1:
            v = jnp.where(odd, swap0_ref[:, cols], swap1_ref[:, cols])
            v = jnp.concatenate([jnp.zeros((SUB - 2, LANES), jnp.float32), v], 0)
        elif t == own_tiles:
            v = jnp.where(odd, swap1_ref[:, cols], swap0_ref[:, cols])
            v = jnp.concatenate([v, jnp.zeros((SUB - 2, LANES), jnp.float32)], 0)
        else:
            v = picture_ref[t * SUB : (t + 1) * SUB, cols]
        if j == -1:
            v = pltpu.roll(v, LANES - 2 - 4 * c, 1)
        elif j == spans:
            v = pltpu.roll(v, (LANES - 2 - 4 * c) % LANES, 1)
        return v

    tiles = {}
    for t in range(-1, own_tiles + 1):
        for j in range(-1, spans + 1):
            four = [tile(t, c, j) for c in range(4)]
            tiles[t, j] = four + [(four[0] + four[1] + four[2]) / 3.0]

    def column_shift(t, j, q, dx):
        if dx == 0:
            return tiles[t, j][q]
        if dx > 0:
            mixed = jnp.where(lane < dx, tiles[t, j + 1][q], tiles[t, j][q])
        else:
            mixed = jnp.where(lane >= LANES + dx, tiles[t, j - 1][q], tiles[t, j][q])
        return pltpu.roll(mixed, (-dx) % LANES, 1)

    no_above, no_below = row_rank == 0, row_rank == row_count - 1
    no_west, no_east = depth_rank == 0, depth_rank == depth_count - 1
    for j in range(spans):
        sums = [[None] * 5 for _ in range(own_tiles)]
        for dx in range(-2, 3):
            shifted = {
                t: [column_shift(t, j, q, dx) for q in range(5)] for t in range(-1, own_tiles + 1)
            }
            for dy in range(-2, 3):
                spatial = -(dx * dx + dy * dy) / (2.0 * SPACE_SCALE * SPACE_SCALE)
                for t in range(own_tiles):
                    if dy == 0:
                        near = shifted[t]
                    elif dy > 0:
                        near = [
                            pltpu.roll(
                                jnp.where(sub < dy, shifted[t + 1][q], shifted[t][q]), SUB - dy, 0
                            )
                            for q in range(5)
                        ]
                    else:
                        near = [
                            pltpu.roll(
                                jnp.where(sub >= SUB + dy, shifted[t - 1][q], shifted[t][q]), -dy, 0
                            )
                            for q in range(5)
                        ]
                    diff = near[4] - tiles[t, j][4]
                    weight = jnp.exp(
                        spatial - diff * diff * (1.0 / (2.0 * RANGE_SCALE * RANGE_SCALE))
                    )
                    blocked = None
                    if t == 0 and dy < 0:
                        blocked = no_above & (sub < -dy)
                    if t == own_tiles - 1 and dy > 0:
                        blocked = no_below & (sub >= SUB - dy)
                    if j == 0 and dx < 0:
                        side = no_west & (lane < -dx)
                        blocked = side if blocked is None else blocked | side
                    if j == spans - 1 and dx > 0:
                        side = no_east & (lane >= LANES - dx)
                        blocked = side if blocked is None else blocked | side
                    if blocked is not None:
                        weight = jnp.where(blocked, 0.0, weight)
                    terms = [weight * near[c] for c in range(4)] + [weight]
                    sums[t] = terms if sums[t][0] is None else [a + b for a, b in zip(sums[t], terms)]
        for t in range(own_tiles):
            inverse = 1.0 / sums[t][4]
            for c in range(4):
                out_ref[c, t * SUB : (t + 1) * SUB, j * LANES : (j + 1) * LANES] = (
                    sums[t][c] * inverse
                )


def compute(density, velocity, palette):
    layers, rows, columns = density.shape
    depth_count, row_count = lax.axis_size("depth"), lax.axis_size("row")
    spans = columns // LANES
    width = columns // depth_count
    line = 4 * width + LANES
    assert spans == SUB and rows % SUB == 0 and width % LANES == 0 and layers % 4 == 0 and layers >= 8
    vmem = pl.BlockSpec(memory_space=pltpu.VMEM)
    smem = pl.BlockSpec(memory_space=pltpu.SMEM)
    f32 = jnp.float32

    def shape(*dims):
        return jax.ShapeDtypeStruct(dims, f32)

    def local(*dims):
        return pltpu.VMEM(dims, f32)

    def params(mebibytes):
        return pltpu.CompilerParams(vmem_limit_bytes=mebibytes << 20)

    row_shape = (4, layers, 2, spans, LANES)
    depth_shape = (4, (2 * rows + 1) * spans, LANES)
    corner_shape = (4, spans, LANES)
    block, row0, row1, corner0, corner1 = pl.pallas_call(
        functools.partial(pack_kernel, layers=layers, rows=rows, spans=spans, chunks=4),
        out_shape=(
            local(4, layers, rows, columns), local(*row_shape), local(*row_shape),
            local(*corner_shape), local(*corner_shape),
        ),
        in_specs=[pl.BlockSpec(memory_space=pltpu.HBM)] * 2,
        out_specs=(vmem,) * 5,
        scratch_shapes=[pltpu.VMEM((2,) + row_shape, f32), pltpu.SemaphoreType.DMA((4, 2))],
        name="pack",
        compiler_params=params(8),
    )(
        pltpu.with_memory_space_constraint(density, pltpu.HBM),
        pltpu.with_memory_space_constraint(velocity, pltpu.HBM),
    )
    row1 = swap_rows(row1, 1)
    row0 = swap_rows(row0, 0)
    depth0, depth1 = pl.pallas_call(
        functools.partial(pack_depth_kernel, layers=layers, rows=rows, spans=spans),
        out_shape=(local(*depth_shape), local(*depth_shape)),
        in_specs=[vmem] * 2,
        out_specs=(vmem,) * 2,
        name="pack_depth",
        compiler_params=params(8),
    )(in_vmem(block), in_vmem(row0))
    depth0, depth1 = swap_depths(depth0, 0), swap_depths(depth1, 1)
    corner0, corner1 = swap_corners(corner0, 1, 0), swap_corners(corner1, 1, 1)

    early, share, edge, late, part = pl.pallas_call(
        functools.partial(
            interior_kernel, layers=layers, rows=rows, columns=columns, depth_count=depth_count
        ),
        grid=(layers // 4,),
        out_shape=(
            pltpu.VMEM((layers, 4, spans * rows, LANES), f32),
            pltpu.VMEM((layers, spans * rows, LANES), f32),
            local(layers, 2, 4, spans, LANES), local(layers, 4, spans * rows, LANES),
            local(4, spans * rows, LANES),
        ),
        in_specs=[smem, vmem],
        out_specs=(vmem,) * 5,
        scratch_shapes=[pltpu.VMEM((4, 4, spans * PITCH, LANES), f32)],
        cost_estimate=pl.CostEstimate(
            flops=80 * layers * rows * columns, bytes_accessed=16 * layers * rows * columns,
            transcendentals=layers * rows * columns,
        ),
        name="interior",
        compiler_params=pltpu.CompilerParams(vmem_limit_bytes=24 << 20),
    )(palette, in_vmem(block))

    settled, moving, *parts = pl.pallas_call(
        functools.partial(
            settle_kernel, layers=layers, rows=rows, columns=columns,
            depth_count=depth_count, row_count=row_count,
        ),
        grid=(layers // 4,),
        out_shape=(shape(layers, rows, columns), shape(3, layers, rows, columns))
        + (shape(rows, line),) * depth_count,
        in_specs=[smem] + [vmem] * 12,
        out_specs=(
            pl.BlockSpec((4, rows, columns), lambda i: (i, 0, 0)),
            pl.BlockSpec((3, 4, rows, columns), lambda i: (0, i, 0, 0)),
        )
        + (vmem,) * depth_count,
        scratch_shapes=[
            pltpu.VMEM((2, 4, layers + 2, 2, spans, LANES), f32),
            pltpu.VMEM((layers, 4, 4, spans, LANES), f32),
            pltpu.VMEM((4, 4, 4, spans, LANES), f32),
            pltpu.VMEM((3, 4, spans * PITCH, LANES), f32),
            pltpu.VMEM((4, 4, spans * PITCH, LANES), f32),
            pltpu.VMEM((4, spans * rows, LANES), f32),
        ],
        name="settle",
        compiler_params=pltpu.CompilerParams(vmem_limit_bytes=32 << 20),
    )(
        palette,
        *(
            in_vmem(x)
            for x in (block, row0, row1, depth0, depth1, corner0, corner1, early, share, edge, late, part)
        ),
    )

    parts = [
        lax.ppermute(part, "depth", [(i, i ^ k) for i in range(depth_count)]) if k else part
        for k, part in enumerate(parts)
    ]
    composed, swap0, swap1 = pl.pallas_call(
        functools.partial(over_kernel, count=depth_count, width=width),
        out_shape=(shape(rows, line), shape(2, line), shape(2, line)),
        in_specs=[vmem] * depth_count,
        out_specs=(vmem, vmem, vmem),
        name="over",
        compiler_params=pltpu.CompilerParams(vmem_limit_bytes=8 << 20),
    )(parts[0], *(in_vmem(parts[k]) for k in transfer_order(depth_count)[1:]))

    swap1, swap0 = swap_rows(swap1, 1), swap_rows(swap0, 0)
    filtered = pl.pallas_call(
        functools.partial(
            filter_kernel, width=width, row_count=row_count, depth_count=depth_count
        ),
        out_shape=shape(4, rows, width),
        in_specs=[vmem] * 3,
        out_specs=vmem,
        name="bilateral",
        compiler_params=pltpu.CompilerParams(vmem_limit_bytes=8 << 20),
    )(composed, in_vmem(swap0), in_vmem(swap1))
    return (filtered, settled, moving)


def solution(mesh):
    in_specs = (P("depth", "row", None), P(None, "depth", "row", None), P())
    out_specs = (P(None, "row", "depth"), P("depth", "row", None), P(None, "depth", "row", None))
    return jax.shard_map(compute, mesh=mesh, in_specs=in_specs, out_specs=out_specs, check_vma=False)
```

```python
import functools
import math

import jax
import jax.numpy as jnp
from jax import lax
from jax.experimental import pallas as pl
from jax.experimental.pallas import tpu as pltpu
from jax.sharding import PartitionSpec as P


DIFFUSION = 0.1
ADVECTION = 0.25
VISCOSITY = 0.15
FRICTION = 0.2
OPTICAL = 2.0
RANGE_SCALE = 0.1
SPACE_SCALE = 1.5
SUB = 8
LANES = 128
PITCH = 40
AXES = ("row", "depth")


def row_pairs(kind, count):
    pairs = []
    for low in range(kind, count - 1, 2):
        pairs += [(low, low + 1), (low + 1, low)]
    return pairs


def swap_rows(array, kind):
    return lax.ppermute(array, "row", row_pairs(kind, lax.axis_size("row")))


def swap_depths(array, kind):
    return lax.ppermute(array, "depth", row_pairs(kind, lax.axis_size("depth")))


def swap_corners(array, row_kind, depth_kind):
    depths = lax.axis_size("depth")
    pairs = [
        (a * depths + c, b * depths + d)
        for a, b in row_pairs(row_kind, lax.axis_size("row"))
        for c, d in row_pairs(depth_kind, depths)
    ]
    return lax.ppermute(array, AXES, pairs)


def in_vmem(array):
    return pltpu.with_memory_space_constraint(array, pltpu.VMEM)


def pack_kernel(
    den_ref, vel_ref, block, row0_ref, row1_ref, c10_ref, c11_ref, sides, load_sem,
    *, layers, rows, spans, chunks,
):
    row_odd = lax.rem(lax.axis_index("row"), 2)
    depth_odd = lax.rem(lax.axis_index("depth"), 2)
    size = layers // chunks

    def loads(k):
        z = slice(k * size, (k + 1) * size)
        return (
            pltpu.make_async_copy(den_ref.at[z], block.at[0, z], load_sem.at[k, 0]),
            pltpu.make_async_copy(vel_ref.at[:, z], block.at[1:4, z], load_sem.at[k, 1]),
        )

    for k in range(chunks):
        for copy in loads(k):
            copy.start()
    for k in range(chunks):
        for copy in loads(k):
            copy.wait()
        for c in range(4):
            for z in range(k * size, (k + 1) * size):
                for side in range(2):
                    for n in range(2):
                        row = n + side * (rows - 2)
                        for j in range(spans):
                            sides[side, c, z, n, j : j + 1, :] = block[
                                c, z, row : row + 1, j * LANES : (j + 1) * LANES
                            ]
        for c in range(4):
            for z in range(k * size, (k + 1) * size):
                for n in range(2):
                    row0_ref[c, z, n] = sides[1 - row_odd, c, z, n]
                    row1_ref[c, z, n] = sides[row_odd, c, z, n]
    for target, side in ((c10_ref, 1 - depth_odd), (c11_ref, depth_odd)):
        for c in range(4):
            target[c] = row1_ref[c, side * (layers - 1), row_odd]


def pack_depth_kernel(block, row0_ref, depth0_ref, depth1_ref, *, layers, rows, spans):
    row_odd = lax.rem(lax.axis_index("row"), 2)
    depth_odd = lax.rem(lax.axis_index("depth"), 2)
    for target, side in ((depth0_ref, 1 - depth_odd), (depth1_ref, depth_odd)):
        for c in range(4):
            for n in range(2):
                z = side * (layers - 2) + n
                for j in range(spans):
                    target[c, pl.ds((n * spans + j) * rows, rows), :] = block[
                        c, z, :, j * LANES : (j + 1) * LANES
                    ]
            target[c, pl.ds(2 * spans * rows, spans), :] = row0_ref[
                c, side * (layers - 1), row_odd
            ]


def row_of(j, row):
    return PITCH * j + SUB + row


def advance(here, up, down, left, right, front, back):
    around = [
        ((front[c] + back[c]) + (up[c] + down[c])) + (left[c] + right[c]) for c in range(4)
    ]
    flux = (
        (right[0] * right[1] - left[0] * left[1])
        + (down[0] * down[2] - up[0] * up[2])
        + (back[0] * back[3] - front[0] * front[3])
    )
    squared = here[0] * here[0]
    new = [
        (1.0 - 6.0 * DIFFUSION) * here[0] + (DIFFUSION * around[0] - (0.5 * ADVECTION) * flux)
    ]
    inverse = 1.0 / ((1.0 + squared) * (1.0 + FRICTION * squared))
    own_share = (1.0 + (1.0 - 6.0 * VISCOSITY) * squared) * inverse
    near_share = (VISCOSITY * squared) * inverse
    for c in range(1, 4):
        new.append(here[c] * own_share + around[c] * near_share)
    return new, near_share


def late_share(value, neighbour, near_share, along, sign):
    out = [
        value[0]
        + neighbour[0] * (DIFFUSION + (sign * 0.5 * ADVECTION) * neighbour[along])
    ]
    return out + [value[c] + near_share * neighbour[c] for c in range(1, 4)]


def neighbours(cells, slots, t, j, spans, first, last):
    oldest, middle, newest = slots
    row = t * SUB

    def at(which, r, jj=j):
        return [cells[which, c, pl.ds(row_of(jj, r), SUB), :] for c in range(4)]

    here = at(middle, row)
    zeros = [jnp.zeros((SUB, LANES), jnp.float32)] * 4
    before = at(middle, row, j - 1) if j > 0 else zeros
    after = at(middle, row, j + 1) if j < spans - 1 else zeros
    left = [pltpu.roll(jnp.where(last, b, x), 1, 1) for b, x in zip(before, here)]
    right = [pltpu.roll(jnp.where(first, a, x), LANES - 1, 1) for a, x in zip(after, here)]
    return (
        here, at(middle, row - 1), at(middle, row + 1), left, right,
        at(oldest, row), at(newest, row),
    )


def render(accum, pixels, cells, rate, mix):
    before = accum[3, pixels, :]
    passed = before * jnp.exp2(rate * (cells[0] * cells[0]))
    weight = before - passed
    accum[3, pixels, :] = passed
    for c in range(3):
        mixed = (mix[c][0] * cells[0] + mix[c][1] * cells[1]) + (
            mix[c][2] * cells[2] + mix[c][3] * cells[3]
        )
        accum[c, pixels, :] = accum[c, pixels, :] + weight * jnp.tanh(mixed)


def beside_in_lines(lines, sub, first, last):
    left, right = [], []
    for value in lines:
        before = jnp.where(sub == 0, 0.0, pltpu.roll(value, 1, 0))
        after = jnp.where(sub == SUB - 1, 0.0, pltpu.roll(value, SUB - 1, 0))
        left.append(pltpu.roll(jnp.where(last, before, value), 1, 1))
        right.append(pltpu.roll(jnp.where(first, after, value), LANES - 1, 1))
    return left, right


def constants(palette_ref, depth_total):
    rate = -OPTICAL / depth_total / math.log(2.0)
    return rate, [[0.5 * palette_ref[c, k] for k in range(4)] for c in range(3)]


def interior_kernel(
    palette_ref, block, early_ref, share_ref, edge_ref, late_ref, part_ref, base,
    *, layers, rows, columns, depth_count,
):
    step = pl.program_id(0)
    own_tiles, spans = rows // SUB, columns // LANES
    lane = lax.broadcasted_iota(jnp.int32, (SUB, LANES), 1)
    first, last = lane == 0, lane == LANES - 1

    @pl.when(step == 0)
    def _():
        line = jnp.zeros((spans, LANES), jnp.float32)
        for slot in range(4):
            for c in range(4):
                for row in (-1, rows):
                    base[slot, c, pl.ds(row_of(0, row), spans, stride=PITCH), :] = line
        base[3] = jnp.zeros((4, spans * PITCH, LANES), jnp.float32)
        base[2] = jnp.zeros((4, spans * PITCH, LANES), jnp.float32)
        for c in range(3):
            part_ref[c] = jnp.zeros((spans * rows, LANES), jnp.float32)
        part_ref[3] = jnp.ones((spans * rows, LANES), jnp.float32)

    def first_step(z, slots):
        for j in range(spans):
            for t in range(own_tiles):
                new, share = advance(*neighbours(base, slots, t, j, spans, first, last))
                cells = pl.ds(j * rows + t * SUB, SUB)
                share_ref[z, cells, :] = share
                for c in range(4):
                    early_ref[z, c, cells, :] = new[c]

    for q in range(4):
        z = 4 * step + q
        for t in range(own_tiles):
            for j in range(spans):
                there = (slice(t * SUB, (t + 1) * SUB), slice(j * LANES, (j + 1) * LANES))
                for c in range(4):
                    base[q, c, pl.ds(row_of(j, t * SUB), SUB), :] = block[(c, z) + there]
        for side, row in ((0, 0), (1, rows - 1)):
            for c in range(4):
                edge_ref[z, side, c] = base[q, c, pl.ds(row_of(0, row), spans, stride=PITCH), :]
        first_step(jnp.maximum(z - 1, 0), ((q + 2) % 4, (q + 3) % 4, q))

    rate, mix = constants(palette_ref, layers * depth_count)

    def inner_neighbours(z, t, j):
        row = j * rows + t * SUB

        def at(layer, start):
            return [early_ref[layer, c, pl.ds(start, SUB), :] for c in range(4)]

        here = at(z, row)
        zeros = [jnp.zeros((SUB, LANES), jnp.float32)] * 4
        before = at(z, row - rows) if j > 0 else zeros
        after = at(z, row + rows) if j < spans - 1 else zeros
        if row > 0:
            up = at(z, row - 1)
        else:
            up = [pltpu.roll(x, 1, 0) for x in here]
        if row + SUB < spans * rows:
            down = at(z, row + 1)
        else:
            down = [pltpu.roll(x, SUB - 1, 0) for x in here]
        left = [pltpu.roll(jnp.where(last, b, x), 1, 1) for b, x in zip(before, here)]
        right = [pltpu.roll(jnp.where(first, a, x), LANES - 1, 1) for a, x in zip(after, here)]
        return here, up, down, left, right, at(z - 1, row), at(z + 1, row)

    @pl.when(step > 0)
    def _():
        for q in range(4):
            z = 4 * step + q - 2
            for j in range(spans):
                for t in range(own_tiles):
                    new, _ = advance(*inner_neighbours(z, t, j))
                    cells = pl.ds(j * rows + t * SUB, SUB)
                    for c in range(4):
                        late_ref[z, c, cells, :] = new[c]
                    render(part_ref, cells, new, rate, mix)

    @pl.when(step == layers // 4 - 1)
    def _():
        base[0] = jnp.zeros((4, spans * PITCH, LANES), jnp.float32)
        first_step(layers - 1, (2, 3, 0))


def settle_kernel(
    palette_ref, block, row0_ref, row1_ref, depth0_ref, depth1_ref, c10_ref, c11_ref,
    early_ref, share_ref, edge_ref, part_ref, whole_ref, lines_ref, *rest,
    layers, rows, columns, depth_count, row_count,
):
    pieces = rest[:depth_count]
    rowbuf, srow, base, sbase, accum = rest[depth_count:]
    own_tiles, spans = rows // SUB, columns // LANES
    row_rank, depth_rank = lax.axis_index("row"), lax.axis_index("depth")
    row_odd, depth_odd = lax.rem(row_rank, 2), lax.rem(depth_rank, 2)
    above, below = 1 - row_odd, row_odd
    sub = lax.broadcasted_iota(jnp.int32, (SUB, LANES), 0)
    lane = lax.broadcasted_iota(jnp.int32, (SUB, LANES), 1)
    first, last = lane == 0, lane == LANES - 1
    from_front = jnp.full((SUB, LANES), depth_odd, jnp.int32) == 1
    tiles = [(t, j) for j in range(spans) for t in range(own_tiles)]
    rate, mix = constants(palette_ref, layers * depth_count)

    def tile_of(t, j):
        return slice(t * SUB, (t + 1) * SUB), slice(j * LANES, (j + 1) * LANES)

    def cells_of(t, j):
        return pl.ds(j * rows + t * SUB, SUB)

    def line(row):
        return pl.ds(row_of(0, row), spans, stride=PITCH)

    def outer_step(slot, front):
        kept = (depth_rank > 0) if front else (depth_rank < depth_count - 1)
        keep = jnp.full((SUB, LANES), jnp.where(kept, 1, 0), jnp.int32) == 1
        chosen = from_front if front else jnp.logical_not(from_front)
        far, near = (0, 1) if front else (1, 0)
        for t, j in tiles:
            there = tile_of(t, j)
            for c in range(4):
                for k, n in ((0, far), (1, near)):
                    cells = pl.ds((n * spans + j) * rows + t * SUB, SUB)
                    base[k, c, pl.ds(row_of(j, t * SUB), SUB), :] = jnp.where(
                        chosen, depth0_ref[c, cells, :], depth1_ref[c, cells, :]
                    )
                base[2, c, pl.ds(row_of(j, t * SUB), SUB), :] = block[
                    (c, 0 if front else layers - 1) + there
                ]
        z = 0 if front else layers + 1
        for c in range(4):
            base[1, c, line(-1), :] = rowbuf[above, c, z, 1]
            base[1, c, line(rows), :] = rowbuf[below, c, z, 0]
        slots = (0, 1, 2) if front else (2, 1, 0)
        for t, j in tiles:
            new, _ = advance(*neighbours(base, slots, t, j, spans, first, last))
            for c in range(4):
                sbase[slot, c, pl.ds(row_of(j, t * SUB), SUB), :] = jnp.where(keep, new[c], 0.0)

    def add_layer(z, slot, sign):
        for t, j in tiles:
            cells = pl.ds(row_of(j, t * SUB), SUB)
            new = late_share(
                [sbase[slot, c, cells, :] for c in range(4)],
                [base[1, c, cells, :] for c in range(4)],
                share_ref[z, cells_of(t, j), :], 3, sign,
            )
            for c in range(4):
                sbase[slot, c, cells, :] = new[c]

    def edge_rows(z):
        for side, kind, k, exists in (
            (0, above, 1, row_rank > 0), (1, below, 0, row_rank < row_count - 1),
        ):
            own_cells = pl.ds(0 if side == 0 else rows - 1, spans, stride=rows)

            def halo(layer, n):
                return [rowbuf[kind, c, layer, n] for c in range(4)]

            here, farther = halo(z + 1, k), halo(z + 1, 1 - k)
            own = [edge_ref[z, side, c] for c in range(4)]
            new = late_share(
                [early_ref[z, c, own_cells, :] for c in range(4)], here,
                share_ref[z, own_cells, :], 2, 1.0 if side == 0 else -1.0,
            )
            for c in range(4):
                srow[z, 1 + side, c] = new[c]
            left, right = beside_in_lines(here, sub, first, last)
            up, down = (farther, own) if side == 0 else (own, farther)
            new, _ = advance(here, up, down, left, right, halo(z, k), halo(z + 2, k))
            inside = jnp.full((SUB, LANES), jnp.where(exists, 1, 0), jnp.int32) == 1
            for c in range(4):
                srow[z, 3 * side, c] = jnp.where(inside, new[c], 0.0)

    def take_layer(z, slot):
        for t, j in tiles:
            for c in range(4):
                sbase[slot, c, pl.ds(row_of(j, t * SUB), SUB), :] = early_ref[z, c, cells_of(t, j), :]
        for n, row in enumerate((-1, 0, rows - 1, rows)):
            for c in range(4):
                sbase[slot, c, line(row), :] = srow[z, n, c]

    def whole_layer(n, slots):
        for t, j in tiles:
            new, _ = advance(*neighbours(sbase, slots, t, j, spans, first, last))
            for c in range(4):
                whole_ref[n, c, cells_of(t, j), :] = new[c]
            render(accum, cells_of(t, j), new, rate, mix)

    def outer_rows(z):
        def values(layer, row):
            n = {-1: 0, 0: 1, rows - 1: 2, rows: 3}.get(row)
            if n is not None:
                return [srow[layer, n, c] for c in range(4)]
            return [early_ref[layer, c, pl.ds(row, spans, stride=rows), :] for c in range(4)]

        for n, row in enumerate((0, 1, rows - 2, rows - 1)):
            here = values(z, row)
            left, right = beside_in_lines(here, sub, first, last)
            new, _ = advance(
                here, values(z, row - 1), values(z, row + 1), left, right,
                values(z - 1, row), values(z + 1, row),
            )
            render(accum, pl.ds(row, spans, stride=rows), new, rate, mix)
            for c in range(4):
                lines_ref[z, n, c] = new[c]

    for kind, source in ((0, row0_ref), (1, row1_ref)):
        for c in range(4):
            for z in range(layers):
                for k in range(2):
                    rowbuf[kind, c, z + 1, k] = source[c, z, k]
    beside = pl.ds(2 * spans * rows, spans)
    corners = (
        (0, 0, lambda c: depth0_ref[c, beside, :]), (0, 1, lambda c: depth1_ref[c, beside, :]),
        (1, 0, lambda c: c10_ref[c]), (1, 1, lambda c: c11_ref[c]),
    )
    for row_kind, depth_kind, source in corners:
        is_above = row_odd if row_kind == 0 else 1 - row_odd
        is_front = depth_odd if depth_kind == 0 else 1 - depth_odd
        for c in range(4):
            rowbuf[row_kind, c, (1 - is_front) * (layers + 1), is_above] = source(c)
    for c in range(3):
        accum[c] = jnp.zeros((spans * rows, LANES), jnp.float32)
    accum[3] = jnp.ones((spans * rows, LANES), jnp.float32)

    @pl.loop(0, layers // 2)
    def _(pair):
        edge_rows(2 * pair)
        edge_rows(2 * pair + 1)

    outer_step(3, True)
    take_layer(0, 0)
    add_layer(0, 0, 1.0)
    take_layer(1, 1)
    take_layer(2, 2)
    whole_layer(0, (3, 0, 1))
    whole_layer(1, (0, 1, 2))
    for t, j in tiles:
        pixels = cells_of(t, j)
        through = accum[3, pixels, :]
        inner = jnp.full((SUB, LANES), True)
        if t == 0:
            inner = sub >= 2
        if t == own_tiles - 1:
            inner = (sub < SUB - 2) if t > 0 else inner & (sub < SUB - 2)
        for c in range(3):
            value = accum[c, pixels, :]
            accum[c, pixels, :] = jnp.where(inner, value + through * part_ref[c, pixels, :], value)
        accum[3, pixels, :] = jnp.where(inner, through * part_ref[3, pixels, :], through)

    @pl.loop(0, (layers - 4) // 2)
    def _(pair):
        outer_rows(2 * pair + 2)
        outer_rows(2 * pair + 3)

    take_layer(layers - 3, 0)
    take_layer(layers - 2, 1)
    take_layer(layers - 1, 2)
    outer_step(3, False)
    add_layer(layers - 1, 2, -1.0)
    whole_layer(2, (0, 1, 2))
    whole_layer(3, (1, 2, 3))

    width = columns // depth_count
    per_piece = width // LANES

    def channels(j, t):
        pixels = pl.ds(j * rows + t * SUB, SUB)
        through = accum[3, pixels, :]
        return [0.5 * (accum[c, pixels, :] + (1.0 - through)) for c in range(3)] + [through]

    for k in range(depth_count):
        piece = depth_rank ^ k
        start = piece * per_piece
        for t in range(own_tiles):
            r = slice(t * SUB, (t + 1) * SUB)
            for jj in range(per_piece):
                values = channels(start + jj, t)
                for c in range(4):
                    pieces[k][r, c * width + jj * LANES : c * width + (jj + 1) * LANES] = (
                        values[c]
                    )
            before = channels(jnp.maximum(start - 1, 0), t)
            after = channels(jnp.minimum(start + per_piece, spans - 1), t)
            edge = jnp.zeros((SUB, LANES), jnp.float32)
            for c in range(4):
                for values, low in ((before, 4 * c), (after, 4 * c + 2)):
                    turned = pltpu.roll(values[c], (4 * c + 2) % LANES, 1)
                    edge = jnp.where((lane >= low) & (lane < low + 2), turned, edge)
            pieces[k][r, 4 * width : 4 * width + LANES] = edge


def assemble_kernel(whole_ref, lines_ref, late_ref, den_out, vel_out, *, layers, rows, columns):
    step = pl.program_id(0)
    own_tiles, spans = rows // SUB, columns // LANES

    def put(q, c, there, value):
        if c == 0:
            den_out[(q,) + there] = value
        else:
            vel_out[(c - 1, q) + there] = value

    def copy_layer(source, z, q):
        for j in range(spans):
            lanes = slice(j * LANES, (j + 1) * LANES)
            for c in range(4):
                for t in range(own_tiles):
                    value = source[z, c, pl.ds(j * rows + t * SUB, SUB), :]
                    put(q, c, (slice(t * SUB, (t + 1) * SUB), lanes), value)

    def inner_layer(z, q):
        copy_layer(late_ref, z, q)
        for n, row in enumerate((0, 1, rows - 2, rows - 1)):
            for j in range(spans):
                for c in range(4):
                    there = (slice(row, row + 1), slice(j * LANES, (j + 1) * LANES))
                    put(q, c, there, lines_ref[z, n, c, j : j + 1, :])

    for q in range(4):
        if q < 2:

            @pl.when(step == 0)
            def _():
                copy_layer(whole_ref, q, q)

            pl.when(step > 0)(functools.partial(inner_layer, 4 * step + q, q))
        else:

            @pl.when(step == layers // 4 - 1)
            def _():
                copy_layer(whole_ref, q, q)

            pl.when(step < layers // 4 - 1)(functools.partial(inner_layer, 4 * step + q, q))


def transfer_order(count):
    return sorted(range(count), key=lambda k: (k != 0, k % 2, k)) if count > 2 else list(range(count))


def over_kernel(*refs, count, width):
    parts = [refs[transfer_order(count).index(k)] for k in range(count)]
    picture_ref, swap0_ref, swap1_ref = refs[count:]
    rows = picture_ref.shape[0]
    depth_rank = lax.axis_index("depth")
    row_odd = lax.rem(lax.axis_index("row"), 2)
    lane = lax.broadcasted_iota(jnp.int32, (rows, LANES), 1)

    def split(ref):
        return [ref[:, c * width : (c + 1) * width] for c in range(4)] + [
            ref[:, 4 * width : 4 * width + LANES]
        ]

    def spread_through(edge):
        out = jnp.ones_like(edge)
        for c in range(3):
            turned = pltpu.roll(edge, LANES - 12 + 4 * c, 1)
            out = jnp.where((lane >= 4 * c) & (lane < 4 * c + 4), turned, out)
        return out

    def over(swapped, a, b):
        near = [jnp.where(swapped, y, x) for x, y in zip(a, b)]
        far = [jnp.where(swapped, x, y) for x, y in zip(a, b)]
        out = [near[c] + near[3] * far[c] for c in range(3)]
        out.append(near[3] * far[3])
        edge = near[4] + spread_through(near[4]) * far[4]
        out.append(jnp.where(lane >= 12, near[4] * far[4], edge))
        return out

    values = [split(ref) for ref in parts]
    bit = 0
    while len(values) > 1:
        swapped = (depth_rank >> bit & 1) == 1
        values = [over(swapped, values[k], values[k + 1]) for k in range(0, len(values), 2)]
        bit += 1
    final = values[0]
    for c in range(4):
        picture_ref[:, c * width : (c + 1) * width] = (1.0 - final[3]) if c == 3 else final[c]
    edge = jnp.where((lane >= 12) & (lane < 16), 1.0 - final[4], final[4])
    picture_ref[:, 4 * width : 4 * width + LANES] = edge
    top, bottom = picture_ref[0:2, :], picture_ref[rows - 2 : rows, :]
    odd = row_odd == 1
    swap0_ref[...] = jnp.where(odd, top, bottom)
    swap1_ref[...] = jnp.where(odd, bottom, top)


def filter_kernel(picture_ref, swap0_ref, swap1_ref, out_ref, *, width, row_count, depth_count):
    row_rank, depth_rank = lax.axis_index("row"), lax.axis_index("depth")
    odd = lax.rem(row_rank, 2) == 1
    rows = picture_ref.shape[0]
    own_tiles = rows // SUB
    spans = width // LANES
    lane = lax.broadcasted_iota(jnp.int32, (SUB, LANES), 1)
    sub = lax.broadcasted_iota(jnp.int32, (SUB, LANES), 0)

    def tile(t, c, j):
        if j == -1 or j == spans:
            cols = slice(4 * width, 4 * width + LANES)
        else:
            cols = slice(c * width + j * LANES, c * width + (j + 1) * LANES)
        if t == -1:
            v = jnp.where(odd, swap0_ref[:, cols], swap1_ref[:, cols])
            v = jnp.concatenate([jnp.zeros((SUB - 2, LANES), jnp.float32), v], 0)
        elif t == own_tiles:
            v = jnp.where(odd, swap1_ref[:, cols], swap0_ref[:, cols])
            v = jnp.concatenate([v, jnp.zeros((SUB - 2, LANES), jnp.float32)], 0)
        else:
            v = picture_ref[t * SUB : (t + 1) * SUB, cols]
        if j == -1:
            v = pltpu.roll(v, LANES - 2 - 4 * c, 1)
        elif j == spans:
            v = pltpu.roll(v, (LANES - 2 - 4 * c) % LANES, 1)
        return v

    tiles = {}
    for t in range(-1, own_tiles + 1):
        for j in range(-1, spans + 1):
            four = [tile(t, c, j) for c in range(4)]
            tiles[t, j] = four + [(four[0] + four[1] + four[2]) / 3.0]

    def column_shift(t, j, q, dx):
        if dx == 0:
            return tiles[t, j][q]
        if dx > 0:
            mixed = jnp.where(lane < dx, tiles[t, j + 1][q], tiles[t, j][q])
        else:
            mixed = jnp.where(lane >= LANES + dx, tiles[t, j - 1][q], tiles[t, j][q])
        return pltpu.roll(mixed, (-dx) % LANES, 1)

    no_above, no_below = row_rank == 0, row_rank == row_count - 1
    no_west, no_east = depth_rank == 0, depth_rank == depth_count - 1
    for j in range(spans):
        sums = [[None] * 5 for _ in range(own_tiles)]
        for dx in range(-2, 3):
            shifted = {
                t: [column_shift(t, j, q, dx) for q in range(5)] for t in range(-1, own_tiles + 1)
            }
            for dy in range(-2, 3):
                spatial = -(dx * dx + dy * dy) / (2.0 * SPACE_SCALE * SPACE_SCALE)
                for t in range(own_tiles):
                    if dy == 0:
                        near = shifted[t]
                    elif dy > 0:
                        near = [
                            pltpu.roll(
                                jnp.where(sub < dy, shifted[t + 1][q], shifted[t][q]), SUB - dy, 0
                            )
                            for q in range(5)
                        ]
                    else:
                        near = [
                            pltpu.roll(
                                jnp.where(sub >= SUB + dy, shifted[t - 1][q], shifted[t][q]), -dy, 0
                            )
                            for q in range(5)
                        ]
                    diff = near[4] - tiles[t, j][4]
                    weight = jnp.exp(
                        spatial - diff * diff * (1.0 / (2.0 * RANGE_SCALE * RANGE_SCALE))
                    )
                    blocked = None
                    if t == 0 and dy < 0:
                        blocked = no_above & (sub < -dy)
                    if t == own_tiles - 1 and dy > 0:
                        blocked = no_below & (sub >= SUB - dy)
                    if j == 0 and dx < 0:
                        side = no_west & (lane < -dx)
                        blocked = side if blocked is None else blocked | side
                    if j == spans - 1 and dx > 0:
                        side = no_east & (lane >= LANES - dx)
                        blocked = side if blocked is None else blocked | side
                    if blocked is not None:
                        weight = jnp.where(blocked, 0.0, weight)
                    terms = [weight * near[c] for c in range(4)] + [weight]
                    sums[t] = terms if sums[t][0] is None else [a + b for a, b in zip(sums[t], terms)]
        for t in range(own_tiles):
            inverse = 1.0 / sums[t][4]
            for c in range(4):
                out_ref[c, t * SUB : (t + 1) * SUB, j * LANES : (j + 1) * LANES] = (
                    sums[t][c] * inverse
                )


def compute(density, velocity, palette):
    layers, rows, columns = density.shape
    depth_count, row_count = lax.axis_size("depth"), lax.axis_size("row")
    spans = columns // LANES
    width = columns // depth_count
    line = 4 * width + LANES
    assert spans == SUB and rows % SUB == 0 and width % LANES == 0 and layers % 4 == 0 and layers >= 8
    vmem = pl.BlockSpec(memory_space=pltpu.VMEM)
    smem = pl.BlockSpec(memory_space=pltpu.SMEM)
    f32 = jnp.float32

    def shape(*dims):
        return jax.ShapeDtypeStruct(dims, f32)

    def local(*dims):
        return pltpu.VMEM(dims, f32)

    def params(mebibytes):
        return pltpu.CompilerParams(vmem_limit_bytes=mebibytes << 20)

    row_shape = (4, layers, 2, spans, LANES)
    depth_shape = (4, (2 * rows + 1) * spans, LANES)
    corner_shape = (4, spans, LANES)
    block, row0, row1, corner0, corner1 = pl.pallas_call(
        functools.partial(pack_kernel, layers=layers, rows=rows, spans=spans, chunks=4),
        out_shape=(
            local(4, layers, rows, columns), local(*row_shape), local(*row_shape),
            local(*corner_shape), local(*corner_shape),
        ),
        in_specs=[pl.BlockSpec(memory_space=pltpu.HBM)] * 2,
        out_specs=(vmem,) * 5,
        scratch_shapes=[pltpu.VMEM((2,) + row_shape, f32), pltpu.SemaphoreType.DMA((4, 2))],
        name="pack",
        compiler_params=params(8),
    )(
        pltpu.with_memory_space_constraint(density, pltpu.HBM),
        pltpu.with_memory_space_constraint(velocity, pltpu.HBM),
    )
    row1 = swap_rows(row1, 1)
    row0 = swap_rows(row0, 0)
    depth0, depth1 = pl.pallas_call(
        functools.partial(pack_depth_kernel, layers=layers, rows=rows, spans=spans),
        out_shape=(local(*depth_shape), local(*depth_shape)),
        in_specs=[vmem] * 2,
        out_specs=(vmem,) * 2,
        name="pack_depth",
        compiler_params=params(8),
    )(in_vmem(block), in_vmem(row0))
    depth0, depth1 = swap_depths(depth0, 0), swap_depths(depth1, 1)
    corner0, corner1 = swap_corners(corner0, 1, 0), swap_corners(corner1, 1, 1)

    early, share, edge, late, part = pl.pallas_call(
        functools.partial(
            interior_kernel, layers=layers, rows=rows, columns=columns, depth_count=depth_count
        ),
        grid=(layers // 4,),
        out_shape=(
            pltpu.VMEM((layers, 4, spans * rows, LANES), f32),
            pltpu.VMEM((layers, spans * rows, LANES), f32),
            local(layers, 2, 4, spans, LANES), local(layers, 4, spans * rows, LANES),
            local(4, spans * rows, LANES),
        ),
        in_specs=[smem, vmem],
        out_specs=(vmem,) * 5,
        scratch_shapes=[pltpu.VMEM((4, 4, spans * PITCH, LANES), f32)],
        cost_estimate=pl.CostEstimate(
            flops=80 * layers * rows * columns, bytes_accessed=16 * layers * rows * columns,
            transcendentals=layers * rows * columns,
        ),
        name="interior",
        compiler_params=pltpu.CompilerParams(vmem_limit_bytes=24 << 20),
    )(palette, in_vmem(block))

    whole, lines, *parts = pl.pallas_call(
        functools.partial(
            settle_kernel, layers=layers, rows=rows, columns=columns,
            depth_count=depth_count, row_count=row_count,
        ),
        out_shape=(local(4, 4, spans * rows, LANES), local(layers, 4, 4, spans, LANES))
        + (local(rows, line),) * depth_count,
        in_specs=[smem] + [vmem] * 11,
        out_specs=(vmem,) * (2 + depth_count),
        scratch_shapes=[
            pltpu.VMEM((2, 4, layers + 2, 2, spans, LANES), f32),
            pltpu.VMEM((layers, 4, 4, spans, LANES), f32),
            pltpu.VMEM((3, 4, spans * PITCH, LANES), f32),
            pltpu.VMEM((4, 4, spans * PITCH, LANES), f32),
            pltpu.VMEM((4, spans * rows, LANES), f32),
        ],
        name="settle",
        compiler_params=params(24),
    )(
        palette,
        *(
            in_vmem(x)
            for x in (block, row0, row1, depth0, depth1, corner0, corner1, early, share, edge, part)
        ),
    )

    settled, moving = pl.pallas_call(
        functools.partial(assemble_kernel, layers=layers, rows=rows, columns=columns),
        grid=(layers // 4,),
        out_shape=(shape(layers, rows, columns), shape(3, layers, rows, columns)),
        in_specs=[vmem] * 3,
        out_specs=(
            pl.BlockSpec((4, rows, columns), lambda i: (i, 0, 0)),
            pl.BlockSpec((3, 4, rows, columns), lambda i: (0, i, 0, 0)),
        ),
        cost_estimate=pl.CostEstimate(
            flops=20 * layers * rows * columns, bytes_accessed=16 * layers * rows * columns,
            transcendentals=0,
        ),
        name="assemble",
        compiler_params=params(16),
    )(in_vmem(whole), in_vmem(lines), in_vmem(late))

    for k in range(1, depth_count):
        parts[k] = lax.ppermute(parts[k], "depth", [(i, i ^ k) for i in range(depth_count)])
    composed, swap0, swap1 = pl.pallas_call(
        functools.partial(over_kernel, count=depth_count, width=width),
        out_shape=(shape(rows, line), shape(2, line), shape(2, line)),
        in_specs=[vmem] * depth_count,
        out_specs=(vmem, vmem, vmem),
        name="over",
        compiler_params=pltpu.CompilerParams(vmem_limit_bytes=8 << 20),
    )(parts[0], *(in_vmem(parts[k]) for k in transfer_order(depth_count)[1:]))

    swap1, swap0 = swap_rows(swap1, 1), swap_rows(swap0, 0)
    filtered = pl.pallas_call(
        functools.partial(
            filter_kernel, width=width, row_count=row_count, depth_count=depth_count
        ),
        out_shape=shape(4, rows, width),
        in_specs=[vmem] * 3,
        out_specs=vmem,
        name="bilateral",
        compiler_params=pltpu.CompilerParams(vmem_limit_bytes=8 << 20),
    )(composed, in_vmem(swap0), in_vmem(swap1))
    return (filtered, settled, moving)


def solution(mesh):
    in_specs = (P("depth", "row", None), P(None, "depth", "row", None), P())
    out_specs = (P(None, "row", "depth"), P("depth", "row", None), P(None, "depth", "row", None))
    return jax.shard_map(compute, mesh=mesh, in_specs=in_specs, out_specs=out_specs, check_vma=False)
```

```python
import functools
import math

import jax
import jax.numpy as jnp
from jax import lax
from jax.experimental import pallas as pl
from jax.experimental.pallas import tpu as pltpu
from jax.sharding import PartitionSpec as P


DIFFUSION = 0.1
ADVECTION = 0.25
VISCOSITY = 0.15
FRICTION = 0.2
OPTICAL = 2.0
RANGE_SCALE = 0.1
SPACE_SCALE = 1.5
SUB = 8
LANES = 128
PITCH = 40
AXES = ("row", "depth")


def row_pairs(kind, count):
    pairs = []
    for low in range(kind, count - 1, 2):
        pairs += [(low, low + 1), (low + 1, low)]
    return pairs


def swap_rows(array, kind):
    return lax.ppermute(array, "row", row_pairs(kind, lax.axis_size("row")))


def swap_depths(array, kind):
    return lax.ppermute(array, "depth", row_pairs(kind, lax.axis_size("depth")))


def swap_corners(array, row_kind, depth_kind):
    depths = lax.axis_size("depth")
    pairs = [
        (a * depths + c, b * depths + d)
        for a, b in row_pairs(row_kind, lax.axis_size("row"))
        for c, d in row_pairs(depth_kind, depths)
    ]
    return lax.ppermute(array, AXES, pairs)


def in_vmem(array):
    return pltpu.with_memory_space_constraint(array, pltpu.VMEM)


def pack_kernel(
    den_ref, vel_ref, block, row0_ref, row1_ref, c10_ref, c11_ref, sides, load_sem,
    *, layers, rows, spans, chunks,
):
    row_odd = lax.rem(lax.axis_index("row"), 2)
    depth_odd = lax.rem(lax.axis_index("depth"), 2)
    size = layers // chunks

    def loads(k):
        z = slice(k * size, (k + 1) * size)
        return (
            pltpu.make_async_copy(den_ref.at[z], block.at[0, z], load_sem.at[k, 0]),
            pltpu.make_async_copy(vel_ref.at[:, z], block.at[1:4, z], load_sem.at[k, 1]),
        )

    for k in range(chunks):
        for copy in loads(k):
            copy.start()
    for k in range(chunks):
        for copy in loads(k):
            copy.wait()
        for c in range(4):
            for z in range(k * size, (k + 1) * size):
                for side in range(2):
                    for n in range(2):
                        row = n + side * (rows - 2)
                        for j in range(spans):
                            sides[side, c, z, n, j : j + 1, :] = block[
                                c, z, row : row + 1, j * LANES : (j + 1) * LANES
                            ]
        for c in range(4):
            for z in range(k * size, (k + 1) * size):
                for n in range(2):
                    row0_ref[c, z, n] = sides[1 - row_odd, c, z, n]
                    row1_ref[c, z, n] = sides[row_odd, c, z, n]
    for target, side in ((c10_ref, 1 - depth_odd), (c11_ref, depth_odd)):
        for c in range(4):
            target[c] = row1_ref[c, side * (layers - 1), row_odd]


def pack_depth_kernel(block, row0_ref, depth0_ref, depth1_ref, *, layers, rows, spans):
    row_odd = lax.rem(lax.axis_index("row"), 2)
    depth_odd = lax.rem(lax.axis_index("depth"), 2)
    for target, side in ((depth0_ref, 1 - depth_odd), (depth1_ref, depth_odd)):
        for c in range(4):
            for n in range(2):
                z = side * (layers - 2) + n
                for j in range(spans):
                    target[c, pl.ds((n * spans + j) * rows, rows), :] = block[
                        c, z, :, j * LANES : (j + 1) * LANES
                    ]
            target[c, pl.ds(2 * spans * rows, spans), :] = row0_ref[
                c, side * (layers - 1), row_odd
            ]


def row_of(j, row):
    return PITCH * j + SUB + row


def advance(here, up, down, left, right, front, back):
    around = [
        ((front[c] + back[c]) + (up[c] + down[c])) + (left[c] + right[c]) for c in range(4)
    ]
    flux = (
        (right[0] * right[1] - left[0] * left[1])
        + (down[0] * down[2] - up[0] * up[2])
        + (back[0] * back[3] - front[0] * front[3])
    )
    squared = here[0] * here[0]
    new = [
        (1.0 - 6.0 * DIFFUSION) * here[0] + (DIFFUSION * around[0] - (0.5 * ADVECTION) * flux)
    ]
    inverse = 1.0 / ((1.0 + squared) * (1.0 + FRICTION * squared))
    own_share = (1.0 + (1.0 - 6.0 * VISCOSITY) * squared) * inverse
    near_share = (VISCOSITY * squared) * inverse
    for c in range(1, 4):
        new.append(here[c] * own_share + around[c] * near_share)
    return new, near_share


def late_share(value, neighbour, near_share, along, sign):
    out = [
        value[0]
        + neighbour[0] * (DIFFUSION + (sign * 0.5 * ADVECTION) * neighbour[along])
    ]
    return out + [value[c] + near_share * neighbour[c] for c in range(1, 4)]


def neighbours(cells, slots, t, j, spans, first, last):
    oldest, middle, newest = slots
    row = t * SUB

    def at(which, r, jj=j):
        return [cells[which, c, pl.ds(row_of(jj, r), SUB), :] for c in range(4)]

    here = at(middle, row)
    zeros = [jnp.zeros((SUB, LANES), jnp.float32)] * 4
    before = at(middle, row, j - 1) if j > 0 else zeros
    after = at(middle, row, j + 1) if j < spans - 1 else zeros
    left = [pltpu.roll(jnp.where(last, b, x), 1, 1) for b, x in zip(before, here)]
    right = [pltpu.roll(jnp.where(first, a, x), LANES - 1, 1) for a, x in zip(after, here)]
    return (
        here, at(middle, row - 1), at(middle, row + 1), left, right,
        at(oldest, row), at(newest, row),
    )


def render(accum, pixels, cells, rate, mix):
    before = accum[3, pixels, :]
    passed = before * jnp.exp2(rate * (cells[0] * cells[0]))
    weight = before - passed
    accum[3, pixels, :] = passed
    for c in range(3):
        mixed = (mix[c][0] * cells[0] + mix[c][1] * cells[1]) + (
            mix[c][2] * cells[2] + mix[c][3] * cells[3]
        )
        accum[c, pixels, :] = accum[c, pixels, :] + weight * jnp.tanh(mixed)


def beside_in_lines(lines, sub, first, last):
    left, right = [], []
    for value in lines:
        before = jnp.where(sub == 0, 0.0, pltpu.roll(value, 1, 0))
        after = jnp.where(sub == SUB - 1, 0.0, pltpu.roll(value, SUB - 1, 0))
        left.append(pltpu.roll(jnp.where(last, before, value), 1, 1))
        right.append(pltpu.roll(jnp.where(first, after, value), LANES - 1, 1))
    return left, right


def constants(palette_ref, depth_total):
    rate = -OPTICAL / depth_total / math.log(2.0)
    return rate, [[0.5 * palette_ref[c, k] for k in range(4)] for c in range(3)]


def interior_kernel(
    palette_ref, block, early_ref, share_ref, edge_ref, late_ref, part_ref, base,
    *, layers, rows, columns, depth_count,
):
    step = pl.program_id(0)
    own_tiles, spans = rows // SUB, columns // LANES
    lane = lax.broadcasted_iota(jnp.int32, (SUB, LANES), 1)
    first, last = lane == 0, lane == LANES - 1

    @pl.when(step == 0)
    def _():
        line = jnp.zeros((spans, LANES), jnp.float32)
        for slot in range(4):
            for c in range(4):
                for row in (-1, rows):
                    base[slot, c, pl.ds(row_of(0, row), spans, stride=PITCH), :] = line
        base[3] = jnp.zeros((4, spans * PITCH, LANES), jnp.float32)
        base[2] = jnp.zeros((4, spans * PITCH, LANES), jnp.float32)
        for c in range(3):
            part_ref[c] = jnp.zeros((spans * rows, LANES), jnp.float32)
        part_ref[3] = jnp.ones((spans * rows, LANES), jnp.float32)

    def first_step(z, slots):
        for j in range(spans):
            for t in range(own_tiles):
                new, share = advance(*neighbours(base, slots, t, j, spans, first, last))
                cells = pl.ds(j * rows + t * SUB, SUB)
                share_ref[z, cells, :] = share
                for c in range(4):
                    early_ref[z, c, cells, :] = new[c]

    for q in range(4):
        z = 4 * step + q
        for t in range(own_tiles):
            for j in range(spans):
                there = (slice(t * SUB, (t + 1) * SUB), slice(j * LANES, (j + 1) * LANES))
                for c in range(4):
                    base[q, c, pl.ds(row_of(j, t * SUB), SUB), :] = block[(c, z) + there]
        for side, row in ((0, 0), (1, rows - 1)):
            for c in range(4):
                edge_ref[z, side, c] = base[q, c, pl.ds(row_of(0, row), spans, stride=PITCH), :]
        first_step(jnp.maximum(z - 1, 0), ((q + 2) % 4, (q + 3) % 4, q))

    rate, mix = constants(palette_ref, layers * depth_count)

    def inner_neighbours(z, t, j):
        row = j * rows + t * SUB

        def at(layer, start):
            return [early_ref[layer, c, pl.ds(start, SUB), :] for c in range(4)]

        here = at(z, row)
        zeros = [jnp.zeros((SUB, LANES), jnp.float32)] * 4
        before = at(z, row - rows) if j > 0 else zeros
        after = at(z, row + rows) if j < spans - 1 else zeros
        if row > 0:
            up = at(z, row - 1)
        else:
            up = [pltpu.roll(x, 1, 0) for x in here]
        if row + SUB < spans * rows:
            down = at(z, row + 1)
        else:
            down = [pltpu.roll(x, SUB - 1, 0) for x in here]
        left = [pltpu.roll(jnp.where(last, b, x), 1, 1) for b, x in zip(before, here)]
        right = [pltpu.roll(jnp.where(first, a, x), LANES - 1, 1) for a, x in zip(after, here)]
        return here, up, down, left, right, at(z - 1, row), at(z + 1, row)

    @pl.when(step > 0)
    def _():
        for q in range(4):
            z = 4 * step + q - 2
            for j in range(spans):
                for t in range(own_tiles):
                    new, _ = advance(*inner_neighbours(z, t, j))
                    cells = pl.ds(j * rows + t * SUB, SUB)
                    for c in range(4):
                        late_ref[z, c, cells, :] = new[c]
                    render(part_ref, cells, new, rate, mix)

    @pl.when(step == layers // 4 - 1)
    def _():
        base[0] = jnp.zeros((4, spans * PITCH, LANES), jnp.float32)
        first_step(layers - 1, (2, 3, 0))


def edge_rows(z, rowbuf, early_ref, share_ref, edge_ref, srow, places, rows, spans):
    above, below, has_above, has_below = places
    sub = lax.broadcasted_iota(jnp.int32, (SUB, LANES), 0)
    lane = lax.broadcasted_iota(jnp.int32, (SUB, LANES), 1)
    first, last = lane == 0, lane == LANES - 1
    for side, kind, k, exists in ((0, above, 1, has_above), (1, below, 0, has_below)):
        own_cells = pl.ds(0 if side == 0 else rows - 1, spans, stride=rows)

        def halo(layer, n):
            return [rowbuf[kind, c, layer, n] for c in range(4)]

        here, farther = halo(z + 1, k), halo(z + 1, 1 - k)
        own = [edge_ref[z, side, c] for c in range(4)]
        new = late_share(
            [early_ref[z, c, own_cells, :] for c in range(4)], here,
            share_ref[z, own_cells, :], 2, 1.0 if side == 0 else -1.0,
        )
        for c in range(4):
            srow[z, 1 + side, c] = new[c]
        left, right = beside_in_lines(here, sub, first, last)
        up, down = (farther, own) if side == 0 else (own, farther)
        new, _ = advance(here, up, down, left, right, halo(z, k), halo(z + 2, k))
        inside = jnp.full((SUB, LANES), jnp.where(exists, 1, 0), jnp.int32) == 1
        for c in range(4):
            srow[z, 3 * side, c] = jnp.where(inside, new[c], 0.0)


def row_places(row_count):
    row_rank = lax.axis_index("row")
    row_odd = lax.rem(row_rank, 2)
    return 1 - row_odd, row_odd, row_rank > 0, row_rank < row_count - 1


def outer_kernel(
    palette_ref, row0_ref, row1_ref, early_ref, share_ref, edge_ref,
    rowbuf, srow, lines_ref, part_ref, *, layers, rows, columns, depth_count, row_count,
):
    spans = columns // LANES
    sub = lax.broadcasted_iota(jnp.int32, (SUB, LANES), 0)
    lane = lax.broadcasted_iota(jnp.int32, (SUB, LANES), 1)
    first, last = lane == 0, lane == LANES - 1
    places = row_places(row_count)
    rate, mix = constants(palette_ref, layers * depth_count)
    for kind, source in ((0, row0_ref), (1, row1_ref)):
        for c in range(4):
            for z in range(layers):
                for k in range(2):
                    rowbuf[kind, c, z + 1, k] = source[c, z, k]
    for c in range(3):
        part_ref[c] = jnp.zeros((4 * spans, LANES), jnp.float32)
    part_ref[3] = jnp.ones((4 * spans, LANES), jnp.float32)

    def outer_rows(z):
        def values(layer, row):
            n = {-1: 0, 0: 1, rows - 1: 2, rows: 3}.get(row)
            if n is not None:
                return [srow[layer, n, c] for c in range(4)]
            return [early_ref[layer, c, pl.ds(row, spans, stride=rows), :] for c in range(4)]

        for n, row in enumerate((0, 1, rows - 2, rows - 1)):
            here = values(z, row)
            left, right = beside_in_lines(here, sub, first, last)
            new, _ = advance(
                here, values(z, row - 1), values(z, row + 1), left, right,
                values(z - 1, row), values(z + 1, row),
            )
            render(part_ref, pl.ds(n * spans, spans), new, rate, mix)
            for c in range(4):
                lines_ref[z, n, c] = new[c]

    def edges(z):
        edge_rows(z, rowbuf, early_ref, share_ref, edge_ref, srow, places, rows, spans)

    @pl.loop(0, (layers - 2) // 2)
    def _(pair):
        edges(2 * pair + 1)
        edges(2 * pair + 2)

    @pl.loop(0, (layers - 4) // 2)
    def _(pair):
        outer_rows(2 * pair + 2)
        outer_rows(2 * pair + 3)


def settle_kernel(
    palette_ref, block, depth0_ref, depth1_ref, c10_ref, c11_ref,
    early_ref, share_ref, edge_ref, part_ref, rows_part_ref, given_rowbuf, given_srow,
    whole_ref, rowbuf, srow, *rest,
    layers, rows, columns, depth_count, row_count,
):
    pieces = rest[:depth_count]
    base, sbase, accum = rest[depth_count:]
    own_tiles, spans = rows // SUB, columns // LANES
    row_rank, depth_rank = lax.axis_index("row"), lax.axis_index("depth")
    row_odd, depth_odd = lax.rem(row_rank, 2), lax.rem(depth_rank, 2)
    above, below = 1 - row_odd, row_odd
    sub = lax.broadcasted_iota(jnp.int32, (SUB, LANES), 0)
    lane = lax.broadcasted_iota(jnp.int32, (SUB, LANES), 1)
    first, last = lane == 0, lane == LANES - 1
    from_front = jnp.full((SUB, LANES), depth_odd, jnp.int32) == 1
    tiles = [(t, j) for j in range(spans) for t in range(own_tiles)]
    rate, mix = constants(palette_ref, layers * depth_count)

    def tile_of(t, j):
        return slice(t * SUB, (t + 1) * SUB), slice(j * LANES, (j + 1) * LANES)

    def cells_of(t, j):
        return pl.ds(j * rows + t * SUB, SUB)

    def line(row):
        return pl.ds(row_of(0, row), spans, stride=PITCH)

    def outer_step(slot, front):
        kept = (depth_rank > 0) if front else (depth_rank < depth_count - 1)
        keep = jnp.full((SUB, LANES), jnp.where(kept, 1, 0), jnp.int32) == 1
        chosen = from_front if front else jnp.logical_not(from_front)
        far, near = (0, 1) if front else (1, 0)
        for t, j in tiles:
            there = tile_of(t, j)
            for c in range(4):
                for k, n in ((0, far), (1, near)):
                    cells = pl.ds((n * spans + j) * rows + t * SUB, SUB)
                    base[k, c, pl.ds(row_of(j, t * SUB), SUB), :] = jnp.where(
                        chosen, depth0_ref[c, cells, :], depth1_ref[c, cells, :]
                    )
                base[2, c, pl.ds(row_of(j, t * SUB), SUB), :] = block[
                    (c, 0 if front else layers - 1) + there
                ]
        z = 0 if front else layers + 1
        for c in range(4):
            base[1, c, line(-1), :] = rowbuf[above, c, z, 1]
            base[1, c, line(rows), :] = rowbuf[below, c, z, 0]
        slots = (0, 1, 2) if front else (2, 1, 0)
        for t, j in tiles:
            new, _ = advance(*neighbours(base, slots, t, j, spans, first, last))
            for c in range(4):
                sbase[slot, c, pl.ds(row_of(j, t * SUB), SUB), :] = jnp.where(keep, new[c], 0.0)

    def add_layer(z, slot, sign):
        for t, j in tiles:
            cells = pl.ds(row_of(j, t * SUB), SUB)
            new = late_share(
                [sbase[slot, c, cells, :] for c in range(4)],
                [base[1, c, cells, :] for c in range(4)],
                share_ref[z, cells_of(t, j), :], 3, sign,
            )
            for c in range(4):
                sbase[slot, c, cells, :] = new[c]

    def take_layer(z, slot):
        for t, j in tiles:
            for c in range(4):
                sbase[slot, c, pl.ds(row_of(j, t * SUB), SUB), :] = early_ref[z, c, cells_of(t, j), :]
        for n, row in enumerate((-1, 0, rows - 1, rows)):
            for c in range(4):
                sbase[slot, c, line(row), :] = srow[z, n, c]

    def whole_layer(n, slots):
        for t, j in tiles:
            new, _ = advance(*neighbours(sbase, slots, t, j, spans, first, last))
            for c in range(4):
                whole_ref[n, c, cells_of(t, j), :] = new[c]
            render(accum, cells_of(t, j), new, rate, mix)

    beside = pl.ds(2 * spans * rows, spans)
    corners = (
        (0, 0, lambda c: depth0_ref[c, beside, :]), (0, 1, lambda c: depth1_ref[c, beside, :]),
        (1, 0, lambda c: c10_ref[c]), (1, 1, lambda c: c11_ref[c]),
    )
    for row_kind, depth_kind, source in corners:
        is_above = row_odd if row_kind == 0 else 1 - row_odd
        is_front = depth_odd if depth_kind == 0 else 1 - depth_odd
        for c in range(4):
            rowbuf[row_kind, c, (1 - is_front) * (layers + 1), is_above] = source(c)
    for c in range(3):
        accum[c] = jnp.zeros((spans * rows, LANES), jnp.float32)
    accum[3] = jnp.ones((spans * rows, LANES), jnp.float32)

    for z in (0, layers - 1):
        edge_rows(
            z, rowbuf, early_ref, share_ref, edge_ref, srow, row_places(row_count), rows, spans
        )

    outer_step(3, True)
    take_layer(0, 0)
    add_layer(0, 0, 1.0)
    take_layer(1, 1)
    take_layer(2, 2)
    whole_layer(0, (3, 0, 1))
    whole_layer(1, (0, 1, 2))
    for t, j in tiles:
        pixels = cells_of(t, j)
        through = accum[3, pixels, :]
        inner = jnp.full((SUB, LANES), True)
        if t == 0:
            inner = sub >= 2
        if t == own_tiles - 1:
            inner = (sub < SUB - 2) if t > 0 else inner & (sub < SUB - 2)
        for c in range(3):
            value = accum[c, pixels, :]
            accum[c, pixels, :] = jnp.where(inner, value + through * part_ref[c, pixels, :], value)
        accum[3, pixels, :] = jnp.where(inner, through * part_ref[3, pixels, :], through)

    for n, row in enumerate((0, 1, rows - 2, rows - 1)):
        pixels, theirs = pl.ds(row, spans, stride=rows), pl.ds(n * spans, spans)
        through = accum[3, pixels, :]
        for c in range(3):
            accum[c, pixels, :] = accum[c, pixels, :] + through * rows_part_ref[c, theirs, :]
        accum[3, pixels, :] = through * rows_part_ref[3, theirs, :]

    take_layer(layers - 3, 0)
    take_layer(layers - 2, 1)
    take_layer(layers - 1, 2)
    outer_step(3, False)
    add_layer(layers - 1, 2, -1.0)
    whole_layer(2, (0, 1, 2))
    whole_layer(3, (1, 2, 3))

    width = columns // depth_count
    per_piece = width // LANES

    def channels(j, t):
        pixels = pl.ds(j * rows + t * SUB, SUB)
        through = accum[3, pixels, :]
        return [0.5 * (accum[c, pixels, :] + (1.0 - through)) for c in range(3)] + [through]

    for k in range(depth_count):
        piece = depth_rank ^ k
        start = piece * per_piece
        for t in range(own_tiles):
            r = slice(t * SUB, (t + 1) * SUB)
            for jj in range(per_piece):
                values = channels(start + jj, t)
                for c in range(4):
                    pieces[k][r, c * width + jj * LANES : c * width + (jj + 1) * LANES] = (
                        values[c]
                    )
            before = channels(jnp.maximum(start - 1, 0), t)
            after = channels(jnp.minimum(start + per_piece, spans - 1), t)
            edge = jnp.zeros((SUB, LANES), jnp.float32)
            for c in range(4):
                for values, low in ((before, 4 * c), (after, 4 * c + 2)):
                    turned = pltpu.roll(values[c], (4 * c + 2) % LANES, 1)
                    edge = jnp.where((lane >= low) & (lane < low + 2), turned, edge)
            pieces[k][r, 4 * width : 4 * width + LANES] = edge


def assemble_kernel(whole_ref, lines_ref, late_ref, den_out, vel_out, *, layers, rows, columns):
    step = pl.program_id(0)
    own_tiles, spans = rows // SUB, columns // LANES

    def put(q, c, there, value):
        if c == 0:
            den_out[(q,) + there] = value
        else:
            vel_out[(c - 1, q) + there] = value

    def copy_layer(source, z, q):
        for j in range(spans):
            lanes = slice(j * LANES, (j + 1) * LANES)
            for c in range(4):
                for t in range(own_tiles):
                    value = source[z, c, pl.ds(j * rows + t * SUB, SUB), :]
                    put(q, c, (slice(t * SUB, (t + 1) * SUB), lanes), value)

    def inner_layer(z, q):
        copy_layer(late_ref, z, q)
        for n, row in enumerate((0, 1, rows - 2, rows - 1)):
            for j in range(spans):
                for c in range(4):
                    there = (slice(row, row + 1), slice(j * LANES, (j + 1) * LANES))
                    put(q, c, there, lines_ref[z, n, c, j : j + 1, :])

    for q in range(4):
        if q < 2:

            @pl.when(step == 0)
            def _():
                copy_layer(whole_ref, q, q)

            pl.when(step > 0)(functools.partial(inner_layer, 4 * step + q, q))
        else:

            @pl.when(step == layers // 4 - 1)
            def _():
                copy_layer(whole_ref, q, q)

            pl.when(step < layers // 4 - 1)(functools.partial(inner_layer, 4 * step + q, q))


def transfer_order(count):
    return sorted(range(count), key=lambda k: (k != 0, k % 2, k)) if count > 2 else list(range(count))


def over_kernel(*refs, count, width):
    parts = [refs[transfer_order(count).index(k)] for k in range(count)]
    picture_ref, swap0_ref, swap1_ref = refs[count:]
    rows = picture_ref.shape[0]
    depth_rank = lax.axis_index("depth")
    row_odd = lax.rem(lax.axis_index("row"), 2)
    lane = lax.broadcasted_iota(jnp.int32, (rows, LANES), 1)

    def split(ref):
        return [ref[:, c * width : (c + 1) * width] for c in range(4)] + [
            ref[:, 4 * width : 4 * width + LANES]
        ]

    def spread_through(edge):
        out = jnp.ones_like(edge)
        for c in range(3):
            turned = pltpu.roll(edge, LANES - 12 + 4 * c, 1)
            out = jnp.where((lane >= 4 * c) & (lane < 4 * c + 4), turned, out)
        return out

    def over(swapped, a, b):
        near = [jnp.where(swapped, y, x) for x, y in zip(a, b)]
        far = [jnp.where(swapped, x, y) for x, y in zip(a, b)]
        out = [near[c] + near[3] * far[c] for c in range(3)]
        out.append(near[3] * far[3])
        edge = near[4] + spread_through(near[4]) * far[4]
        out.append(jnp.where(lane >= 12, near[4] * far[4], edge))
        return out

    values = [split(ref) for ref in parts]
    bit = 0
    while len(values) > 1:
        swapped = (depth_rank >> bit & 1) == 1
        values = [over(swapped, values[k], values[k + 1]) for k in range(0, len(values), 2)]
        bit += 1
    final = values[0]
    for c in range(4):
        picture_ref[:, c * width : (c + 1) * width] = (1.0 - final[3]) if c == 3 else final[c]
    edge = jnp.where((lane >= 12) & (lane < 16), 1.0 - final[4], final[4])
    picture_ref[:, 4 * width : 4 * width + LANES] = edge
    top, bottom = picture_ref[0:2, :], picture_ref[rows - 2 : rows, :]
    odd = row_odd == 1
    swap0_ref[...] = jnp.where(odd, top, bottom)
    swap1_ref[...] = jnp.where(odd, bottom, top)


def filter_kernel(picture_ref, swap0_ref, swap1_ref, out_ref, *, width, row_count, depth_count):
    row_rank, depth_rank = lax.axis_index("row"), lax.axis_index("depth")
    odd = lax.rem(row_rank, 2) == 1
    rows = picture_ref.shape[0]
    own_tiles = rows // SUB
    spans = width // LANES
    lane = lax.broadcasted_iota(jnp.int32, (SUB, LANES), 1)
    sub = lax.broadcasted_iota(jnp.int32, (SUB, LANES), 0)

    def tile(t, c, j):
        if j == -1 or j == spans:
            cols = slice(4 * width, 4 * width + LANES)
        else:
            cols = slice(c * width + j * LANES, c * width + (j + 1) * LANES)
        if t == -1:
            v = jnp.where(odd, swap0_ref[:, cols], swap1_ref[:, cols])
            v = jnp.concatenate([jnp.zeros((SUB - 2, LANES), jnp.float32), v], 0)
        elif t == own_tiles:
            v = jnp.where(odd, swap1_ref[:, cols], swap0_ref[:, cols])
            v = jnp.concatenate([v, jnp.zeros((SUB - 2, LANES), jnp.float32)], 0)
        else:
            v = picture_ref[t * SUB : (t + 1) * SUB, cols]
        if j == -1:
            v = pltpu.roll(v, LANES - 2 - 4 * c, 1)
        elif j == spans:
            v = pltpu.roll(v, (LANES - 2 - 4 * c) % LANES, 1)
        return v

    tiles = {}
    for t in range(-1, own_tiles + 1):
        for j in range(-1, spans + 1):
            four = [tile(t, c, j) for c in range(4)]
            tiles[t, j] = four + [(four[0] + four[1] + four[2]) / 3.0]

    def column_shift(t, j, q, dx):
        if dx == 0:
            return tiles[t, j][q]
        if dx > 0:
            mixed = jnp.where(lane < dx, tiles[t, j + 1][q], tiles[t, j][q])
        else:
            mixed = jnp.where(lane >= LANES + dx, tiles[t, j - 1][q], tiles[t, j][q])
        return pltpu.roll(mixed, (-dx) % LANES, 1)

    no_above, no_below = row_rank == 0, row_rank == row_count - 1
    no_west, no_east = depth_rank == 0, depth_rank == depth_count - 1
    for j in range(spans):
        sums = [[None] * 5 for _ in range(own_tiles)]
        for dx in range(-2, 3):
            shifted = {
                t: [column_shift(t, j, q, dx) for q in range(5)] for t in range(-1, own_tiles + 1)
            }
            for dy in range(-2, 3):
                spatial = -(dx * dx + dy * dy) / (2.0 * SPACE_SCALE * SPACE_SCALE)
                for t in range(own_tiles):
                    if dy == 0:
                        near = shifted[t]
                    elif dy > 0:
                        near = [
                            pltpu.roll(
                                jnp.where(sub < dy, shifted[t + 1][q], shifted[t][q]), SUB - dy, 0
                            )
                            for q in range(5)
                        ]
                    else:
                        near = [
                            pltpu.roll(
                                jnp.where(sub >= SUB + dy, shifted[t - 1][q], shifted[t][q]), -dy, 0
                            )
                            for q in range(5)
                        ]
                    diff = near[4] - tiles[t, j][4]
                    weight = jnp.exp(
                        spatial - diff * diff * (1.0 / (2.0 * RANGE_SCALE * RANGE_SCALE))
                    )
                    blocked = None
                    if t == 0 and dy < 0:
                        blocked = no_above & (sub < -dy)
                    if t == own_tiles - 1 and dy > 0:
                        blocked = no_below & (sub >= SUB - dy)
                    if j == 0 and dx < 0:
                        side = no_west & (lane < -dx)
                        blocked = side if blocked is None else blocked | side
                    if j == spans - 1 and dx > 0:
                        side = no_east & (lane >= LANES - dx)
                        blocked = side if blocked is None else blocked | side
                    if blocked is not None:
                        weight = jnp.where(blocked, 0.0, weight)
                    terms = [weight * near[c] for c in range(4)] + [weight]
                    sums[t] = terms if sums[t][0] is None else [a + b for a, b in zip(sums[t], terms)]
        for t in range(own_tiles):
            inverse = 1.0 / sums[t][4]
            for c in range(4):
                out_ref[c, t * SUB : (t + 1) * SUB, j * LANES : (j + 1) * LANES] = (
                    sums[t][c] * inverse
                )


def compute(density, velocity, palette):
    layers, rows, columns = density.shape
    depth_count, row_count = lax.axis_size("depth"), lax.axis_size("row")
    spans = columns // LANES
    width = columns // depth_count
    line = 4 * width + LANES
    assert spans == SUB and rows % SUB == 0 and width % LANES == 0 and layers % 4 == 0 and layers >= 8
    vmem = pl.BlockSpec(memory_space=pltpu.VMEM)
    smem = pl.BlockSpec(memory_space=pltpu.SMEM)
    f32 = jnp.float32

    def shape(*dims):
        return jax.ShapeDtypeStruct(dims, f32)

    def local(*dims):
        return pltpu.VMEM(dims, f32)

    def params(mebibytes):
        return pltpu.CompilerParams(vmem_limit_bytes=mebibytes << 20)

    row_shape = (4, layers, 2, spans, LANES)
    depth_shape = (4, (2 * rows + 1) * spans, LANES)
    corner_shape = (4, spans, LANES)
    block, row0, row1, corner0, corner1 = pl.pallas_call(
        functools.partial(pack_kernel, layers=layers, rows=rows, spans=spans, chunks=4),
        out_shape=(
            local(4, layers, rows, columns), local(*row_shape), local(*row_shape),
            local(*corner_shape), local(*corner_shape),
        ),
        in_specs=[pl.BlockSpec(memory_space=pltpu.HBM)] * 2,
        out_specs=(vmem,) * 5,
        scratch_shapes=[pltpu.VMEM((2,) + row_shape, f32), pltpu.SemaphoreType.DMA((4, 2))],
        name="pack",
        compiler_params=params(8),
    )(
        pltpu.with_memory_space_constraint(density, pltpu.HBM),
        pltpu.with_memory_space_constraint(velocity, pltpu.HBM),
    )
    row1 = swap_rows(row1, 1)
    row0 = swap_rows(row0, 0)
    depth0, depth1 = pl.pallas_call(
        functools.partial(pack_depth_kernel, layers=layers, rows=rows, spans=spans),
        out_shape=(local(*depth_shape), local(*depth_shape)),
        in_specs=[vmem] * 2,
        out_specs=(vmem,) * 2,
        name="pack_depth",
        compiler_params=params(8),
    )(in_vmem(block), in_vmem(row0))
    depth0, depth1 = swap_depths(depth0, 0), swap_depths(depth1, 1)
    corner0, corner1 = swap_corners(corner0, 1, 0), swap_corners(corner1, 1, 1)

    early, share, edge, late, part = pl.pallas_call(
        functools.partial(
            interior_kernel, layers=layers, rows=rows, columns=columns, depth_count=depth_count
        ),
        grid=(layers // 4,),
        out_shape=(
            pltpu.VMEM((layers, 4, spans * rows, LANES), f32),
            pltpu.VMEM((layers, spans * rows, LANES), f32),
            local(layers, 2, 4, spans, LANES), local(layers, 4, spans * rows, LANES),
            local(4, spans * rows, LANES),
        ),
        in_specs=[smem, vmem],
        out_specs=(vmem,) * 5,
        scratch_shapes=[pltpu.VMEM((4, 4, spans * PITCH, LANES), f32)],
        cost_estimate=pl.CostEstimate(
            flops=80 * layers * rows * columns, bytes_accessed=16 * layers * rows * columns,
            transcendentals=layers * rows * columns,
        ),
        name="interior",
        compiler_params=pltpu.CompilerParams(vmem_limit_bytes=24 << 20),
    )(palette, in_vmem(block))

    rowbuf_shape = (2, 4, layers + 2, 2, spans, LANES)
    srow_shape = (layers, 4, 4, spans, LANES)
    rowbuf, srow, lines, rows_part = pl.pallas_call(
        functools.partial(
            outer_kernel, layers=layers, rows=rows, columns=columns,
            depth_count=depth_count, row_count=row_count,
        ),
        out_shape=(
            local(*rowbuf_shape), local(*srow_shape), local(*srow_shape),
            local(4, 4 * spans, LANES),
        ),
        in_specs=[smem] + [vmem] * 5,
        out_specs=(vmem,) * 4,
        cost_estimate=pl.CostEstimate(
            flops=40 * layers * rows * columns, bytes_accessed=4 * layers * rows * columns,
            transcendentals=layers * rows * columns,
        ),
        name="outer",
        compiler_params=params(16),
    )(palette, *(in_vmem(x) for x in (row0, row1, early, share, edge)))

    whole, unused, unused, *parts = pl.pallas_call(
        functools.partial(
            settle_kernel, layers=layers, rows=rows, columns=columns,
            depth_count=depth_count, row_count=row_count,
        ),
        out_shape=(local(4, 4, spans * rows, LANES), local(*rowbuf_shape), local(*srow_shape))
        + (local(rows, line),) * depth_count,
        in_specs=[smem] + [vmem] * 12,
        out_specs=(vmem,) * (3 + depth_count),
        input_output_aliases={11: 1, 12: 2},
        scratch_shapes=[
            pltpu.VMEM((3, 4, spans * PITCH, LANES), f32),
            pltpu.VMEM((4, 4, spans * PITCH, LANES), f32),
            pltpu.VMEM((4, spans * rows, LANES), f32),
        ],
        name="settle",
        compiler_params=params(24),
    )(
        palette,
        *(
            in_vmem(x)
            for x in (
                block, depth0, depth1, corner0, corner1, early, share, edge, part, rows_part,
                rowbuf, srow,
            )
        ),
    )

    settled, moving = pl.pallas_call(
        functools.partial(assemble_kernel, layers=layers, rows=rows, columns=columns),
        grid=(layers // 4,),
        out_shape=(shape(layers, rows, columns), shape(3, layers, rows, columns)),
        in_specs=[vmem] * 3,
        out_specs=(
            pl.BlockSpec((4, rows, columns), lambda i: (i, 0, 0)),
            pl.BlockSpec((3, 4, rows, columns), lambda i: (0, i, 0, 0)),
        ),
        cost_estimate=pl.CostEstimate(
            flops=20 * layers * rows * columns, bytes_accessed=16 * layers * rows * columns,
            transcendentals=0,
        ),
        name="assemble",
        compiler_params=params(16),
    )(in_vmem(whole), in_vmem(lines), in_vmem(late))

    for k in range(1, depth_count):
        parts[k] = lax.ppermute(parts[k], "depth", [(i, i ^ k) for i in range(depth_count)])
    composed, swap0, swap1 = pl.pallas_call(
        functools.partial(over_kernel, count=depth_count, width=width),
        out_shape=(shape(rows, line), shape(2, line), shape(2, line)),
        in_specs=[vmem] * depth_count,
        out_specs=(vmem, vmem, vmem),
        name="over",
        compiler_params=pltpu.CompilerParams(vmem_limit_bytes=8 << 20),
    )(parts[0], *(in_vmem(parts[k]) for k in transfer_order(depth_count)[1:]))

    swap1, swap0 = swap_rows(swap1, 1), swap_rows(swap0, 0)
    filtered = pl.pallas_call(
        functools.partial(
            filter_kernel, width=width, row_count=row_count, depth_count=depth_count
        ),
        out_shape=shape(4, rows, width),
        in_specs=[vmem] * 3,
        out_specs=vmem,
        name="bilateral",
        compiler_params=pltpu.CompilerParams(vmem_limit_bytes=8 << 20),
    )(composed, in_vmem(swap0), in_vmem(swap1))
    return (filtered, settled, moving)


def solution(mesh):
    in_specs = (P("depth", "row", None), P(None, "depth", "row", None), P())
    out_specs = (P(None, "row", "depth"), P("depth", "row", None), P(None, "depth", "row", None))
    return jax.shard_map(compute, mesh=mesh, in_specs=in_specs, out_specs=out_specs, check_vma=False)
```

```python
import functools
import math

import jax
import jax.numpy as jnp
from jax import lax
from jax.experimental import pallas as pl
from jax.experimental.pallas import tpu as pltpu
from jax.sharding import PartitionSpec as P


DIFFUSION = 0.1
ADVECTION = 0.25
VISCOSITY = 0.15
FRICTION = 0.2
OPTICAL = 2.0
RANGE_SCALE = 0.1
SPACE_SCALE = 1.5
SUB = 8
LANES = 128
PITCH = 40


def row_pairs(kind, count):
    pairs = []
    for low in range(kind, count - 1, 2):
        pairs += [(low, low + 1), (low + 1, low)]
    return pairs


def swap_rows(array, kind):
    return lax.ppermute(array, "row", row_pairs(kind, lax.axis_size("row")))


def swap_depths(array, kind):
    return lax.ppermute(array, "depth", row_pairs(kind, lax.axis_size("depth")))


def in_vmem(array):
    return pltpu.with_memory_space_constraint(array, pltpu.VMEM)


def pack_kernel(
    den_ref, vel_ref, block, row0_ref, row1_ref, corner_ref, sides, load_sem,
    *, layers, rows, spans, chunks,
):
    row_odd = lax.rem(lax.axis_index("row"), 2)
    size = layers // chunks

    def loads(k):
        z = slice(k * size, (k + 1) * size)
        return (
            pltpu.make_async_copy(den_ref.at[z], block.at[0, z], load_sem.at[k, 0]),
            pltpu.make_async_copy(vel_ref.at[:, z], block.at[1:4, z], load_sem.at[k, 1]),
        )

    for k in range(chunks):
        for copy in loads(k):
            copy.start()
    for k in range(chunks):
        for copy in loads(k):
            copy.wait()
        for c in range(4):
            for z in range(k * size, (k + 1) * size):
                for side in range(2):
                    for n in range(2):
                        row = n + side * (rows - 2)
                        for j in range(spans):
                            sides[side, c, z, n, j : j + 1, :] = block[
                                c, z, row : row + 1, j * LANES : (j + 1) * LANES
                            ]
        for c in range(4):
            for z in range(k * size, (k + 1) * size):
                for n in range(2):
                    row0_ref[c, z, n] = sides[1 - row_odd, c, z, n]
                    row1_ref[c, z, n] = sides[row_odd, c, z, n]
    for n in range(2):
        for c in range(4):
            corner_ref[n, c] = row1_ref[c, n * (layers - 1), row_odd]


def pack_depth_kernel(block, row0_ref, corner_ref, depth0_ref, depth1_ref, *, layers, rows, spans):
    row_odd = lax.rem(lax.axis_index("row"), 2)
    depth_odd = lax.rem(lax.axis_index("depth"), 2)
    for target, side in ((depth0_ref, 1 - depth_odd), (depth1_ref, depth_odd)):
        for c in range(4):
            for n in range(2):
                z = side * (layers - 2) + n
                for j in range(spans):
                    target[c, pl.ds((n * spans + j) * rows, rows), :] = block[
                        c, z, :, j * LANES : (j + 1) * LANES
                    ]
            target[c, pl.ds(2 * spans * rows, spans), :] = row0_ref[
                c, side * (layers - 1), row_odd
            ]
            target[c, pl.ds((2 * rows + 1) * spans, spans), :] = corner_ref[side, c]


def row_of(j, row):
    return PITCH * j + SUB + row


def advance(here, up, down, left, right, front, back):
    around = [
        ((front[c] + back[c]) + (up[c] + down[c])) + (left[c] + right[c]) for c in range(4)
    ]
    flux = (
        (right[0] * right[1] - left[0] * left[1])
        + (down[0] * down[2] - up[0] * up[2])
        + (back[0] * back[3] - front[0] * front[3])
    )
    squared = here[0] * here[0]
    new = [
        (1.0 - 6.0 * DIFFUSION) * here[0] + (DIFFUSION * around[0] - (0.5 * ADVECTION) * flux)
    ]
    inverse = 1.0 / ((1.0 + squared) * (1.0 + FRICTION * squared))
    own_share = (1.0 + (1.0 - 6.0 * VISCOSITY) * squared) * inverse
    near_share = (VISCOSITY * squared) * inverse
    for c in range(1, 4):
        new.append(here[c] * own_share + around[c] * near_share)
    return new, near_share


def late_share(value, neighbour, near_share, along, sign):
    out = [
        value[0]
        + neighbour[0] * (DIFFUSION + (sign * 0.5 * ADVECTION) * neighbour[along])
    ]
    return out + [value[c] + near_share * neighbour[c] for c in range(1, 4)]


def neighbours(cells, slots, t, j, spans, first, last):
    oldest, middle, newest = slots
    row = t * SUB

    def at(which, r, jj=j):
        return [cells[which, c, pl.ds(row_of(jj, r), SUB), :] for c in range(4)]

    here = at(middle, row)
    zeros = [jnp.zeros((SUB, LANES), jnp.float32)] * 4
    before = at(middle, row, j - 1) if j > 0 else zeros
    after = at(middle, row, j + 1) if j < spans - 1 else zeros
    left = [pltpu.roll(jnp.where(last, b, x), 1, 1) for b, x in zip(before, here)]
    right = [pltpu.roll(jnp.where(first, a, x), LANES - 1, 1) for a, x in zip(after, here)]
    return (
        here, at(middle, row - 1), at(middle, row + 1), left, right,
        at(oldest, row), at(newest, row),
    )


def render(accum, pixels, cells, rate, mix):
    before = accum[3, pixels, :]
    passed = before * jnp.exp2(rate * (cells[0] * cells[0]))
    weight = before - passed
    accum[3, pixels, :] = passed
    for c in range(3):
        mixed = (mix[c][0] * cells[0] + mix[c][1] * cells[1]) + (
            mix[c][2] * cells[2] + mix[c][3] * cells[3]
        )
        accum[c, pixels, :] = accum[c, pixels, :] + weight * jnp.tanh(mixed)


def beside_in_lines(lines, sub, first, last):
    left, right = [], []
    for value in lines:
        before = jnp.where(sub == 0, 0.0, pltpu.roll(value, 1, 0))
        after = jnp.where(sub == SUB - 1, 0.0, pltpu.roll(value, SUB - 1, 0))
        left.append(pltpu.roll(jnp.where(last, before, value), 1, 1))
        right.append(pltpu.roll(jnp.where(first, after, value), LANES - 1, 1))
    return left, right


def constants(palette_ref, depth_total):
    rate = -OPTICAL / depth_total / math.log(2.0)
    return rate, [[0.5 * palette_ref[c, k] for k in range(4)] for c in range(3)]


def interior_kernel(
    palette_ref, block, early_ref, share_ref, edge_ref, late_ref, part_ref, base,
    *, layers, rows, columns, depth_count,
):
    step = pl.program_id(0)
    own_tiles, spans = rows // SUB, columns // LANES
    lane = lax.broadcasted_iota(jnp.int32, (SUB, LANES), 1)
    first, last = lane == 0, lane == LANES - 1

    @pl.when(step == 0)
    def _():
        line = jnp.zeros((spans, LANES), jnp.float32)
        for slot in range(4):
            for c in range(4):
                for row in (-1, rows):
                    base[slot, c, pl.ds(row_of(0, row), spans, stride=PITCH), :] = line
        base[3] = jnp.zeros((4, spans * PITCH, LANES), jnp.float32)
        base[2] = jnp.zeros((4, spans * PITCH, LANES), jnp.float32)
        for c in range(3):
            part_ref[c] = jnp.zeros((spans * rows, LANES), jnp.float32)
        part_ref[3] = jnp.ones((spans * rows, LANES), jnp.float32)

    def first_step(z, slots):
        for j in range(spans):
            for t in range(own_tiles):
                new, share = advance(*neighbours(base, slots, t, j, spans, first, last))
                cells = pl.ds(j * rows + t * SUB, SUB)
                share_ref[z, cells, :] = share
                for c in range(4):
                    early_ref[z, c, cells, :] = new[c]

    for q in range(4):
        z = 4 * step + q
        for t in range(own_tiles):
            for j in range(spans):
                there = (slice(t * SUB, (t + 1) * SUB), slice(j * LANES, (j + 1) * LANES))
                for c in range(4):
                    base[q, c, pl.ds(row_of(j, t * SUB), SUB), :] = block[(c, z) + there]
        for side, row in ((0, 0), (1, rows - 1)):
            for c in range(4):
                edge_ref[z, side, c] = base[q, c, pl.ds(row_of(0, row), spans, stride=PITCH), :]
        first_step(jnp.maximum(z - 1, 0), ((q + 2) % 4, (q + 3) % 4, q))

    rate, mix = constants(palette_ref, layers * depth_count)

    def inner_neighbours(z, t, j):
        row = j * rows + t * SUB

        def at(layer, start):
            return [early_ref[layer, c, pl.ds(start, SUB), :] for c in range(4)]

        here = at(z, row)
        zeros = [jnp.zeros((SUB, LANES), jnp.float32)] * 4
        before = at(z, row - rows) if j > 0 else zeros
        after = at(z, row + rows) if j < spans - 1 else zeros
        if row > 0:
            up = at(z, row - 1)
        else:
            up = [pltpu.roll(x, 1, 0) for x in here]
        if row + SUB < spans * rows:
            down = at(z, row + 1)
        else:
            down = [pltpu.roll(x, SUB - 1, 0) for x in here]
        left = [pltpu.roll(jnp.where(last, b, x), 1, 1) for b, x in zip(before, here)]
        right = [pltpu.roll(jnp.where(first, a, x), LANES - 1, 1) for a, x in zip(after, here)]
        return here, up, down, left, right, at(z - 1, row), at(z + 1, row)

    @pl.when(step > 0)
    def _():
        for q in range(4):
            z = 4 * step + q - 2
            for j in range(spans):
                for t in range(own_tiles):
                    new, _ = advance(*inner_neighbours(z, t, j))
                    cells = pl.ds(j * rows + t * SUB, SUB)
                    for c in range(4):
                        late_ref[z, c, cells, :] = new[c]
                    render(part_ref, cells, new, rate, mix)

    @pl.when(step == layers // 4 - 1)
    def _():
        base[0] = jnp.zeros((4, spans * PITCH, LANES), jnp.float32)
        first_step(layers - 1, (2, 3, 0))


def edge_rows(z, rowbuf, early_ref, share_ref, edge_ref, srow, places, rows, spans):
    above, below, has_above, has_below = places
    sub = lax.broadcasted_iota(jnp.int32, (SUB, LANES), 0)
    lane = lax.broadcasted_iota(jnp.int32, (SUB, LANES), 1)
    first, last = lane == 0, lane == LANES - 1
    for side, kind, k, exists in ((0, above, 1, has_above), (1, below, 0, has_below)):
        own_cells = pl.ds(0 if side == 0 else rows - 1, spans, stride=rows)

        def halo(layer, n):
            return [rowbuf[kind, c, layer, n] for c in range(4)]

        here, farther = halo(z + 1, k), halo(z + 1, 1 - k)
        own = [edge_ref[z, side, c] for c in range(4)]
        new = late_share(
            [early_ref[z, c, own_cells, :] for c in range(4)], here,
            share_ref[z, own_cells, :], 2, 1.0 if side == 0 else -1.0,
        )
        for c in range(4):
            srow[z, 1 + side, c] = new[c]
        left, right = beside_in_lines(here, sub, first, last)
        up, down = (farther, own) if side == 0 else (own, farther)
        new, _ = advance(here, up, down, left, right, halo(z, k), halo(z + 2, k))
        inside = jnp.full((SUB, LANES), jnp.where(exists, 1, 0), jnp.int32) == 1
        for c in range(4):
            srow[z, 3 * side, c] = jnp.where(inside, new[c], 0.0)


def row_places(row_count):
    row_rank = lax.axis_index("row")
    row_odd = lax.rem(row_rank, 2)
    return 1 - row_odd, row_odd, row_rank > 0, row_rank < row_count - 1


def outer_kernel(
    palette_ref, row0_ref, row1_ref, early_ref, share_ref, edge_ref,
    rowbuf, srow, lines_ref, part_ref, *, layers, rows, columns, depth_count, row_count,
):
    spans = columns // LANES
    sub = lax.broadcasted_iota(jnp.int32, (SUB, LANES), 0)
    lane = lax.broadcasted_iota(jnp.int32, (SUB, LANES), 1)
    first, last = lane == 0, lane == LANES - 1
    places = row_places(row_count)
    rate, mix = constants(palette_ref, layers * depth_count)
    for kind, source in ((0, row0_ref), (1, row1_ref)):
        for c in range(4):
            for z in range(layers):
                for k in range(2):
                    rowbuf[kind, c, z + 1, k] = source[c, z, k]
    for c in range(3):
        part_ref[c] = jnp.zeros((4 * spans, LANES), jnp.float32)
    part_ref[3] = jnp.ones((4 * spans, LANES), jnp.float32)

    def outer_rows(z):
        def values(layer, row):
            n = {-1: 0, 0: 1, rows - 1: 2, rows: 3}.get(row)
            if n is not None:
                return [srow[layer, n, c] for c in range(4)]
            return [early_ref[layer, c, pl.ds(row, spans, stride=rows), :] for c in range(4)]

        for n, row in enumerate((0, 1, rows - 2, rows - 1)):
            here = values(z, row)
            left, right = beside_in_lines(here, sub, first, last)
            new, _ = advance(
                here, values(z, row - 1), values(z, row + 1), left, right,
                values(z - 1, row), values(z + 1, row),
            )
            render(part_ref, pl.ds(n * spans, spans), new, rate, mix)
            for c in range(4):
                lines_ref[z, n, c] = new[c]

    def edges(z):
        edge_rows(z, rowbuf, early_ref, share_ref, edge_ref, srow, places, rows, spans)

    @pl.loop(0, (layers - 2) // 2)
    def _(pair):
        edges(2 * pair + 1)
        edges(2 * pair + 2)

    @pl.loop(0, (layers - 4) // 2)
    def _(pair):
        outer_rows(2 * pair + 2)
        outer_rows(2 * pair + 3)


def settle_kernel(
    palette_ref, block, depth0_ref, depth1_ref,
    early_ref, share_ref, edge_ref, part_ref, rows_part_ref, given_rowbuf, given_srow,
    whole_ref, rowbuf, srow, *rest,
    layers, rows, columns, depth_count, row_count,
):
    pieces = rest[:depth_count]
    base, sbase, accum = rest[depth_count:]
    own_tiles, spans = rows // SUB, columns // LANES
    row_rank, depth_rank = lax.axis_index("row"), lax.axis_index("depth")
    row_odd, depth_odd = lax.rem(row_rank, 2), lax.rem(depth_rank, 2)
    above, below = 1 - row_odd, row_odd
    sub = lax.broadcasted_iota(jnp.int32, (SUB, LANES), 0)
    lane = lax.broadcasted_iota(jnp.int32, (SUB, LANES), 1)
    first, last = lane == 0, lane == LANES - 1
    from_front = jnp.full((SUB, LANES), depth_odd, jnp.int32) == 1
    tiles = [(t, j) for j in range(spans) for t in range(own_tiles)]
    rate, mix = constants(palette_ref, layers * depth_count)

    def tile_of(t, j):
        return slice(t * SUB, (t + 1) * SUB), slice(j * LANES, (j + 1) * LANES)

    def cells_of(t, j):
        return pl.ds(j * rows + t * SUB, SUB)

    def line(row):
        return pl.ds(row_of(0, row), spans, stride=PITCH)

    def outer_step(slot, front):
        kept = (depth_rank > 0) if front else (depth_rank < depth_count - 1)
        keep = jnp.full((SUB, LANES), jnp.where(kept, 1, 0), jnp.int32) == 1
        chosen = from_front if front else jnp.logical_not(from_front)
        far, near = (0, 1) if front else (1, 0)
        for t, j in tiles:
            there = tile_of(t, j)
            for c in range(4):
                for k, n in ((0, far), (1, near)):
                    cells = pl.ds((n * spans + j) * rows + t * SUB, SUB)
                    base[k, c, pl.ds(row_of(j, t * SUB), SUB), :] = jnp.where(
                        chosen, depth0_ref[c, cells, :], depth1_ref[c, cells, :]
                    )
                base[2, c, pl.ds(row_of(j, t * SUB), SUB), :] = block[
                    (c, 0 if front else layers - 1) + there
                ]
        z = 0 if front else layers + 1
        for c in range(4):
            base[1, c, line(-1), :] = rowbuf[above, c, z, 1]
            base[1, c, line(rows), :] = rowbuf[below, c, z, 0]
        slots = (0, 1, 2) if front else (2, 1, 0)
        for t, j in tiles:
            new, _ = advance(*neighbours(base, slots, t, j, spans, first, last))
            for c in range(4):
                sbase[slot, c, pl.ds(row_of(j, t * SUB), SUB), :] = jnp.where(keep, new[c], 0.0)

    def add_layer(z, slot, sign):
        for t, j in tiles:
            cells = pl.ds(row_of(j, t * SUB), SUB)
            new = late_share(
                [sbase[slot, c, cells, :] for c in range(4)],
                [base[1, c, cells, :] for c in range(4)],
                share_ref[z, cells_of(t, j), :], 3, sign,
            )
            for c in range(4):
                sbase[slot, c, cells, :] = new[c]

    def take_layer(z, slot):
        for t, j in tiles:
            for c in range(4):
                sbase[slot, c, pl.ds(row_of(j, t * SUB), SUB), :] = early_ref[z, c, cells_of(t, j), :]
        for n, row in enumerate((-1, 0, rows - 1, rows)):
            for c in range(4):
                sbase[slot, c, line(row), :] = srow[z, n, c]

    def whole_layer(n, slots):
        for t, j in tiles:
            new, _ = advance(*neighbours(sbase, slots, t, j, spans, first, last))
            for c in range(4):
                whole_ref[n, c, cells_of(t, j), :] = new[c]
            render(accum, cells_of(t, j), new, rate, mix)

    for row_kind, depth_kind in ((0, 0), (0, 1), (1, 0), (1, 1)):
        received = depth0_ref if depth_kind == 0 else depth1_ref
        beside = pl.ds((2 * rows + row_kind) * spans, spans)
        is_above = row_odd if row_kind == 0 else 1 - row_odd
        is_front = depth_odd if depth_kind == 0 else 1 - depth_odd
        for c in range(4):
            rowbuf[row_kind, c, (1 - is_front) * (layers + 1), is_above] = received[c, beside, :]
    for c in range(3):
        accum[c] = jnp.zeros((spans * rows, LANES), jnp.float32)
    accum[3] = jnp.ones((spans * rows, LANES), jnp.float32)

    for z in (0, layers - 1):
        edge_rows(
            z, rowbuf, early_ref, share_ref, edge_ref, srow, row_places(row_count), rows, spans
        )

    outer_step(3, True)
    take_layer(0, 0)
    add_layer(0, 0, 1.0)
    take_layer(1, 1)
    take_layer(2, 2)
    whole_layer(0, (3, 0, 1))
    whole_layer(1, (0, 1, 2))
    for t, j in tiles:
        pixels = cells_of(t, j)
        through = accum[3, pixels, :]
        inner = jnp.full((SUB, LANES), True)
        if t == 0:
            inner = sub >= 2
        if t == own_tiles - 1:
            inner = (sub < SUB - 2) if t > 0 else inner & (sub < SUB - 2)
        for c in range(3):
            value = accum[c, pixels, :]
            accum[c, pixels, :] = jnp.where(inner, value + through * part_ref[c, pixels, :], value)
        accum[3, pixels, :] = jnp.where(inner, through * part_ref[3, pixels, :], through)

    for n, row in enumerate((0, 1, rows - 2, rows - 1)):
        pixels, theirs = pl.ds(row, spans, stride=rows), pl.ds(n * spans, spans)
        through = accum[3, pixels, :]
        for c in range(3):
            accum[c, pixels, :] = accum[c, pixels, :] + through * rows_part_ref[c, theirs, :]
        accum[3, pixels, :] = through * rows_part_ref[3, theirs, :]

    take_layer(layers - 3, 0)
    take_layer(layers - 2, 1)
    take_layer(layers - 1, 2)
    outer_step(3, False)
    add_layer(layers - 1, 2, -1.0)
    whole_layer(2, (0, 1, 2))
    whole_layer(3, (1, 2, 3))

    width = columns // depth_count
    per_piece = width // LANES

    def channels(j, t):
        pixels = pl.ds(j * rows + t * SUB, SUB)
        through = accum[3, pixels, :]
        return [0.5 * (accum[c, pixels, :] + (1.0 - through)) for c in range(3)] + [through]

    for k in range(depth_count):
        piece = depth_rank ^ k
        start = piece * per_piece
        for t in range(own_tiles):
            r = slice(t * SUB, (t + 1) * SUB)
            for jj in range(per_piece):
                values = channels(start + jj, t)
                for c in range(4):
                    pieces[k][r, c * width + jj * LANES : c * width + (jj + 1) * LANES] = (
                        values[c]
                    )
            before = channels(jnp.maximum(start - 1, 0), t)
            after = channels(jnp.minimum(start + per_piece, spans - 1), t)
            edge = jnp.zeros((SUB, LANES), jnp.float32)
            for c in range(4):
                for values, low in ((before, 4 * c), (after, 4 * c + 2)):
                    turned = pltpu.roll(values[c], (4 * c + 2) % LANES, 1)
                    edge = jnp.where((lane >= low) & (lane < low + 2), turned, edge)
            pieces[k][r, 4 * width : 4 * width + LANES] = edge


def assemble_kernel(whole_ref, lines_ref, late_ref, den_out, vel_out, *, layers, rows, columns):
    step = pl.program_id(0)
    own_tiles, spans = rows // SUB, columns // LANES

    def put(q, c, there, value):
        if c == 0:
            den_out[(q,) + there] = value
        else:
            vel_out[(c - 1, q) + there] = value

    def copy_layer(source, z, q):
        for j in range(spans):
            lanes = slice(j * LANES, (j + 1) * LANES)
            for c in range(4):
                for t in range(own_tiles):
                    value = source[z, c, pl.ds(j * rows + t * SUB, SUB), :]
                    put(q, c, (slice(t * SUB, (t + 1) * SUB), lanes), value)

    def inner_layer(z, q):
        copy_layer(late_ref, z, q)
        for n, row in enumerate((0, 1, rows - 2, rows - 1)):
            for j in range(spans):
                for c in range(4):
                    there = (slice(row, row + 1), slice(j * LANES, (j + 1) * LANES))
                    put(q, c, there, lines_ref[z, n, c, j : j + 1, :])

    for q in range(4):
        if q < 2:

            @pl.when(step == 0)
            def _():
                copy_layer(whole_ref, q, q)

            pl.when(step > 0)(functools.partial(inner_layer, 4 * step + q, q))
        else:

            @pl.when(step == layers // 4 - 1)
            def _():
                copy_layer(whole_ref, q, q)

            pl.when(step < layers // 4 - 1)(functools.partial(inner_layer, 4 * step + q, q))


def transfer_order(count):
    return sorted(range(count), key=lambda k: (k != 0, k % 2, k)) if count > 2 else list(range(count))


def over_kernel(*refs, count, width):
    parts = [refs[transfer_order(count).index(k)] for k in range(count)]
    picture_ref, swap0_ref, swap1_ref = refs[count:]
    rows = picture_ref.shape[0]
    depth_rank = lax.axis_index("depth")
    row_odd = lax.rem(lax.axis_index("row"), 2)
    lane = lax.broadcasted_iota(jnp.int32, (rows, LANES), 1)

    def split(ref):
        return [ref[:, c * width : (c + 1) * width] for c in range(4)] + [
            ref[:, 4 * width : 4 * width + LANES]
        ]

    def spread_through(edge):
        out = jnp.ones_like(edge)
        for c in range(3):
            turned = pltpu.roll(edge, LANES - 12 + 4 * c, 1)
            out = jnp.where((lane >= 4 * c) & (lane < 4 * c + 4), turned, out)
        return out

    def over(swapped, a, b):
        near = [jnp.where(swapped, y, x) for x, y in zip(a, b)]
        far = [jnp.where(swapped, x, y) for x, y in zip(a, b)]
        out = [near[c] + near[3] * far[c] for c in range(3)]
        out.append(near[3] * far[3])
        edge = near[4] + spread_through(near[4]) * far[4]
        out.append(jnp.where(lane >= 12, near[4] * far[4], edge))
        return out

    values = [split(ref) for ref in parts]
    bit = 0
    while len(values) > 1:
        swapped = (depth_rank >> bit & 1) == 1
        values = [over(swapped, values[k], values[k + 1]) for k in range(0, len(values), 2)]
        bit += 1
    final = values[0]
    for c in range(4):
        picture_ref[:, c * width : (c + 1) * width] = (1.0 - final[3]) if c == 3 else final[c]
    edge = jnp.where((lane >= 12) & (lane < 16), 1.0 - final[4], final[4])
    picture_ref[:, 4 * width : 4 * width + LANES] = edge
    top, bottom = picture_ref[0:2, :], picture_ref[rows - 2 : rows, :]
    odd = row_odd == 1
    swap0_ref[...] = jnp.where(odd, top, bottom)
    swap1_ref[...] = jnp.where(odd, bottom, top)


def filter_kernel(picture_ref, swap0_ref, swap1_ref, out_ref, *, width, row_count, depth_count):
    row_rank, depth_rank = lax.axis_index("row"), lax.axis_index("depth")
    odd = lax.rem(row_rank, 2) == 1
    rows = picture_ref.shape[0]
    own_tiles = rows // SUB
    spans = width // LANES
    lane = lax.broadcasted_iota(jnp.int32, (SUB, LANES), 1)
    sub = lax.broadcasted_iota(jnp.int32, (SUB, LANES), 0)

    def tile(t, c, j):
        if j == -1 or j == spans:
            cols = slice(4 * width, 4 * width + LANES)
        else:
            cols = slice(c * width + j * LANES, c * width + (j + 1) * LANES)
        if t == -1:
            v = jnp.where(odd, swap0_ref[:, cols], swap1_ref[:, cols])
            v = jnp.concatenate([jnp.zeros((SUB - 2, LANES), jnp.float32), v], 0)
        elif t == own_tiles:
            v = jnp.where(odd, swap1_ref[:, cols], swap0_ref[:, cols])
            v = jnp.concatenate([v, jnp.zeros((SUB - 2, LANES), jnp.float32)], 0)
        else:
            v = picture_ref[t * SUB : (t + 1) * SUB, cols]
        if j == -1:
            v = pltpu.roll(v, LANES - 2 - 4 * c, 1)
        elif j == spans:
            v = pltpu.roll(v, (LANES - 2 - 4 * c) % LANES, 1)
        return v

    tiles = {}
    for t in range(-1, own_tiles + 1):
        for j in range(-1, spans + 1):
            four = [tile(t, c, j) for c in range(4)]
            tiles[t, j] = four + [(four[0] + four[1] + four[2]) / 3.0]

    def column_shift(t, j, q, dx):
        if dx == 0:
            return tiles[t, j][q]
        if dx > 0:
            mixed = jnp.where(lane < dx, tiles[t, j + 1][q], tiles[t, j][q])
        else:
            mixed = jnp.where(lane >= LANES + dx, tiles[t, j - 1][q], tiles[t, j][q])
        return pltpu.roll(mixed, (-dx) % LANES, 1)

    no_above, no_below = row_rank == 0, row_rank == row_count - 1
    no_west, no_east = depth_rank == 0, depth_rank == depth_count - 1
    for j in range(spans):
        sums = [[None] * 5 for _ in range(own_tiles)]
        for dx in range(-2, 3):
            shifted = {
                t: [column_shift(t, j, q, dx) for q in range(5)] for t in range(-1, own_tiles + 1)
            }
            for dy in range(-2, 3):
                spatial = -(dx * dx + dy * dy) / (2.0 * SPACE_SCALE * SPACE_SCALE)
                for t in range(own_tiles):
                    if dy == 0:
                        near = shifted[t]
                    elif dy > 0:
                        near = [
                            pltpu.roll(
                                jnp.where(sub < dy, shifted[t + 1][q], shifted[t][q]), SUB - dy, 0
                            )
                            for q in range(5)
                        ]
                    else:
                        near = [
                            pltpu.roll(
                                jnp.where(sub >= SUB + dy, shifted[t - 1][q], shifted[t][q]), -dy, 0
                            )
                            for q in range(5)
                        ]
                    diff = near[4] - tiles[t, j][4]
                    weight = jnp.exp(
                        spatial - diff * diff * (1.0 / (2.0 * RANGE_SCALE * RANGE_SCALE))
                    )
                    blocked = None
                    if t == 0 and dy < 0:
                        blocked = no_above & (sub < -dy)
                    if t == own_tiles - 1 and dy > 0:
                        blocked = no_below & (sub >= SUB - dy)
                    if j == 0 and dx < 0:
                        side = no_west & (lane < -dx)
                        blocked = side if blocked is None else blocked | side
                    if j == spans - 1 and dx > 0:
                        side = no_east & (lane >= LANES - dx)
                        blocked = side if blocked is None else blocked | side
                    if blocked is not None:
                        weight = jnp.where(blocked, 0.0, weight)
                    terms = [weight * near[c] for c in range(4)] + [weight]
                    sums[t] = terms if sums[t][0] is None else [a + b for a, b in zip(sums[t], terms)]
        for t in range(own_tiles):
            inverse = 1.0 / sums[t][4]
            for c in range(4):
                out_ref[c, t * SUB : (t + 1) * SUB, j * LANES : (j + 1) * LANES] = (
                    sums[t][c] * inverse
                )


def compute(density, velocity, palette):
    layers, rows, columns = density.shape
    depth_count, row_count = lax.axis_size("depth"), lax.axis_size("row")
    spans = columns // LANES
    width = columns // depth_count
    line = 4 * width + LANES
    assert spans == SUB and rows % SUB == 0 and width % LANES == 0 and layers % 4 == 0 and layers >= 8
    vmem = pl.BlockSpec(memory_space=pltpu.VMEM)
    smem = pl.BlockSpec(memory_space=pltpu.SMEM)
    f32 = jnp.float32

    def shape(*dims):
        return jax.ShapeDtypeStruct(dims, f32)

    def local(*dims):
        return pltpu.VMEM(dims, f32)

    def params(mebibytes):
        return pltpu.CompilerParams(vmem_limit_bytes=mebibytes << 20)

    row_shape = (4, layers, 2, spans, LANES)
    depth_shape = (4, (2 * rows + 2) * spans, LANES)
    corner_shape = (2, 4, spans, LANES)
    block, row0, row1, corner = pl.pallas_call(
        functools.partial(pack_kernel, layers=layers, rows=rows, spans=spans, chunks=4),
        out_shape=(
            local(4, layers, rows, columns), local(*row_shape), local(*row_shape),
            local(*corner_shape),
        ),
        in_specs=[pl.BlockSpec(memory_space=pltpu.HBM)] * 2,
        out_specs=(vmem,) * 4,
        scratch_shapes=[pltpu.VMEM((2,) + row_shape, f32), pltpu.SemaphoreType.DMA((4, 2))],
        name="pack",
        compiler_params=params(8),
    )(
        pltpu.with_memory_space_constraint(density, pltpu.HBM),
        pltpu.with_memory_space_constraint(velocity, pltpu.HBM),
    )
    corner = swap_rows(corner, 1)
    row1 = swap_rows(row1, 1)
    row0 = swap_rows(row0, 0)
    depth0, depth1 = pl.pallas_call(
        functools.partial(pack_depth_kernel, layers=layers, rows=rows, spans=spans),
        out_shape=(local(*depth_shape), local(*depth_shape)),
        in_specs=[vmem] * 3,
        out_specs=(vmem,) * 2,
        name="pack_depth",
        compiler_params=params(8),
    )(in_vmem(block), in_vmem(row0), in_vmem(corner))
    depth0, depth1 = swap_depths(depth0, 0), swap_depths(depth1, 1)

    early, share, edge, late, part = pl.pallas_call(
        functools.partial(
            interior_kernel, layers=layers, rows=rows, columns=columns, depth_count=depth_count
        ),
        grid=(layers // 4,),
        out_shape=(
            pltpu.VMEM((layers, 4, spans * rows, LANES), f32),
            pltpu.VMEM((layers, spans * rows, LANES), f32),
            local(layers, 2, 4, spans, LANES), local(layers, 4, spans * rows, LANES),
            local(4, spans * rows, LANES),
        ),
        in_specs=[smem, vmem],
        out_specs=(vmem,) * 5,
        scratch_shapes=[pltpu.VMEM((4, 4, spans * PITCH, LANES), f32)],
        cost_estimate=pl.CostEstimate(
            flops=80 * layers * rows * columns, bytes_accessed=16 * layers * rows * columns,
            transcendentals=layers * rows * columns,
        ),
        name="interior",
        compiler_params=pltpu.CompilerParams(vmem_limit_bytes=24 << 20),
    )(palette, in_vmem(block))

    rowbuf_shape = (2, 4, layers + 2, 2, spans, LANES)
    srow_shape = (layers, 4, 4, spans, LANES)
    rowbuf, srow, lines, rows_part = pl.pallas_call(
        functools.partial(
            outer_kernel, layers=layers, rows=rows, columns=columns,
            depth_count=depth_count, row_count=row_count,
        ),
        out_shape=(
            local(*rowbuf_shape), local(*srow_shape), local(*srow_shape),
            local(4, 4 * spans, LANES),
        ),
        in_specs=[smem] + [vmem] * 5,
        out_specs=(vmem,) * 4,
        cost_estimate=pl.CostEstimate(
            flops=40 * layers * rows * columns, bytes_accessed=4 * layers * rows * columns,
            transcendentals=layers * rows * columns,
        ),
        name="outer",
        compiler_params=params(16),
    )(palette, *(in_vmem(x) for x in (row0, row1, early, share, edge)))

    whole, unused, unused, *parts = pl.pallas_call(
        functools.partial(
            settle_kernel, layers=layers, rows=rows, columns=columns,
            depth_count=depth_count, row_count=row_count,
        ),
        out_shape=(local(4, 4, spans * rows, LANES), local(*rowbuf_shape), local(*srow_shape))
        + (local(rows, line),) * depth_count,
        in_specs=[smem] + [vmem] * 10,
        out_specs=(vmem,) * (3 + depth_count),
        input_output_aliases={9: 1, 10: 2},
        scratch_shapes=[
            pltpu.VMEM((3, 4, spans * PITCH, LANES), f32),
            pltpu.VMEM((4, 4, spans * PITCH, LANES), f32),
            pltpu.VMEM((4, spans * rows, LANES), f32),
        ],
        name="settle",
        compiler_params=params(24),
    )(
        palette,
        *(
            in_vmem(x)
            for x in (
                block, depth0, depth1, early, share, edge, part, rows_part,
                rowbuf, srow,
            )
        ),
    )

    settled, moving = pl.pallas_call(
        functools.partial(assemble_kernel, layers=layers, rows=rows, columns=columns),
        grid=(layers // 4,),
        out_shape=(shape(layers, rows, columns), shape(3, layers, rows, columns)),
        in_specs=[vmem] * 3,
        out_specs=(
            pl.BlockSpec((4, rows, columns), lambda i: (i, 0, 0)),
            pl.BlockSpec((3, 4, rows, columns), lambda i: (0, i, 0, 0)),
        ),
        cost_estimate=pl.CostEstimate(
            flops=20 * layers * rows * columns, bytes_accessed=16 * layers * rows * columns,
            transcendentals=0,
        ),
        name="assemble",
        compiler_params=params(16),
    )(in_vmem(whole), in_vmem(lines), in_vmem(late))

    for k in range(1, depth_count):
        parts[k] = lax.ppermute(parts[k], "depth", [(i, i ^ k) for i in range(depth_count)])
    composed, swap0, swap1 = pl.pallas_call(
        functools.partial(over_kernel, count=depth_count, width=width),
        out_shape=(shape(rows, line), shape(2, line), shape(2, line)),
        in_specs=[vmem] * depth_count,
        out_specs=(vmem, vmem, vmem),
        name="over",
        compiler_params=pltpu.CompilerParams(vmem_limit_bytes=8 << 20),
    )(parts[0], *(in_vmem(parts[k]) for k in transfer_order(depth_count)[1:]))

    swap1, swap0 = swap_rows(swap1, 1), swap_rows(swap0, 0)
    filtered = pl.pallas_call(
        functools.partial(
            filter_kernel, width=width, row_count=row_count, depth_count=depth_count
        ),
        out_shape=shape(4, rows, width),
        in_specs=[vmem] * 3,
        out_specs=vmem,
        name="bilateral",
        compiler_params=pltpu.CompilerParams(vmem_limit_bytes=8 << 20),
    )(composed, in_vmem(swap0), in_vmem(swap1))
    return (filtered, settled, moving)


def solution(mesh):
    in_specs = (P("depth", "row", None), P(None, "depth", "row", None), P())
    out_specs = (P(None, "row", "depth"), P("depth", "row", None), P(None, "depth", "row", None))
    return jax.shard_map(compute, mesh=mesh, in_specs=in_specs, out_specs=out_specs, check_vma=False)
```

```python
import functools
import math

import jax
import jax.numpy as jnp
from jax import lax
from jax.experimental import pallas as pl
from jax.experimental.pallas import tpu as pltpu
from jax.sharding import PartitionSpec as P


DIFFUSION = 0.1
ADVECTION = 0.25
VISCOSITY = 0.15
FRICTION = 0.2
OPTICAL = 2.0
RANGE_SCALE = 0.1
SPACE_SCALE = 1.5
SUB = 8
LANES = 128
PITCH = 40
AXES = ("row", "depth")


def row_pairs(kind, count):
    pairs = []
    for low in range(kind, count - 1, 2):
        pairs += [(low, low + 1), (low + 1, low)]
    return pairs


def swap_rows(array, kind):
    return lax.ppermute(array, "row", row_pairs(kind, lax.axis_size("row")))


def swap_depths(array, kind):
    return lax.ppermute(array, "depth", row_pairs(kind, lax.axis_size("depth")))


def swap_corners(array, row_kind, depth_kind):
    depths = lax.axis_size("depth")
    pairs = [
        (a * depths + c, b * depths + d)
        for a, b in row_pairs(row_kind, lax.axis_size("row"))
        for c, d in row_pairs(depth_kind, depths)
    ]
    return lax.ppermute(array, AXES, pairs)


def in_vmem(array):
    return pltpu.with_memory_space_constraint(array, pltpu.VMEM)


def pack_kernel(
    den_ref, vel_ref, block, row0_ref, row1_ref, c10_ref, c11_ref, sides, load_sem,
    *, layers, rows, spans, chunks,
):
    row_odd = lax.rem(lax.axis_index("row"), 2)
    depth_odd = lax.rem(lax.axis_index("depth"), 2)
    size = layers // chunks

    def loads(k):
        z = slice(k * size, (k + 1) * size)
        return (
            pltpu.make_async_copy(den_ref.at[z], block.at[0, z], load_sem.at[k, 0]),
            pltpu.make_async_copy(vel_ref.at[:, z], block.at[1:4, z], load_sem.at[k, 1]),
        )

    for k in range(chunks):
        for copy in loads(k):
            copy.start()
    for k in range(chunks):
        for copy in loads(k):
            copy.wait()
        for c in range(4):
            for z in range(k * size, (k + 1) * size):
                for side in range(2):
                    for n in range(2):
                        row = n + side * (rows - 2)
                        for j in range(spans):
                            sides[side, c, z, n, j : j + 1, :] = block[
                                c, z, row : row + 1, j * LANES : (j + 1) * LANES
                            ]
        for c in range(4):
            for z in range(k * size, (k + 1) * size):
                for n in range(2):
                    row0_ref[c, z, n] = sides[1 - row_odd, c, z, n]
                    row1_ref[c, z, n] = sides[row_odd, c, z, n]
    for target, side in ((c10_ref, 1 - depth_odd), (c11_ref, depth_odd)):
        for c in range(4):
            target[c] = row1_ref[c, side * (layers - 1), row_odd]


def pack_depth_kernel(block, row0_ref, depth0_ref, depth1_ref, *, layers, rows, spans):
    row_odd = lax.rem(lax.axis_index("row"), 2)
    depth_odd = lax.rem(lax.axis_index("depth"), 2)
    for target, side in ((depth0_ref, 1 - depth_odd), (depth1_ref, depth_odd)):
        for c in range(4):
            for n in range(2):
                z = side * (layers - 2) + n
                for j in range(spans):
                    target[c, pl.ds((n * spans + j) * rows, rows), :] = block[
                        c, z, :, j * LANES : (j + 1) * LANES
                    ]
            target[c, pl.ds(2 * spans * rows, spans), :] = row0_ref[
                c, side * (layers - 1), row_odd
            ]


def row_of(j, row):
    return PITCH * j + SUB + row


def advance(here, up, down, left, right, front, back):
    around = [
        ((front[c] + back[c]) + (up[c] + down[c])) + (left[c] + right[c]) for c in range(4)
    ]
    flux = (
        (right[0] * right[1] - left[0] * left[1])
        + (down[0] * down[2] - up[0] * up[2])
        + (back[0] * back[3] - front[0] * front[3])
    )
    squared = here[0] * here[0]
    new = [
        (1.0 - 6.0 * DIFFUSION) * here[0] + (DIFFUSION * around[0] - (0.5 * ADVECTION) * flux)
    ]
    inverse = 1.0 / ((1.0 + squared) * (1.0 + FRICTION * squared))
    own_share = (1.0 + (1.0 - 6.0 * VISCOSITY) * squared) * inverse
    near_share = (VISCOSITY * squared) * inverse
    for c in range(1, 4):
        new.append(here[c] * own_share + around[c] * near_share)
    return new, near_share


def late_share(value, neighbour, near_share, along, sign):
    out = [
        value[0]
        + neighbour[0] * (DIFFUSION + (sign * 0.5 * ADVECTION) * neighbour[along])
    ]
    return out + [value[c] + near_share * neighbour[c] for c in range(1, 4)]


def neighbours(cells, slots, t, j, spans, first, last):
    oldest, middle, newest = slots
    row = t * SUB

    def at(which, r, jj=j):
        return [cells[which, c, pl.ds(row_of(jj, r), SUB), :] for c in range(4)]

    here = at(middle, row)
    zeros = [jnp.zeros((SUB, LANES), jnp.float32)] * 4
    before = at(middle, row, j - 1) if j > 0 else zeros
    after = at(middle, row, j + 1) if j < spans - 1 else zeros
    left = [pltpu.roll(jnp.where(last, b, x), 1, 1) for b, x in zip(before, here)]
    right = [pltpu.roll(jnp.where(first, a, x), LANES - 1, 1) for a, x in zip(after, here)]
    return (
        here, at(middle, row - 1), at(middle, row + 1), left, right,
        at(oldest, row), at(newest, row),
    )


def render(accum, pixels, cells, rate, mix):
    before = accum[3, pixels, :]
    passed = before * jnp.exp2(rate * (cells[0] * cells[0]))
    weight = before - passed
    accum[3, pixels, :] = passed
    for c in range(3):
        mixed = (mix[c][0] * cells[0] + mix[c][1] * cells[1]) + (
            mix[c][2] * cells[2] + mix[c][3] * cells[3]
        )
        accum[c, pixels, :] = accum[c, pixels, :] + weight * jnp.tanh(mixed)


def beside_in_lines(lines, sub, first, last):
    left, right = [], []
    for value in lines:
        before = jnp.where(sub == 0, 0.0, pltpu.roll(value, 1, 0))
        after = jnp.where(sub == SUB - 1, 0.0, pltpu.roll(value, SUB - 1, 0))
        left.append(pltpu.roll(jnp.where(last, before, value), 1, 1))
        right.append(pltpu.roll(jnp.where(first, after, value), LANES - 1, 1))
    return left, right


def constants(palette_ref, depth_total):
    rate = -OPTICAL / depth_total / math.log(2.0)
    return rate, [[0.5 * palette_ref[c, k] for k in range(4)] for c in range(3)]


def interior_kernel(
    palette_ref, block, early_ref, share_ref, edge_ref, late_ref, part_ref, base,
    *, layers, rows, columns, depth_count,
):
    step = pl.program_id(0)
    own_tiles, spans = rows // SUB, columns // LANES
    lane = lax.broadcasted_iota(jnp.int32, (SUB, LANES), 1)
    first, last = lane == 0, lane == LANES - 1

    @pl.when(step == 0)
    def _():
        line = jnp.zeros((spans, LANES), jnp.float32)
        for slot in range(4):
            for c in range(4):
                for row in (-1, rows):
                    base[slot, c, pl.ds(row_of(0, row), spans, stride=PITCH), :] = line
        base[3] = jnp.zeros((4, spans * PITCH, LANES), jnp.float32)
        base[2] = jnp.zeros((4, spans * PITCH, LANES), jnp.float32)
        for c in range(3):
            part_ref[c] = jnp.zeros((spans * rows, LANES), jnp.float32)
        part_ref[3] = jnp.ones((spans * rows, LANES), jnp.float32)

    def first_step(z, slots):
        for j in range(spans):
            for t in range(own_tiles):
                new, share = advance(*neighbours(base, slots, t, j, spans, first, last))
                cells = pl.ds(j * rows + t * SUB, SUB)
                share_ref[z, cells, :] = share
                for c in range(4):
                    early_ref[z, c, cells, :] = new[c]

    for q in range(4):
        z = 4 * step + q
        for t in range(own_tiles):
            for j in range(spans):
                there = (slice(t * SUB, (t + 1) * SUB), slice(j * LANES, (j + 1) * LANES))
                for c in range(4):
                    base[q, c, pl.ds(row_of(j, t * SUB), SUB), :] = block[(c, z) + there]
        for side, row in ((0, 0), (1, rows - 1)):
            for c in range(4):
                edge_ref[z, side, c] = base[q, c, pl.ds(row_of(0, row), spans, stride=PITCH), :]
        first_step(jnp.maximum(z - 1, 0), ((q + 2) % 4, (q + 3) % 4, q))

    rate, mix = constants(palette_ref, layers * depth_count)

    def inner_neighbours(z, t, j):
        row = j * rows + t * SUB

        def at(layer, start):
            return [early_ref[layer, c, pl.ds(start, SUB), :] for c in range(4)]

        here = at(z, row)
        zeros = [jnp.zeros((SUB, LANES), jnp.float32)] * 4
        before = at(z, row - rows) if j > 0 else zeros
        after = at(z, row + rows) if j < spans - 1 else zeros
        if row > 0:
            up = at(z, row - 1)
        else:
            up = [pltpu.roll(x, 1, 0) for x in here]
        if row + SUB < spans * rows:
            down = at(z, row + 1)
        else:
            down = [pltpu.roll(x, SUB - 1, 0) for x in here]
        left = [pltpu.roll(jnp.where(last, b, x), 1, 1) for b, x in zip(before, here)]
        right = [pltpu.roll(jnp.where(first, a, x), LANES - 1, 1) for a, x in zip(after, here)]
        return here, up, down, left, right, at(z - 1, row), at(z + 1, row)

    @pl.when(step > 0)
    def _():
        for q in range(4):
            z = 4 * step + q - 2
            for j in range(spans):
                for t in range(own_tiles):
                    new, _ = advance(*inner_neighbours(z, t, j))
                    cells = pl.ds(j * rows + t * SUB, SUB)
                    for c in range(4):
                        late_ref[z, c, cells, :] = new[c]
                    render(part_ref, cells, new, rate, mix)

    @pl.when(step == layers // 4 - 1)
    def _():
        base[0] = jnp.zeros((4, spans * PITCH, LANES), jnp.float32)
        first_step(layers - 1, (2, 3, 0))


def edge_rows(z, rowbuf, early_ref, share_ref, edge_ref, srow, places, rows, spans):
    above, below, has_above, has_below = places
    sub = lax.broadcasted_iota(jnp.int32, (SUB, LANES), 0)
    lane = lax.broadcasted_iota(jnp.int32, (SUB, LANES), 1)
    first, last = lane == 0, lane == LANES - 1
    for side, kind, k, exists in ((0, above, 1, has_above), (1, below, 0, has_below)):
        own_cells = pl.ds(0 if side == 0 else rows - 1, spans, stride=rows)

        def halo(layer, n):
            return [rowbuf[kind, c, layer, n] for c in range(4)]

        here, farther = halo(z + 1, k), halo(z + 1, 1 - k)
        own = [edge_ref[z, side, c] for c in range(4)]
        new = late_share(
            [early_ref[z, c, own_cells, :] for c in range(4)], here,
            share_ref[z, own_cells, :], 2, 1.0 if side == 0 else -1.0,
        )
        for c in range(4):
            srow[z, 1 + side, c] = new[c]
        left, right = beside_in_lines(here, sub, first, last)
        up, down = (farther, own) if side == 0 else (own, farther)
        new, _ = advance(here, up, down, left, right, halo(z, k), halo(z + 2, k))
        inside = jnp.full((SUB, LANES), jnp.where(exists, 1, 0), jnp.int32) == 1
        for c in range(4):
            srow[z, 3 * side, c] = jnp.where(inside, new[c], 0.0)


def row_places(row_count):
    row_rank = lax.axis_index("row")
    row_odd = lax.rem(row_rank, 2)
    return 1 - row_odd, row_odd, row_rank > 0, row_rank < row_count - 1


def outer_kernel(
    palette_ref, row0_ref, row1_ref, early_ref, share_ref, edge_ref,
    rowbuf, srow, lines_ref, part_ref, *, layers, rows, columns, depth_count, row_count,
):
    spans = columns // LANES
    sub = lax.broadcasted_iota(jnp.int32, (SUB, LANES), 0)
    lane = lax.broadcasted_iota(jnp.int32, (SUB, LANES), 1)
    first, last = lane == 0, lane == LANES - 1
    places = row_places(row_count)
    rate, mix = constants(palette_ref, layers * depth_count)
    for kind, source in ((0, row0_ref), (1, row1_ref)):
        for c in range(4):
            for z in range(layers):
                for k in range(2):
                    rowbuf[kind, c, z + 1, k] = source[c, z, k]
    for c in range(3):
        part_ref[c] = jnp.zeros((4 * spans, LANES), jnp.float32)
    part_ref[3] = jnp.ones((4 * spans, LANES), jnp.float32)

    def outer_rows(z):
        def values(layer, row):
            n = {-1: 0, 0: 1, rows - 1: 2, rows: 3}.get(row)
            if n is not None:
                return [srow[layer, n, c] for c in range(4)]
            return [early_ref[layer, c, pl.ds(row, spans, stride=rows), :] for c in range(4)]

        for n, row in enumerate((0, 1, rows - 2, rows - 1)):
            here = values(z, row)
            left, right = beside_in_lines(here, sub, first, last)
            new, _ = advance(
                here, values(z, row - 1), values(z, row + 1), left, right,
                values(z - 1, row), values(z + 1, row),
            )
            render(part_ref, pl.ds(n * spans, spans), new, rate, mix)
            for c in range(4):
                lines_ref[z, n, c] = new[c]

    def edges(z):
        edge_rows(z, rowbuf, early_ref, share_ref, edge_ref, srow, places, rows, spans)

    by = 7 if (layers - 2) % 7 == 0 else 2

    @pl.loop(0, (layers - 2) // by)
    def _(group):
        for n in range(by):
            edges(by * group + n + 1)

    @pl.loop(0, (layers - 4) // 4)
    def _(group):
        for n in range(4):
            outer_rows(4 * group + n + 2)


def settle_kernel(
    palette_ref, block, depth0_ref, depth1_ref, c10_ref, c11_ref,
    early_ref, share_ref, edge_ref, part_ref, rows_part_ref, given_rowbuf, given_srow,
    whole_ref, rowbuf, srow, *rest,
    layers, rows, columns, depth_count, row_count,
):
    pieces = rest[:depth_count]
    base, sbase, accum = rest[depth_count:]
    own_tiles, spans = rows // SUB, columns // LANES
    row_rank, depth_rank = lax.axis_index("row"), lax.axis_index("depth")
    row_odd, depth_odd = lax.rem(row_rank, 2), lax.rem(depth_rank, 2)
    above, below = 1 - row_odd, row_odd
    sub = lax.broadcasted_iota(jnp.int32, (SUB, LANES), 0)
    lane = lax.broadcasted_iota(jnp.int32, (SUB, LANES), 1)
    first, last = lane == 0, lane == LANES - 1
    from_front = jnp.full((SUB, LANES), depth_odd, jnp.int32) == 1
    tiles = [(t, j) for j in range(spans) for t in range(own_tiles)]
    rate, mix = constants(palette_ref, layers * depth_count)

    def tile_of(t, j):
        return slice(t * SUB, (t + 1) * SUB), slice(j * LANES, (j + 1) * LANES)

    def cells_of(t, j):
        return pl.ds(j * rows + t * SUB, SUB)

    def line(row):
        return pl.ds(row_of(0, row), spans, stride=PITCH)

    def outer_step(slot, front):
        kept = (depth_rank > 0) if front else (depth_rank < depth_count - 1)
        keep = jnp.full((SUB, LANES), jnp.where(kept, 1, 0), jnp.int32) == 1
        chosen = from_front if front else jnp.logical_not(from_front)
        far, near = (0, 1) if front else (1, 0)
        for t, j in tiles:
            there = tile_of(t, j)
            for c in range(4):
                for k, n in ((0, far), (1, near)):
                    cells = pl.ds((n * spans + j) * rows + t * SUB, SUB)
                    base[k, c, pl.ds(row_of(j, t * SUB), SUB), :] = jnp.where(
                        chosen, depth0_ref[c, cells, :], depth1_ref[c, cells, :]
                    )
                base[2, c, pl.ds(row_of(j, t * SUB), SUB), :] = block[
                    (c, 0 if front else layers - 1) + there
                ]
        z = 0 if front else layers + 1
        for c in range(4):
            base[1, c, line(-1), :] = rowbuf[above, c, z, 1]
            base[1, c, line(rows), :] = rowbuf[below, c, z, 0]
        slots = (0, 1, 2) if front else (2, 1, 0)
        for t, j in tiles:
            new, _ = advance(*neighbours(base, slots, t, j, spans, first, last))
            for c in range(4):
                sbase[slot, c, pl.ds(row_of(j, t * SUB), SUB), :] = jnp.where(keep, new[c], 0.0)

    def add_layer(z, slot, sign):
        for t, j in tiles:
            cells = pl.ds(row_of(j, t * SUB), SUB)
            new = late_share(
                [sbase[slot, c, cells, :] for c in range(4)],
                [base[1, c, cells, :] for c in range(4)],
                share_ref[z, cells_of(t, j), :], 3, sign,
            )
            for c in range(4):
                sbase[slot, c, cells, :] = new[c]

    def take_layer(z, slot):
        for t, j in tiles:
            for c in range(4):
                sbase[slot, c, pl.ds(row_of(j, t * SUB), SUB), :] = early_ref[z, c, cells_of(t, j), :]
        for n, row in enumerate((-1, 0, rows - 1, rows)):
            for c in range(4):
                sbase[slot, c, line(row), :] = srow[z, n, c]

    def whole_layer(n, slots):
        for t, j in tiles:
            new, _ = advance(*neighbours(sbase, slots, t, j, spans, first, last))
            for c in range(4):
                whole_ref[n, c, cells_of(t, j), :] = new[c]
            render(accum, cells_of(t, j), new, rate, mix)

    beside = pl.ds(2 * spans * rows, spans)
    corners = (
        (0, 0, lambda c: depth0_ref[c, beside, :]), (0, 1, lambda c: depth1_ref[c, beside, :]),
        (1, 0, lambda c: c10_ref[c]), (1, 1, lambda c: c11_ref[c]),
    )
    for row_kind, depth_kind, source in corners:
        is_above = row_odd if row_kind == 0 else 1 - row_odd
        is_front = depth_odd if depth_kind == 0 else 1 - depth_odd
        for c in range(4):
            rowbuf[row_kind, c, (1 - is_front) * (layers + 1), is_above] = source(c)
    for c in range(3):
        accum[c] = jnp.zeros((spans * rows, LANES), jnp.float32)
    accum[3] = jnp.ones((spans * rows, LANES), jnp.float32)

    for z in (0, layers - 1):
        edge_rows(
            z, rowbuf, early_ref, share_ref, edge_ref, srow, row_places(row_count), rows, spans
        )

    outer_step(3, True)
    take_layer(0, 0)
    add_layer(0, 0, 1.0)
    take_layer(1, 1)
    take_layer(2, 2)
    whole_layer(0, (3, 0, 1))
    whole_layer(1, (0, 1, 2))
    for t, j in tiles:
        pixels = cells_of(t, j)
        through = accum[3, pixels, :]
        inner = jnp.full((SUB, LANES), True)
        if t == 0:
            inner = sub >= 2
        if t == own_tiles - 1:
            inner = (sub < SUB - 2) if t > 0 else inner & (sub < SUB - 2)
        for c in range(3):
            value = accum[c, pixels, :]
            accum[c, pixels, :] = jnp.where(inner, value + through * part_ref[c, pixels, :], value)
        accum[3, pixels, :] = jnp.where(inner, through * part_ref[3, pixels, :], through)

    for n, row in enumerate((0, 1, rows - 2, rows - 1)):
        pixels, theirs = pl.ds(row, spans, stride=rows), pl.ds(n * spans, spans)
        through = accum[3, pixels, :]
        for c in range(3):
            accum[c, pixels, :] = accum[c, pixels, :] + through * rows_part_ref[c, theirs, :]
        accum[3, pixels, :] = through * rows_part_ref[3, theirs, :]

    take_layer(layers - 3, 0)
    take_layer(layers - 2, 1)
    take_layer(layers - 1, 2)
    outer_step(3, False)
    add_layer(layers - 1, 2, -1.0)
    whole_layer(2, (0, 1, 2))
    whole_layer(3, (1, 2, 3))

    width = columns // depth_count
    per_piece = width // LANES

    def channels(j, t):
        pixels = pl.ds(j * rows + t * SUB, SUB)
        through = accum[3, pixels, :]
        return [0.5 * (accum[c, pixels, :] + (1.0 - through)) for c in range(3)] + [through]

    for k in range(depth_count):
        piece = depth_rank ^ k
        start = piece * per_piece
        for t in range(own_tiles):
            r = slice(t * SUB, (t + 1) * SUB)
            for jj in range(per_piece):
                values = channels(start + jj, t)
                for c in range(4):
                    pieces[k][r, c * width + jj * LANES : c * width + (jj + 1) * LANES] = (
                        values[c]
                    )
            before = channels(jnp.maximum(start - 1, 0), t)
            after = channels(jnp.minimum(start + per_piece, spans - 1), t)
            edge = jnp.zeros((SUB, LANES), jnp.float32)
            for c in range(4):
                for values, low in ((before, 4 * c), (after, 4 * c + 2)):
                    turned = pltpu.roll(values[c], (4 * c + 2) % LANES, 1)
                    edge = jnp.where((lane >= low) & (lane < low + 2), turned, edge)
            pieces[k][r, 4 * width : 4 * width + LANES] = edge


def assemble_kernel(whole_ref, lines_ref, late_ref, den_out, vel_out, *, layers, rows, columns):
    step = pl.program_id(0)
    own_tiles, spans = rows // SUB, columns // LANES

    def put(q, c, there, value):
        if c == 0:
            den_out[(q,) + there] = value
        else:
            vel_out[(c - 1, q) + there] = value

    def copy_layer(source, z, q):
        for j in range(spans):
            lanes = slice(j * LANES, (j + 1) * LANES)
            for c in range(4):
                for t in range(own_tiles):
                    value = source[z, c, pl.ds(j * rows + t * SUB, SUB), :]
                    put(q, c, (slice(t * SUB, (t + 1) * SUB), lanes), value)

    def inner_layer(z, q):
        copy_layer(late_ref, z, q)
        for n, row in enumerate((0, 1, rows - 2, rows - 1)):
            for j in range(spans):
                for c in range(4):
                    there = (slice(row, row + 1), slice(j * LANES, (j + 1) * LANES))
                    put(q, c, there, lines_ref[z, n, c, j : j + 1, :])

    for q in range(4):
        if q < 2:

            @pl.when(step == 0)
            def _():
                copy_layer(whole_ref, q, q)

            pl.when(step > 0)(functools.partial(inner_layer, 4 * step + q, q))
        else:

            @pl.when(step == layers // 4 - 1)
            def _():
                copy_layer(whole_ref, q, q)

            pl.when(step < layers // 4 - 1)(functools.partial(inner_layer, 4 * step + q, q))


def transfer_order(count):
    return sorted(range(count), key=lambda k: (k != 0, k % 2, k)) if count > 2 else list(range(count))


def over_kernel(*refs, count, width):
    parts = [refs[transfer_order(count).index(k)] for k in range(count)]
    picture_ref, swap0_ref, swap1_ref = refs[count:]
    rows = picture_ref.shape[0]
    depth_rank = lax.axis_index("depth")
    row_odd = lax.rem(lax.axis_index("row"), 2)
    lane = lax.broadcasted_iota(jnp.int32, (rows, LANES), 1)

    def split(ref):
        return [ref[:, c * width : (c + 1) * width] for c in range(4)] + [
            ref[:, 4 * width : 4 * width + LANES]
        ]

    def spread_through(edge):
        out = jnp.ones_like(edge)
        for c in range(3):
            turned = pltpu.roll(edge, LANES - 12 + 4 * c, 1)
            out = jnp.where((lane >= 4 * c) & (lane < 4 * c + 4), turned, out)
        return out

    def over(swapped, a, b):
        near = [jnp.where(swapped, y, x) for x, y in zip(a, b)]
        far = [jnp.where(swapped, x, y) for x, y in zip(a, b)]
        out = [near[c] + near[3] * far[c] for c in range(3)]
        out.append(near[3] * far[3])
        edge = near[4] + spread_through(near[4]) * far[4]
        out.append(jnp.where(lane >= 12, near[4] * far[4], edge))
        return out

    values = [split(ref) for ref in parts]
    bit = 0
    while len(values) > 1:
        swapped = (depth_rank >> bit & 1) == 1
        values = [over(swapped, values[k], values[k + 1]) for k in range(0, len(values), 2)]
        bit += 1
    final = values[0]
    for c in range(4):
        picture_ref[:, c * width : (c + 1) * width] = (1.0 - final[3]) if c == 3 else final[c]
    edge = jnp.where((lane >= 12) & (lane < 16), 1.0 - final[4], final[4])
    picture_ref[:, 4 * width : 4 * width + LANES] = edge
    top, bottom = picture_ref[0:2, :], picture_ref[rows - 2 : rows, :]
    odd = row_odd == 1
    swap0_ref[...] = jnp.where(odd, top, bottom)
    swap1_ref[...] = jnp.where(odd, bottom, top)


def filter_kernel(picture_ref, swap0_ref, swap1_ref, out_ref, *, width, row_count, depth_count):
    row_rank, depth_rank = lax.axis_index("row"), lax.axis_index("depth")
    odd = lax.rem(row_rank, 2) == 1
    rows = picture_ref.shape[0]
    own_tiles = rows // SUB
    spans = width // LANES
    lane = lax.broadcasted_iota(jnp.int32, (SUB, LANES), 1)
    sub = lax.broadcasted_iota(jnp.int32, (SUB, LANES), 0)

    def tile(t, c, j):
        if j == -1 or j == spans:
            cols = slice(4 * width, 4 * width + LANES)
        else:
            cols = slice(c * width + j * LANES, c * width + (j + 1) * LANES)
        if t == -1:
            v = jnp.where(odd, swap0_ref[:, cols], swap1_ref[:, cols])
            v = jnp.concatenate([jnp.zeros((SUB - 2, LANES), jnp.float32), v], 0)
        elif t == own_tiles:
            v = jnp.where(odd, swap1_ref[:, cols], swap0_ref[:, cols])
            v = jnp.concatenate([v, jnp.zeros((SUB - 2, LANES), jnp.float32)], 0)
        else:
            v = picture_ref[t * SUB : (t + 1) * SUB, cols]
        if j == -1:
            v = pltpu.roll(v, LANES - 2 - 4 * c, 1)
        elif j == spans:
            v = pltpu.roll(v, (LANES - 2 - 4 * c) % LANES, 1)
        return v

    tiles = {}
    for t in range(-1, own_tiles + 1):
        for j in range(-1, spans + 1):
            four = [tile(t, c, j) for c in range(4)]
            tiles[t, j] = four + [(four[0] + four[1] + four[2]) / 3.0]

    def column_shift(t, j, q, dx):
        if dx == 0:
            return tiles[t, j][q]
        if dx > 0:
            mixed = jnp.where(lane < dx, tiles[t, j + 1][q], tiles[t, j][q])
        else:
            mixed = jnp.where(lane >= LANES + dx, tiles[t, j - 1][q], tiles[t, j][q])
        return pltpu.roll(mixed, (-dx) % LANES, 1)

    no_above, no_below = row_rank == 0, row_rank == row_count - 1
    no_west, no_east = depth_rank == 0, depth_rank == depth_count - 1
    for j in range(spans):
        sums = [[None] * 5 for _ in range(own_tiles)]
        for dx in range(-2, 3):
            shifted = {
                t: [column_shift(t, j, q, dx) for q in range(5)] for t in range(-1, own_tiles + 1)
            }
            for dy in range(-2, 3):
                spatial = -(dx * dx + dy * dy) / (2.0 * SPACE_SCALE * SPACE_SCALE)
                for t in range(own_tiles):
                    if dy == 0:
                        near = shifted[t]
                    elif dy > 0:
                        near = [
                            pltpu.roll(
                                jnp.where(sub < dy, shifted[t + 1][q], shifted[t][q]), SUB - dy, 0
                            )
                            for q in range(5)
                        ]
                    else:
                        near = [
                            pltpu.roll(
                                jnp.where(sub >= SUB + dy, shifted[t - 1][q], shifted[t][q]), -dy, 0
                            )
                            for q in range(5)
                        ]
                    diff = near[4] - tiles[t, j][4]
                    weight = jnp.exp(
                        spatial - diff * diff * (1.0 / (2.0 * RANGE_SCALE * RANGE_SCALE))
                    )
                    blocked = None
                    if t == 0 and dy < 0:
                        blocked = no_above & (sub < -dy)
                    if t == own_tiles - 1 and dy > 0:
                        blocked = no_below & (sub >= SUB - dy)
                    if j == 0 and dx < 0:
                        side = no_west & (lane < -dx)
                        blocked = side if blocked is None else blocked | side
                    if j == spans - 1 and dx > 0:
                        side = no_east & (lane >= LANES - dx)
                        blocked = side if blocked is None else blocked | side
                    if blocked is not None:
                        weight = jnp.where(blocked, 0.0, weight)
                    terms = [weight * near[c] for c in range(4)] + [weight]
                    sums[t] = terms if sums[t][0] is None else [a + b for a, b in zip(sums[t], terms)]
        for t in range(own_tiles):
            inverse = 1.0 / sums[t][4]
            for c in range(4):
                out_ref[c, t * SUB : (t + 1) * SUB, j * LANES : (j + 1) * LANES] = (
                    sums[t][c] * inverse
                )


def compute(density, velocity, palette):
    layers, rows, columns = density.shape
    depth_count, row_count = lax.axis_size("depth"), lax.axis_size("row")
    spans = columns // LANES
    width = columns // depth_count
    line = 4 * width + LANES
    assert spans == SUB and rows % SUB == 0 and width % LANES == 0 and layers % 4 == 0 and layers >= 8
    vmem = pl.BlockSpec(memory_space=pltpu.VMEM)
    smem = pl.BlockSpec(memory_space=pltpu.SMEM)
    f32 = jnp.float32

    def shape(*dims):
        return jax.ShapeDtypeStruct(dims, f32)

    def local(*dims):
        return pltpu.VMEM(dims, f32)

    def params(mebibytes):
        return pltpu.CompilerParams(vmem_limit_bytes=mebibytes << 20)

    row_shape = (4, layers, 2, spans, LANES)
    depth_shape = (4, (2 * rows + 1) * spans, LANES)
    corner_shape = (4, spans, LANES)
    block, row0, row1, corner0, corner1 = pl.pallas_call(
        functools.partial(pack_kernel, layers=layers, rows=rows, spans=spans, chunks=4),
        out_shape=(
            local(4, layers, rows, columns), local(*row_shape), local(*row_shape),
            local(*corner_shape), local(*corner_shape),
        ),
        in_specs=[pl.BlockSpec(memory_space=pltpu.HBM)] * 2,
        out_specs=(vmem,) * 5,
        scratch_shapes=[pltpu.VMEM((2,) + row_shape, f32), pltpu.SemaphoreType.DMA((4, 2))],
        name="pack",
        compiler_params=params(8),
    )(
        pltpu.with_memory_space_constraint(density, pltpu.HBM),
        pltpu.with_memory_space_constraint(velocity, pltpu.HBM),
    )
    row1 = swap_rows(row1, 1)
    row0 = swap_rows(row0, 0)
    depth0, depth1 = pl.pallas_call(
        functools.partial(pack_depth_kernel, layers=layers, rows=rows, spans=spans),
        out_shape=(local(*depth_shape), local(*depth_shape)),
        in_specs=[vmem] * 2,
        out_specs=(vmem,) * 2,
        name="pack_depth",
        compiler_params=params(8),
    )(in_vmem(block), in_vmem(row0))
    depth0, depth1 = swap_depths(depth0, 0), swap_depths(depth1, 1)
    corner0, corner1 = swap_corners(corner0, 1, 0), swap_corners(corner1, 1, 1)

    early, share, edge, late, part = pl.pallas_call(
        functools.partial(
            interior_kernel, layers=layers, rows=rows, columns=columns, depth_count=depth_count
        ),
        grid=(layers // 4,),
        out_shape=(
            pltpu.VMEM((layers, 4, spans * rows, LANES), f32),
            pltpu.VMEM((layers, spans * rows, LANES), f32),
            local(layers, 2, 4, spans, LANES), local(layers, 4, spans * rows, LANES),
            local(4, spans * rows, LANES),
        ),
        in_specs=[smem, vmem],
        out_specs=(vmem,) * 5,
        scratch_shapes=[pltpu.VMEM((4, 4, spans * PITCH, LANES), f32)],
        cost_estimate=pl.CostEstimate(
            flops=80 * layers * rows * columns, bytes_accessed=16 * layers * rows * columns,
            transcendentals=layers * rows * columns,
        ),
        name="interior",
        compiler_params=pltpu.CompilerParams(vmem_limit_bytes=24 << 20),
    )(palette, in_vmem(block))

    rowbuf_shape = (2, 4, layers + 2, 2, spans, LANES)
    srow_shape = (layers, 4, 4, spans, LANES)
    rowbuf, srow, lines, rows_part = pl.pallas_call(
        functools.partial(
            outer_kernel, layers=layers, rows=rows, columns=columns,
            depth_count=depth_count, row_count=row_count,
        ),
        out_shape=(
            local(*rowbuf_shape), local(*srow_shape), local(*srow_shape),
            local(4, 4 * spans, LANES),
        ),
        in_specs=[smem] + [vmem] * 5,
        out_specs=(vmem,) * 4,
        cost_estimate=pl.CostEstimate(
            flops=40 * layers * rows * columns, bytes_accessed=4 * layers * rows * columns,
            transcendentals=layers * rows * columns,
        ),
        name="outer",
        compiler_params=params(16),
    )(palette, *(in_vmem(x) for x in (row0, row1, early, share, edge)))

    whole, unused, unused, *parts = pl.pallas_call(
        functools.partial(
            settle_kernel, layers=layers, rows=rows, columns=columns,
            depth_count=depth_count, row_count=row_count,
        ),
        out_shape=(local(4, 4, spans * rows, LANES), local(*rowbuf_shape), local(*srow_shape))
        + (local(rows, line),) * depth_count,
        in_specs=[smem] + [vmem] * 12,
        out_specs=(vmem,) * (3 + depth_count),
        input_output_aliases={11: 1, 12: 2},
        scratch_shapes=[
            pltpu.VMEM((3, 4, spans * PITCH, LANES), f32),
            pltpu.VMEM((4, 4, spans * PITCH, LANES), f32),
            pltpu.VMEM((4, spans * rows, LANES), f32),
        ],
        name="settle",
        compiler_params=params(24),
    )(
        palette,
        *(
            in_vmem(x)
            for x in (
                block, depth0, depth1, corner0, corner1, early, share, edge, part, rows_part,
                rowbuf, srow,
            )
        ),
    )

    settled, moving = pl.pallas_call(
        functools.partial(assemble_kernel, layers=layers, rows=rows, columns=columns),
        grid=(layers // 4,),
        out_shape=(shape(layers, rows, columns), shape(3, layers, rows, columns)),
        in_specs=[vmem] * 3,
        out_specs=(
            pl.BlockSpec((4, rows, columns), lambda i: (i, 0, 0)),
            pl.BlockSpec((3, 4, rows, columns), lambda i: (0, i, 0, 0)),
        ),
        cost_estimate=pl.CostEstimate(
            flops=20 * layers * rows * columns, bytes_accessed=16 * layers * rows * columns,
            transcendentals=0,
        ),
        name="assemble",
        compiler_params=params(16),
    )(in_vmem(whole), in_vmem(lines), in_vmem(late))

    for k in range(1, depth_count):
        parts[k] = lax.ppermute(parts[k], "depth", [(i, i ^ k) for i in range(depth_count)])
    composed, swap0, swap1 = pl.pallas_call(
        functools.partial(over_kernel, count=depth_count, width=width),
        out_shape=(shape(rows, line), shape(2, line), shape(2, line)),
        in_specs=[vmem] * depth_count,
        out_specs=(vmem, vmem, vmem),
        name="over",
        compiler_params=pltpu.CompilerParams(vmem_limit_bytes=8 << 20),
    )(parts[0], *(in_vmem(parts[k]) for k in transfer_order(depth_count)[1:]))

    swap1, swap0 = swap_rows(swap1, 1), swap_rows(swap0, 0)
    filtered = pl.pallas_call(
        functools.partial(
            filter_kernel, width=width, row_count=row_count, depth_count=depth_count
        ),
        out_shape=shape(4, rows, width),
        in_specs=[vmem] * 3,
        out_specs=vmem,
        name="bilateral",
        compiler_params=pltpu.CompilerParams(vmem_limit_bytes=8 << 20),
    )(composed, in_vmem(swap0), in_vmem(swap1))
    return (filtered, settled, moving)


def solution(mesh):
    in_specs = (P("depth", "row", None), P(None, "depth", "row", None), P())
    out_specs = (P(None, "row", "depth"), P("depth", "row", None), P(None, "depth", "row", None))
    return jax.shard_map(compute, mesh=mesh, in_specs=in_specs, out_specs=out_specs, check_vma=False)
```
